32 devices in a mesh: fsdp: 2 (over y), ctx: 8 (over z, x), tp: 2 (over core).
Axes of the slice: x: 2, y: 2, z: 4, core: 2. Of those that a mesh axis runs over, the one named last changes fastest.
Arguments:
- hidden_in: bfloat16 [4096, 2048], P(('fsdp', 'ctx'), 'tp'), may hold values from -6 to 6
- cotangent: bfloat16 [4096, 2048], P(('fsdp', 'ctx'), 'tp'), may hold values from -6 to 6
- positions: int32 [2, 2048], P('fsdp'), may hold values from 0 to 2047, each once within a row
- seq_lengths: int32 [2, 3], P('fsdp'), may hold values from 1 to 1024, 2048 in all within a row
- expert_ids: int32 [4096, 8], P(('fsdp', 'ctx')), may hold values from 0 to 15, all different within a row; in each aligned block of 256 rows (0 to 255, 256 to 511, ...) at most 160 rows name the same one
- attn_norm: bfloat16 [2048], P('tp'), may hold values from 0.099609375 to 1.8984375
- ffn_norm: bfloat16 [2048], P('tp'), may hold values from 0.099609375 to 1.8984375
- query_norm: bfloat16 [128], replicated, may hold values from 0.099609375 to 1.8984375
- key_norm: bfloat16 [128], replicated, may hold values from 0.099609375 to 1.8984375
- w_query: bfloat16 [2048, 2048], P('fsdp', 'tp'), may hold values from -0.125 to 0.125
- w_key: bfloat16 [2048, 2048], P('fsdp', 'tp'), may hold values from -0.125 to 0.125
- w_value: bfloat16 [2048, 2048], P('fsdp', 'tp'), may hold values from -0.125 to 0.125
- w_out: bfloat16 [2048, 2048], P('tp', 'fsdp'), may hold values from -2 to 2
- w_router: bfloat16 [16, 2048], P(None, 'fsdp'), may hold values from -0.0625 to 0.0625
- w_gate: bfloat16 [16, 2048, 1024], P(None, 'fsdp', 'tp'), may hold values from -0.125 to 0.125
- w_up: bfloat16 [16, 2048, 1024], P(None, 'fsdp', 'tp'), may hold values from -0.125 to 0.125
- w_down: bfloat16 [16, 2048, 1024], P(None, 'fsdp', 'tp'), may hold values from -2 to 2
Outputs:
- hidden_out: bfloat16 [4096, 2048], P(('fsdp', 'ctx'), 'tp')
- grad_hidden: float32 [4096, 2048], P(('fsdp', 'ctx'), 'tp')
- grad_attn_norm: float32 [2048], replicated
- grad_ffn_norm: float32 [2048], replicated
- grad_query_norm: float32 [128], replicated
- grad_key_norm: float32 [128], replicated
- grad_query: float32 [2048, 2048], P(('fsdp', 'ctx'), 'tp')
- grad_key: float32 [2048, 2048], P(('fsdp', 'ctx'), 'tp')
- grad_value: float32 [2048, 2048], P(('fsdp', 'ctx'), 'tp')
- grad_out: float32 [2048, 2048], P('tp', ('fsdp', 'ctx'))
- grad_router: float32 [16, 2048], P(None, ('fsdp', 'ctx'))
- grad_gate: float32 [16, 2048, 1024], P(None, ('fsdp', 'ctx'), 'tp')
- grad_up: float32 [16, 2048, 1024], P(None, ('fsdp', 'ctx'), 'tp')
- grad_down: float32 [16, 2048, 1024], P(None, ('fsdp', 'ctx'), 'tp')
- stream_rms: float32 [3], replicated
The draws below stay inside these ranges and needn't reach their ends.
Inputs may be any that keep to these rules, and one draw needn't show every extreme that they name: Each row of positions names every position of its pack once. `seq_lengths`: each row sums to 2048; the longest sequence of every pack has 1024 tokens. `expert_ids`: a token's 8 experts are different, and every expert is chosen by some token; within the rows of one device (aligned blocks of 256 rows) no expert is chosen more than 160 times, and some expert is chosen exactly 160 times in some block.
All inputs are finite; a program needn't handle non-finite values.
Results may differ from the reference program's by a relative error of at most 0.029.
Values may be sent and summed in bfloat16 or wider, within the bound.
A program may use at most 448 MiB of HBM per device.

```python
import math
import jax
import jax.numpy as jnp
import numpy as np
from jax import lax

D = 2048
HEADS = 16
HD = 128
FF = 1024
TOPK = 8
EXPERTS = 16
TOK_DEV = 256
CAP = 160
PACK = 2048
PACKS = 2
TOKENS = 4096
MOST = 1024
SLOTS = 3


def block_levels(rng, dims, shards, low, high):
    gain = 1.0
    for dim, parts in shards:
        steps = jax.random.uniform(jax.random.fold_in(jax.random.fold_in(rng, 6), dim), (parts,), jnp.float32, low / len(shards), high / len(shards))
        gain = gain * jnp.repeat(jnp.exp(steps), dims[dim] // parts).reshape((-1,) + (1,) * (len(dims) - 1 - dim))
    return gain


def profile(count, total, most, slope):
    loads = [(1 << 20) // math.isqrt(rank ** slope) + 1 for rank in range(2, count + 1)]
    surplus, holding = total - most - (count - 1), [1] * (count - 1)
    while surplus > 0:
        movable = [i for i in range(count - 1) if holding[i] < most]
        whole, left = sum([loads[i] for i in movable]), surplus
        for i in movable:
            more = min(most - holding[i], max(1, left * loads[i] // whole), surplus)
            holding[i] = holding[i] + more
            surplus = surplus - more
    return np.array([most] + holding)


def ragged_sizes(key, amount, total, limit, slope):
    if amount == 2:
        one = jax.random.randint(key, (), max(1, total - limit), min(limit, total - 1) + 1)
        return jnp.stack([one, total - one])
    tallies = jnp.asarray(profile(amount, total, limit, slope), jnp.int32)
    twos = (amount - 1) // 2
    giver, receiver = tallies[1:1 + 2 * twos:2], tallies[2:2 + 2 * twos:2]
    slack = jnp.minimum(giver - 1, limit - receiver)
    passed = jax.random.randint(jax.random.fold_in(key, 1), (twos,), 0, 1 << 20) % (slack + 1)
    tallies = tallies.at[1:1 + 2 * twos:2].set(giver - passed).at[2:2 + 2 * twos:2].set(receiver + passed)
    return tallies[jax.random.permutation(jax.random.fold_in(key, 2), amount)]


def shared_out(key, own, number, rows, amount, top, bound, lean):
    ranking = jax.random.permutation(key, amount)
    packed, ordinary = shares(amount, rows * top, bound, lean, True), shares(amount, rows * top, bound, lean, False)
    places = jnp.arange(amount)

    def named(tallies, rotation):
        used = int((tallies > 0).sum())
        fixed = max(1, used // 4)
        moved = fixed + (places - fixed + rotation * (used - fixed)) % max(1, amount - fixed)
        return jnp.zeros((amount,), jnp.int32).at[ranking[jnp.where(places < fixed, places, moved)]].set(jnp.asarray(tallies, jnp.int32))

    tallies = jnp.where(number % 4 == 0, named(packed, number // 4), named(ordinary, number - number // 4 - 1))
    mixed = jax.random.permutation(jax.random.fold_in(own, 3), amount)
    source_of, receiver = mixed[0:amount // 2 * 2:2], mixed[1:amount // 2 * 2:2]
    margin = jnp.minimum(tallies[source_of] - 1, bound - tallies[receiver]) // 2
    margin = jnp.where((source_of == ranking[0]) | (receiver == ranking[0]) | (tallies[receiver] == 0), 0, jnp.maximum(margin, 0))
    moved = jax.random.randint(jax.random.fold_in(own, 4), (amount // 2,), 0, 1 << 20) % (margin + 1)
    tallies = tallies.at[source_of].add(-moved).at[receiver].add(moved)
    members = jnp.searchsorted(jnp.cumsum(tallies), jnp.arange(rows * top), side="right").astype(jnp.int32)
    table = members.reshape(top, rows).T
    table = table[jax.random.permutation(jax.random.fold_in(own, 1), rows)]
    rotation = jax.random.randint(jax.random.fold_in(own, 2), (rows, 1), 0, top)
    return jnp.take_along_axis(table, (jnp.arange(top)[None, :] + rotation) % top, axis=1)


def shares(count, total, most, lean, full):
    portions = [(1 << 20) // math.isqrt(rank ** lean) + 1 for rank in range(1, count + 1)]
    largest = most if full else min(most, max(-(-total // count), total * portions[0] // sum(portions)))
    least = 1 if total - largest >= count - 1 else 0
    counts, rest = [largest] + [least] * (count - 1), total - largest - least * (count - 1)
    while rest > 0:
        candidates = [i for i in range(1, count) if counts[i] < largest] or [i for i in range(1, count) if counts[i] < most]
        whole, left = sum([portions[i] for i in candidates]), rest
        for i in candidates:
            extra = min(most - counts[i], max(1, left * portions[i] // whole), rest)
            counts[i] = counts[i] + extra
            rest = rest - extra
    return np.array(counts)


def centred(key, dims, width, most, split=(), kind=jnp.bfloat16):
    values = width * jax.random.normal(key, dims, jnp.float32)
    if split:
        values = values * block_levels(key, dims, split, -0.22, 0.18)
    return jnp.clip(values, -most, most).astype(kind)


def setup_inputs(seed: int = 0) -> dict:
    key_list = jax.random.split(jax.random.key(seed), 18)
    hidden_in = centred(key_list[0], (TOKENS, D), 1.0, 6.0, ((0, 16), (1, 2)))
    cotangent = centred(key_list[1], (TOKENS, D), 1.0, 6.0, ((0, 16), (1, 2)))
    positions = jax.vmap(lambda own: jax.random.permutation(own, PACK))(jax.random.split(key_list[2], PACKS)).reshape((PACKS, PACK)).astype(jnp.int32)
    seq_lengths = jax.vmap(lambda own: ragged_sizes(own, SLOTS, PACK, MOST, 2))(jax.random.split(key_list[3], PACKS)).reshape((PACKS, SLOTS)).astype(jnp.int32)
    expert_ids_keys = jax.random.split(jax.random.fold_in(key_list[4], 1), TOKENS // TOK_DEV)
    expert_ids_turns = jax.random.permutation(jax.random.fold_in(key_list[4], 3), TOKENS // TOK_DEV)
    expert_ids = jax.vmap(lambda own, number: shared_out(jax.random.fold_in(key_list[4], 2), own, number, TOK_DEV, EXPERTS, TOPK, CAP, 1))(expert_ids_keys, expert_ids_turns).reshape((TOKENS, TOPK))
    attn_norm = jnp.clip(1.0 + 0.18 * jax.random.normal(key_list[5], (D,), jnp.float32), 0.099609375, 1.8984375).astype(jnp.bfloat16)
    ffn_norm = jnp.clip(1.0 + 0.18 * jax.random.normal(key_list[6], (D,), jnp.float32), 0.099609375, 1.8984375).astype(jnp.bfloat16)
    query_norm = jnp.clip(1.0 + 0.18 * jax.random.normal(key_list[7], (HD,), jnp.float32), 0.099609375, 1.8984375).astype(jnp.bfloat16)
    key_norm = jnp.clip(1.0 + 0.18 * jax.random.normal(key_list[8], (HD,), jnp.float32), 0.099609375, 1.8984375).astype(jnp.bfloat16)
    w_query = centred(key_list[9], (D, D), D ** -0.5, 0.125, ((0, 2), (1, 2)))
    w_key = centred(key_list[10], (D, D), D ** -0.5, 0.125, ((0, 2), (1, 2)))
    w_value = centred(key_list[11], (D, D), D ** -0.5, 0.125, ((0, 2), (1, 2)))
    w_out = centred(key_list[12], (D, D), 8 ** -0.5, 2.0, ((0, 2), (1, 2)))
    w_router = centred(key_list[13], (EXPERTS, D), (4 * D) ** -0.5, 0.0625, ((1, 2),))
    w_gate = centred(key_list[14], (EXPERTS, D, FF), D ** -0.5, 0.125, ((1, 2), (2, 2)))
    w_up = centred(key_list[15], (EXPERTS, D, FF), D ** -0.5, 0.125, ((1, 2), (2, 2)))
    w_down = centred(key_list[16], (EXPERTS, D, FF), (max(1, FF // 128)) ** -0.5, 2.0, ((1, 2), (2, 2)))
    return {"hidden_in": hidden_in, "cotangent": cotangent, "positions": positions, "seq_lengths": seq_lengths, "expert_ids": expert_ids, "attn_norm": attn_norm, "ffn_norm": ffn_norm, "query_norm": query_norm, "key_norm": key_norm, "w_query": w_query, "w_key": w_key, "w_value": w_value, "w_out": w_out, "w_router": w_router, "w_gate": w_gate, "w_up": w_up, "w_down": w_down}


norm_eps = 1e-06
rope_base = 10000.0
highest = lax.Precision.HIGHEST

@jax.custom_vjp
def low(v):
    return lax.optimization_barrier(v.astype(jnp.bfloat16)).astype(jnp.float32)

@jax.custom_vjp
def low_back(v):
    return v

def low_keep(v):
    return (low(v), None)

def low_pass(kept, grad):
    return (grad,)

def back_keep(v):
    return (v, None)

def back_low(kept, grad):
    return (low(grad),)
low.defvjp(low_keep, low_pass)
low_back.defvjp(back_keep, back_low)

def locate(pack_spots, lengths_row):
    seq_ends = jnp.cumsum(lengths_row).astype(jnp.int32)
    starts = (seq_ends - lengths_row).astype(jnp.int32)
    segment = lax.optimization_barrier(jnp.sum((pack_spots[:, None] >= seq_ends[None, :]).astype(jnp.int32), axis=1)).astype(jnp.int32)
    slot_ids = jnp.arange(lengths_row.shape[0], dtype=jnp.int32)
    seq_begin = lax.optimization_barrier(jnp.sum(jnp.where(segment[:, None] == slot_ids[None, :], starts[None, :], 0), axis=1)).astype(jnp.int32)
    return (segment, (pack_spots - seq_begin).astype(jnp.int32))

def rope_tables(pack_spots, head_dim):
    half_dim = head_dim // 2
    inv_freq = rope_base ** (-(jnp.arange(half_dim, dtype=jnp.float32) * 2.0 / head_dim))
    angle_grid = pack_spots.astype(jnp.float32)[:, None] * inv_freq[None, :]
    cosine = jnp.concatenate([jnp.cos(angle_grid), jnp.cos(angle_grid)], axis=1)
    sine_table = jnp.concatenate([jnp.sin(angle_grid), jnp.sin(angle_grid)], axis=1)
    return (cosine[:, None, :], sine_table[:, None, :])

def rotate(tensor, cosine, sine_table):
    half_dim = tensor.shape[-1] // 2
    turned = jnp.concatenate([-tensor[..., half_dim:], tensor[..., :half_dim]], axis=-1)
    return tensor * cosine + turned * sine_table

def normalize(tensor, gain_vec):
    return tensor * lax.rsqrt(lax.optimization_barrier(jnp.mean(tensor * tensor, axis=-1, keepdims=True)) + norm_eps) * gain_vec

def hi_dot(left, right):
    return jnp.dot(left, right, precision=highest, preferred_element_type=jnp.float32)

def reference(hidden_in, cotangent, positions, seq_lengths, expert_ids, attn_norm, ffn_norm, query_norm, key_norm, w_query, w_key, w_value, w_out, w_router, w_gate, w_up, w_down):
    seg_all, place_all = jax.vmap(locate)(positions, seq_lengths)
    segments = seg_all.reshape(TOKENS)
    places = place_all.reshape(TOKENS)
    cosine, sine_table = rope_tables(places, HD)
    chosen = lax.optimization_barrier(jnp.sum((expert_ids[:, :, None] == jnp.arange(EXPERTS, dtype=jnp.int32)[None, None, :]).astype(jnp.float32), axis=1))
    score_scale = HD ** (-0.5)
    qblock = min(512, PACK)
    blocks = PACK // qblock

    def attend(query_all, key_all, value_all):

        def one_pack(pack_args):
            query_pack, key_pack, value_pack, seg_pack = pack_args

            def one_block(block_args):
                query_block, seg_block = block_args
                scores = low_back(jnp.einsum('qhd,khd->hqk', query_block, key_pack, precision=highest) * score_scale)
                scores = jnp.where(seg_block[None, :, None] == seg_pack[None, None, :], scores, -1e+30)
                row_peak = lax.optimization_barrier(jnp.max(scores, axis=2, keepdims=True))
                row_exp = jnp.exp(scores - row_peak)
                probs = low(row_exp / lax.optimization_barrier(jnp.sum(row_exp, axis=2, keepdims=True)))
                return jnp.einsum('hqk,khd->qhd', probs, value_pack, precision=highest)
            block_out = lax.map(jax.checkpoint(one_block), (query_pack.reshape(blocks, qblock, HEADS, HD), seg_pack.reshape(blocks, qblock)))
            return block_out.reshape(PACK, HEADS, HD)
        result = lax.map(one_pack, (query_all.reshape(PACKS, PACK, HEADS, HD), key_all.reshape(PACKS, PACK, HEADS, HD), value_all.reshape(PACKS, PACK, HEADS, HD), segments.reshape(PACKS, PACK)))
        return result.reshape(TOKENS, HEADS, HD)

    def forward(hidden, gain_first, gain_second, gain_query, gain_key, query_w, key_w, value_w, out_w, router_w, gate_w, up_w, down_w):
        normed_first = low(normalize(hidden, gain_first))
        query_raw = low_back(hi_dot(normed_first, query_w)).reshape(TOKENS, HEADS, HD)
        key_raw = low_back(hi_dot(normed_first, key_w)).reshape(TOKENS, HEADS, HD)
        value_all = low(low_back(hi_dot(normed_first, value_w))).reshape(TOKENS, HEADS, HD)
        query_rot = low(rotate(normalize(query_raw, gain_query), cosine, sine_table))
        key_rot = low(rotate(normalize(key_raw, gain_key), cosine, sine_table))
        attended = attend(query_rot, key_rot, value_all)
        attended_low = low(low_back(attended.reshape(TOKENS, D)))
        attn_branch = low_back(hi_dot(attended_low, out_w))
        middle = hidden + attn_branch
        normed_second = low(normalize(middle, gain_second))
        logits = low_back(hi_dot(normed_second, router_w.T))
        logit_peak = lax.optimization_barrier(jnp.max(logits, axis=1, keepdims=True))
        logit_exp = jnp.exp(logits - logit_peak)
        route_probs = logit_exp / lax.optimization_barrier(jnp.sum(logit_exp, axis=1, keepdims=True))
        gate_weights = route_probs * chosen
        gate_proj = low_back(jnp.einsum('nd,edf->enf', normed_second, gate_w, precision=highest))
        up_proj = low_back(jnp.einsum('nd,edf->enf', normed_second, up_w, precision=highest))
        activity = gate_proj * jax.nn.sigmoid(gate_proj) * up_proj
        mixed = low(low_back(gate_weights.T[:, :, None] * activity))
        expert_branch = low_back(jnp.einsum('enf,edf->nd', mixed, down_w, precision=highest))
        result = middle + expert_branch
        stream_sums = jnp.stack([jnp.sum(middle * middle), jnp.sum(attn_branch * attn_branch), jnp.sum(expert_branch * expert_branch)])
        return (result, stream_sums)
    result, pull_back, stream_sums = jax.vjp(forward, hidden_in.astype(jnp.float32), attn_norm.astype(jnp.float32), ffn_norm.astype(jnp.float32), query_norm.astype(jnp.float32), key_norm.astype(jnp.float32), w_query.astype(jnp.float32), w_key.astype(jnp.float32), w_value.astype(jnp.float32), w_out.astype(jnp.float32), w_router.astype(jnp.float32), w_gate.astype(jnp.float32), w_up.astype(jnp.float32), w_down.astype(jnp.float32), has_aux=True)
    all_grads = pull_back(cotangent.astype(jnp.float32))
    stream_rms = jnp.sqrt(stream_sums / (TOKENS * D))
    return (result.astype(jnp.bfloat16), all_grads[0], all_grads[1], all_grads[2], all_grads[3], all_grads[4], all_grads[5], all_grads[6], all_grads[7], all_grads[8], all_grads[9], all_grads[10], all_grads[11], all_grads[12], stream_rms)
```

```python
import jax
import numpy as np
import jax.numpy as jnp
from jax import lax
from jax.sharding import PartitionSpec as P

norm_eps = 1e-06
rope_base = 10000.0


def locate(pack_spots, lengths_row):
    seq_ends = jnp.cumsum(lengths_row)
    starts = seq_ends - lengths_row
    segment = jnp.sum((pack_spots[:, None] >= seq_ends[None, :]).astype(jnp.int32), axis=1)
    slot_ids = jnp.arange(lengths_row.shape[0], dtype=jnp.int32)
    seq_begin = jnp.sum(
        jnp.where(segment[:, None] == slot_ids[None, :], starts[None, :], 0), axis=1
    )
    return (segment, pack_spots - seq_begin)


def rope_tables(pack_spots, head_dim):
    half_dim = head_dim // 2
    inv_freq = rope_base ** (-(jnp.arange(half_dim, dtype=jnp.float32) * 2.0 / head_dim))
    angle_grid = pack_spots.astype(jnp.float32)[:, None] * inv_freq[None, :]
    cosine = jnp.concatenate([jnp.cos(angle_grid), jnp.cos(angle_grid)], axis=1)
    sine_table = jnp.concatenate([jnp.sin(angle_grid), jnp.sin(angle_grid)], axis=1)
    return (cosine[:, None, :], sine_table[:, None, :])


def rotate(tensor, cosine, sine_table):
    half_dim = tensor.shape[-1] // 2
    turned = jnp.concatenate([-tensor[..., half_dim:], tensor[..., :half_dim]], axis=-1)
    return tensor * cosine + turned * sine_table


def unrotate(grad_rot, cosine, sine_table):
    half_dim = grad_rot.shape[-1] // 2
    shifted = grad_rot * sine_table
    turned = jnp.concatenate([shifted[..., half_dim:], -shifted[..., :half_dim]], axis=-1)
    return grad_rot * cosine + turned


def on_device(
    hidden_in,
    cotangent,
    positions,
    seq_lengths,
    expert_ids,
    attn_norm,
    ffn_norm,
    query_norm,
    key_norm,
    w_query,
    w_key,
    w_value,
    w_out,
    w_router,
    w_gate,
    w_up,
    w_down,
):
    tok_rows, col_count = hidden_in.shape
    packs_axis, ctx_size, tp_size = (
        lax.axis_size("fsdp"),
        lax.axis_size("ctx"),
        lax.axis_size("tp"),
    )
    ctx_place, tp_place = lax.axis_index("ctx"), lax.axis_index("tp")
    width_all = col_count * tp_size
    pack_rows = tok_rows * ctx_size
    head_dim = query_norm.shape[0]
    local_heads = w_query.shape[1] // head_dim
    expert_count = w_gate.shape[0]
    own_experts = expert_count // ctx_size
    own_heads = max(1, local_heads // ctx_size)
    sharers = max(1, ctx_size // local_heads)
    head_cols = own_heads * head_dim
    score_scale = head_dim ** (-0.5)
    wide = jnp.float32
    slim = jnp.bfloat16

    masks_even = [ctx_size >> (i + 1) for i in range(ctx_size.bit_length() - 1)]
    masks_odd = masks_even[:-2] + masks_even[:-3:-1]

    def offsets(masks):
        return np.array(
            [
                sum(mask for bit, mask in enumerate(masks) if (j >> bit) & 1)
                for j in range(ctx_size)
            ],
            np.int32,
        )

    block_order = ctx_place ^ jnp.where(
        tp_place % 2 == 0, jnp.asarray(offsets(masks_even)), jnp.asarray(offsets(masks_odd))
    )

    def move(tensor, step):
        pairs = []
        for f in range(packs_axis):
            for c in range(ctx_size):
                for t in range(tp_size):
                    to_c, to_t = step(c, t)
                    pairs.append(
                        (
                            (f * ctx_size + c) * tp_size + t,
                            (f * ctx_size + to_c) * tp_size + to_t,
                        )
                    )
        return lax.ppermute(tensor, ("fsdp", "ctx", "tp"), pairs)

    def ctx_step(index):
        return lambda c, t: (c ^ (masks_even, masks_odd)[t % 2][index], t)

    def tp_step(shift):
        return lambda c, t: (c, t ^ shift)

    def reorder(tensor, shift):
        if shift % 2 == 0:
            return tensor
        shape = tensor.shape
        return jnp.swapaxes(tensor.reshape((2, 2, shape[0] // 4) + shape[1:]), 0, 1).reshape(shape)

    def by_place(parts):
        shift = 1
        while shift < tp_size:
            swap = (tp_place & shift) > 0
            parts = [jnp.where(swap, parts[i ^ shift], parts[i]) for i in range(tp_size)]
            shift *= 2
        return parts

    def gather_pack(tensor):
        held = tensor[None]
        for index in range(len(masks_even)):
            held = jnp.concatenate([held, move(held, ctx_step(index))], axis=0)
        parts = [held]
        for shift in range(1, tp_size):
            parts.append(reorder(move(held, tp_step(shift)), shift))
        return [part.reshape(pack_rows, col_count) for part in by_place(parts)]

    def scatter_pack(tensor):
        def columns(shift):
            return lax.dynamic_slice_in_dim(
                tensor, (tp_place ^ shift) * col_count, col_count, 1
            ).reshape(ctx_size, tok_rows, col_count)

        total = columns(0).astype(wide)
        for shift in range(1, tp_size):
            total = total + reorder(move(columns(shift), tp_step(shift)), shift).astype(wide)
        for index in reversed(range(len(masks_even))):
            half = total.shape[0] // 2
            total = total.astype(slim)
            total = total[:half].astype(wide) + move(total[half:], ctx_step(index)).astype(wide)
        return total[0]

    def row_total(tensor):
        return lax.psum(tensor, "tp")

    def dot(left, right, dims):
        return lax.dot_general(left, right, ((dims[:1], dims[1:]), ((), ())), preferred_element_type=wide)

    head_place = ctx_place if sharers == 1 else ctx_place % local_heads

    def head_slice(weight, axis):
        return lax.dynamic_slice_in_dim(weight, head_place * head_cols, head_cols, axis)

    def expert_slice(weight):
        return lax.dynamic_slice_in_dim(weight, ctx_place * own_experts, own_experts, 0)

    qkv_weight = lax.all_gather(
        jnp.concatenate([head_slice(w, 1) for w in (w_query, w_key, w_value)], axis=1),
        "fsdp",
        axis=0,
        tiled=True,
    )
    out_weight = lax.all_gather(head_slice(w_out, 0), "fsdp", axis=1, tiled=True)
    router_full = lax.all_gather(w_router, "fsdp", axis=1, tiled=True)
    gate_weight, up_weight, down_weight = (
        lax.all_gather(expert_slice(w), "fsdp", axis=1, tiled=True)
        for w in (w_gate, w_up, w_down)
    )
    gain_first_all, gain_second_all = (
        lax.all_gather(g, "tp", axis=0, tiled=True).astype(wide) for g in (attn_norm, ffn_norm)
    )

    def in_order(table):
        return table.reshape((ctx_size, tok_rows) + table.shape[1:])[block_order].reshape(table.shape)

    segment, place = locate(in_order(positions[0]), seq_lengths[0])
    cosine, sine_table = rope_tables(place, head_dim)
    ids_all = in_order(lax.all_gather(expert_ids, "ctx", axis=0, tiled=True))
    expert_range = jnp.arange(expert_count, dtype=jnp.int32)
    chosen = jnp.sum(
        (ids_all[:, :, None] == expert_range[None, None, :]).astype(wide), axis=1
    )

    def query_rows(tensor):
        if sharers == 1:
            return tensor
        shape = tensor.shape
        return tensor.reshape((ctx_size // 2, 2, tok_rows) + shape[1:])[:, 0].reshape(
            (shape[0] // 2,) + shape[1:]
        )

    def all_rows(tensor):
        if sharers == 1:
            return tensor
        shape = tensor.shape
        part = tensor.reshape((ctx_size // 2, 1, tok_rows) + shape[1:])
        return jnp.concatenate([part, jnp.zeros_like(part)], axis=1).reshape(
            (shape[0] * 2,) + shape[1:]
        )

    hidden_all = jnp.concatenate(gather_pack(hidden_in), axis=1).astype(wide)
    inv_all = lax.rsqrt(jnp.mean(hidden_all * hidden_all, axis=1, keepdims=True) + norm_eps)
    normed_first = (hidden_all * inv_all * gain_first_all).astype(slim)
    qkv_raw = dot(normed_first, qkv_weight, (1, 0))

    def heads_of(tensor):
        return tensor.reshape(-1, own_heads, head_dim)

    query_raw = heads_of(query_rows(qkv_raw[:, :head_cols]))
    key_raw = heads_of(qkv_raw[:, head_cols : 2 * head_cols])
    value_low = heads_of(qkv_raw[:, 2 * head_cols :]).astype(slim)
    gain_query = query_norm.astype(wide)
    gain_key = key_norm.astype(wide)
    query_turn = (query_rows(cosine), query_rows(sine_table))
    key_turn = (cosine, sine_table)

    def prepare(raw_proj, gain_vec, turn):
        inverse = lax.rsqrt(jnp.mean(raw_proj * raw_proj, axis=2, keepdims=True) + norm_eps)
        return rotate(raw_proj * inverse * gain_vec, *turn).astype(slim), inverse

    query_low, query_inv = prepare(query_raw, gain_query, query_turn)
    key_low, key_inv = prepare(key_raw, gain_key, key_turn)
    same_seq = (query_rows(segment)[:, None] == segment[None, :])[None]

    def scores_of():
        raw_scores = (
            jnp.einsum("qhd,khd->hqk", query_low, key_low, preferred_element_type=wide)
            * score_scale
        )
        return jnp.where(same_seq, raw_scores, -1e30)

    scores = scores_of()
    row_peak = jnp.max(scores, axis=2, keepdims=True)
    row_exp = jnp.exp(scores - row_peak)
    row_sum = jnp.sum(row_exp, axis=2, keepdims=True)
    log_total = row_peak + jnp.log(row_sum)
    probs_low = (row_exp / row_sum).astype(slim)
    attended_low = all_rows(
        jnp.einsum("hqk,khd->qhd", probs_low, value_low, preferred_element_type=wide)
        .reshape(-1, head_cols)
        .astype(slim)
    )
    attn_branch = scatter_pack(dot(attended_low, out_weight, (1, 0)).astype(slim))

    resid_in = hidden_in.astype(wide)
    middle = resid_in + attn_branch
    gain_second = ffn_norm.astype(wide)
    inv_second = lax.rsqrt(row_total(jnp.sum(middle * middle, axis=1)) / width_all + norm_eps)[
        :, None
    ]
    normed_second = jnp.concatenate(
        gather_pack((middle * inv_second * gain_second).astype(slim)), axis=1
    )
    cotangent_all = jnp.concatenate(gather_pack(cotangent), axis=1)

    logits = dot(normed_second, router_full, (1, 1))
    logit_exp = jnp.exp(logits - jnp.max(logits, axis=1, keepdims=True))
    route_probs = logit_exp / jnp.sum(logit_exp, axis=1, keepdims=True)
    gate_weights = route_probs * chosen
    expert_part = 0.0
    back_part = 0.0
    grad_logits = 0.0
    grad_gate_list, grad_up_list, grad_down_list = [], [], []
    for slot in range(own_experts):
        mine = (expert_range == ctx_place * own_experts + slot).astype(wide)[None, :]
        gates = jnp.sum(gate_weights * mine, axis=1, keepdims=True)
        gate_proj = dot(normed_second, gate_weight[slot], (1, 0))
        up_proj = dot(normed_second, up_weight[slot], (1, 0))
        gate_sigmoid = jax.nn.sigmoid(gate_proj)
        activity = gate_proj * gate_sigmoid * up_proj
        mixed_low = (gates * activity).astype(slim)
        expert_part = expert_part + dot(mixed_low, down_weight[slot], (1, 1))
        grad_mixed = dot(cotangent_all, down_weight[slot], (1, 0)).astype(slim).astype(wide)
        grad_gates = jnp.sum(grad_mixed * activity, axis=1, keepdims=True)
        grad_activity = grad_mixed * gates
        grad_gate_low = (
            grad_activity * up_proj * gate_sigmoid * (1.0 + gate_proj * (1.0 - gate_sigmoid))
        ).astype(slim)
        grad_up_low = (grad_activity * gate_proj * gate_sigmoid).astype(slim)
        grad_logits = grad_logits + gates * grad_gates * (mine - route_probs)
        back_part = back_part + dot(grad_gate_low, gate_weight[slot], (1, 1))
        back_part = back_part + dot(grad_up_low, up_weight[slot], (1, 1))
        grad_gate_list.append(dot(normed_second, grad_gate_low, (0, 0)))
        grad_up_list.append(dot(normed_second, grad_up_low, (0, 0)))
        grad_down_list.append(dot(cotangent_all, mixed_low, (0, 0)))
    grad_logits_low = grad_logits.astype(slim)
    back_part = back_part + dot(grad_logits_low, router_full, (1, 0))
    grad_second = scatter_pack(back_part.astype(slim))
    expert_branch = scatter_pack(expert_part.astype(slim))
    hidden_out = (middle + expert_branch).astype(slim)
    grad_router = row_total(
        lax.psum_scatter(
            dot(grad_logits_low, normed_second, (0, 0)).astype(slim),
            ("fsdp", "ctx"),
            scatter_dimension=1,
            tiled=True,
        ).astype(wide)
    )

    def spread_experts(parts):
        mine = lax.psum_scatter(
            jnp.stack(parts).astype(slim), "fsdp", scatter_dimension=1, tiled=True
        )
        return lax.all_to_all(mine, "ctx", split_axis=1, concat_axis=0, tiled=True).astype(wide)

    grad_gate = spread_experts(grad_gate_list)
    grad_up = spread_experts(grad_up_list)
    grad_down = spread_experts(grad_down_list)

    gain_two_grad = jnp.sum(grad_second * middle * inv_second, axis=0)
    second_scaled = grad_second * gain_second
    second_inner = row_total(jnp.sum(second_scaled * middle, axis=1))[:, None]
    grad_middle = (
        cotangent.astype(wide)
        + inv_second * second_scaled
        - middle * inv_second**3 * second_inner / width_all
    )
    grad_middle_all = jnp.concatenate(gather_pack(grad_middle.astype(slim)), axis=1)

    grad_attended = dot(grad_middle_all, out_weight, (1, 1)).astype(slim)
    grad_out_part = dot(attended_low, grad_middle_all, (0, 0))
    probs_back = jnp.exp(scores_of() - log_total)
    grad_att_heads = heads_of(query_rows(grad_attended))
    grad_probs = jnp.einsum(
        "qhd,khd->hqk", grad_att_heads, value_low, preferred_element_type=wide
    )
    grad_scores = (
        probs_back * (grad_probs - jnp.sum(probs_back * grad_probs, axis=2, keepdims=True))
    ).astype(slim)
    grad_query_rot = (
        jnp.einsum("hqk,khd->qhd", grad_scores, key_low, preferred_element_type=wide) * score_scale
    )
    grad_key_rot = (
        jnp.einsum("hqk,qhd->khd", grad_scores, query_low, preferred_element_type=wide)
        * score_scale
    )
    grad_value_low = jnp.einsum(
        "hqk,qhd->khd", probs_back.astype(slim), grad_att_heads, preferred_element_type=wide
    ).astype(slim)

    def prepare_back(grad_rot, raw_proj, inverse, gain_vec, turn):
        grad_normed = unrotate(grad_rot, *turn)
        weighted = grad_normed * gain_vec
        grad_raw = inverse * weighted - raw_proj * inverse**3 * jnp.mean(
            weighted * raw_proj, axis=2, keepdims=True
        )
        gain_grad = jnp.sum(grad_normed * raw_proj * inverse, axis=(0, 1))
        return grad_raw.reshape(-1, head_cols).astype(slim), gain_grad

    grad_query_low, query_gain_grad = prepare_back(
        grad_query_rot, query_raw, query_inv, gain_query, query_turn
    )
    grad_key_low, key_gain_grad = prepare_back(
        grad_key_rot, key_raw, key_inv, gain_key, key_turn
    )
    grad_qkv_low = jnp.concatenate(
        [all_rows(grad_query_low), grad_key_low, grad_value_low.reshape(-1, head_cols)], axis=1
    )
    grad_first = scatter_pack(dot(grad_qkv_low, qkv_weight, (1, 1)).astype(slim))
    grad_qkv_part = dot(normed_first, grad_qkv_low, (0, 0))

    def over_sharers(tensor):
        if sharers == 1:
            return tensor.astype(wide)
        return jnp.sum(
            tensor.reshape((sharers, local_heads) + tensor.shape[1:]).astype(wide), axis=0
        )

    qkv_mine = lax.psum_scatter(
        grad_qkv_part.astype(slim), "fsdp", scatter_dimension=0, tiled=True
    )
    qkv_rows = qkv_mine.shape[0] // ctx_size
    qkv_mine = over_sharers(
        lax.all_to_all(
            qkv_mine.reshape(ctx_size, qkv_rows, 3 * head_cols), "ctx", split_axis=0, concat_axis=0
        )
    )
    grad_query, grad_key, grad_value = (
        jnp.swapaxes(qkv_mine[:, :, i * head_cols : (i + 1) * head_cols], 0, 1).reshape(qkv_rows, -1)
        for i in range(3)
    )
    out_mine = lax.psum_scatter(
        grad_out_part.astype(slim), "fsdp", scatter_dimension=1, tiled=True
    )
    out_cols = out_mine.shape[1] // ctx_size
    out_mine = jnp.swapaxes(out_mine.reshape(head_cols, ctx_size, out_cols), 0, 1)
    grad_out = over_sharers(
        lax.all_to_all(out_mine, "ctx", split_axis=0, concat_axis=0)
    ).reshape(-1, out_cols)

    gain_first = attn_norm.astype(wide)
    inv_first = lax.dynamic_slice_in_dim(inv_all, 0, tok_rows, 0)
    gain_one_grad = jnp.sum(grad_first * resid_in * inv_first, axis=0)
    first_scaled = grad_first * gain_first
    first_inner = row_total(jnp.sum(first_scaled * resid_in, axis=1))[:, None]
    grad_hidden = (
        grad_middle + inv_first * first_scaled - resid_in * inv_first**3 * first_inner / width_all
    )
    gains_part = lax.dynamic_update_slice(
        jnp.zeros((2, width_all), wide),
        jnp.stack([gain_one_grad, gain_two_grad]),
        (0, tp_place * col_count),
    )
    stream_part = jnp.stack(
        [
            jnp.sum(middle * middle),
            jnp.sum(attn_branch * attn_branch),
            jnp.sum(expert_branch * expert_branch),
        ]
    )
    stream_sums, gains_sum, query_gain_sum, key_gain_sum = lax.psum(
        (stream_part, gains_part, query_gain_grad, key_gain_grad), ("fsdp", "ctx", "tp")
    )
    token_count = tok_rows * packs_axis * ctx_size
    stream_rms = jnp.sqrt(stream_sums / (token_count * width_all))
    return (
        hidden_out,
        grad_hidden,
        gains_sum[0],
        gains_sum[1],
        query_gain_sum,
        key_gain_sum,
        grad_query,
        grad_key,
        grad_value,
        grad_out,
        grad_router,
        grad_gate,
        grad_up,
        grad_down,
        stream_rms,
    )


def solution(mesh):
    return jax.shard_map(
        on_device,
        mesh=mesh,
        in_specs=(
            P(("fsdp", "ctx"), "tp"),
            P(("fsdp", "ctx"), "tp"),
            P("fsdp", None),
            P("fsdp", None),
            P(("fsdp", "ctx"), None),
            P("tp"),
            P("tp"),
            P(),
            P(),
            P("fsdp", "tp"),
            P("fsdp", "tp"),
            P("fsdp", "tp"),
            P("tp", "fsdp"),
            P(None, "fsdp"),
            P(None, "fsdp", "tp"),
            P(None, "fsdp", "tp"),
            P(None, "fsdp", "tp"),
        ),
        out_specs=(
            P(("fsdp", "ctx"), "tp"),
            P(("fsdp", "ctx"), "tp"),
            P(),
            P(),
            P(),
            P(),
            P(("fsdp", "ctx"), "tp"),
            P(("fsdp", "ctx"), "tp"),
            P(("fsdp", "ctx"), "tp"),
            P("tp", ("fsdp", "ctx")),
            P(None, ("fsdp", "ctx")),
            P(None, ("fsdp", "ctx"), "tp"),
            P(None, ("fsdp", "ctx"), "tp"),
            P(None, ("fsdp", "ctx"), "tp"),
            P(),
        ),
        check_vma=False,
    )
```

```python
import jax
import jax.numpy as jnp
from jax import lax
from jax.experimental import pallas as pl
from jax.experimental.pallas import tpu as pltpu
from jax.sharding import PartitionSpec as P

norm_eps = 1e-06
rope_base = 10000.0


def locate(pack_spots, lengths_row):
    seq_ends = jnp.cumsum(lengths_row)
    starts = seq_ends - lengths_row
    segment = jnp.sum((pack_spots[:, None] >= seq_ends[None, :]).astype(jnp.int32), axis=1)
    slot_ids = jnp.arange(lengths_row.shape[0], dtype=jnp.int32)
    seq_begin = jnp.sum(
        jnp.where(segment[:, None] == slot_ids[None, :], starts[None, :], 0), axis=1
    )
    return (segment, pack_spots - seq_begin)


def rope_tables(pack_spots, head_dim):
    half_dim = head_dim // 2
    inv_freq = rope_base ** (-(jnp.arange(half_dim, dtype=jnp.float32) * 2.0 / head_dim))
    angle_grid = pack_spots.astype(jnp.float32)[:, None] * inv_freq[None, :]
    cosine, sine = jnp.cos(angle_grid), jnp.sin(angle_grid)
    return jnp.concatenate([cosine, cosine], axis=1), jnp.concatenate([-sine, sine], axis=1)


def unrotate(grad_rot, cosine, sine):
    return grad_rot * cosine + jnp.roll(grad_rot * sine, grad_rot.shape[1] // 2, axis=1)


CHUNKS = 2
MESH_ID = pl.DeviceIdType.MESH
VMEM_LIMIT = 64 * 1000 * 1000


class Pack:
    def __init__(self, ctx_size, tp_size, rows, cols):
        self.line = ctx_size // 2
        self.tp_size, self.rows, self.cols = tp_size, rows, cols
        self.chunk = rows // CHUNKS
        self.steps = self.line * CHUNKS
        place = lax.axis_index("ctx")
        self.a, self.b = place // 2, place % 2
        self.t = lax.axis_index("tp")
        self.has_up, self.has_down = self.a < self.line - 1, self.a > 0

    def up(self):
        return {"ctx": (self.a + 1) * 2 + self.b}

    def down(self):
        return {"ctx": (self.a - 1) * 2 + self.b}

    def pair(self):
        return {"ctx": self.a * 2 + (1 - self.b)}

    def sibling(self, shift):
        return {"tp": self.t ^ shift}

    def meet(self):
        barrier = pltpu.get_barrier_semaphore()

        def greet(device):
            pl.semaphore_signal(barrier, inc=1, device_id=device, device_id_type=MESH_ID)

        @pl.when(self.has_up)
        def _():
            greet(self.up())

        @pl.when(self.has_down)
        def _():
            greet(self.down())

        greet(self.pair())
        for shift in range(1, self.tp_size):
            greet(self.sibling(shift))
        pl.semaphore_wait(
            barrier,
            self.tp_size + jnp.where(self.has_up, 1, 0) + jnp.where(self.has_down, 1, 0),
        )

    def row0(self, block, k):
        return pl.multiple_of(block * self.rows + k * self.chunk, self.chunk)

    def region(self, ref, block, k, part):
        return ref.at[
            pl.ds(self.row0(block, k), self.chunk),
            pl.ds(pl.multiple_of(part * self.cols, self.cols), self.cols),
        ]


def remote(src, dst, send_sem, recv_sem, device):
    return pltpu.make_async_remote_copy(
        src_ref=src,
        dst_ref=dst,
        send_sem=send_sem,
        recv_sem=recv_sem,
        device_id=device,
        device_id_type=MESH_ID,
    )


def loop(count, body):
    lax.fori_loop(0, count, lambda i, carry: (body(i), carry)[1], 0)


def gather_scratch(ctx_size, tp_size, rows, cols, dtype):
    line, dma = ctx_size // 2, pltpu.SemaphoreType.DMA
    return [
        pltpu.VMEM((ctx_size * rows, tp_size * cols), dtype),
        dma((2 * line * CHUNKS,)),
        dma((2 * line * CHUNKS,)),
        dma((4 * line * (tp_size - 1) * CHUNKS,)),
        dma((ctx_size * CHUNKS,)),
        dma(((tp_size - 1) * ctx_size * CHUNKS,)),
        dma,
    ]


def gather_steps(pack, src, scratch, before, compute):
    buf, line_sems, pair_sems, tp_sems, own_sems, sib_sems, local_sem = scratch
    line, t, a, b = pack.line, pack.t, pack.a, pack.b
    ctx_size = 2 * line

    def part(block, k):
        return pack.region(buf, block, k, t)

    def line_copy(piece, block, k, down, dist):
        return remote(
            piece,
            part(block, k),
            line_sems.at[(down * line + dist) * CHUNKS + k],
            own_sems.at[block * CHUNKS + k],
            pack.down() if down else pack.up(),
        )

    def pair_copy(piece, block, k, slot):
        return remote(
            piece,
            part(block, k),
            pair_sems.at[slot * CHUNKS + k],
            own_sems.at[block * CHUNKS + k],
            pack.pair(),
        )

    def tp_copy(piece, block, k, slot, shift):
        return remote(
            piece,
            part(block, k),
            tp_sems.at[(slot * (pack.tp_size - 1) + shift - 1) * CHUNKS + k],
            sib_sems.at[((shift - 1) * ctx_size + block) * CHUNKS + k],
            pack.sibling(shift),
        )

    def send_tp(piece, block, k, slot):
        for shift in range(1, pack.tp_size):
            tp_copy(piece, block, k, slot, shift).start()

    def await_own(block, k):
        piece = part(block, k)
        pair_copy(piece, block, k, 0).wait_recv()

    pack.meet()
    mine = a * 2 + b
    own_copy = pltpu.make_async_copy(
        src,
        buf.at[
            pl.ds(pl.multiple_of(mine * pack.rows, pack.rows), pack.rows),
            pl.ds(pl.multiple_of(t * pack.cols, pack.cols), pack.cols),
        ],
        local_sem,
    )
    own_copy.start()
    for k in range(CHUNKS):
        piece = src.at[pl.ds(k * pack.chunk, pack.chunk), :]

        @pl.when(pack.has_up)
        def _():
            line_copy(piece, mine, k, 0, 0).start()

        @pl.when(pack.has_down)
        def _():
            line_copy(piece, mine, k, 1, 0).start()

        pair_copy(piece, mine, k, 0).start()
    for k in range(CHUNKS):
        send_tp(src.at[pl.ds(k * pack.chunk, pack.chunk), :], mine, k, 0)
    before()
    own_copy.wait()

    def ways(dist):
        below, above = a - dist, a + dist
        return (
            (0, below, below >= 0, jnp.logical_and(below >= 0, pack.has_up)),
            (1, above, above < line, jnp.logical_and(above < line, pack.has_down)),
        )

    def from_line(dist, k):
        for down, node, there, onward in ways(dist):
            block = node * 2 + b

            @pl.when(there)
            def _():
                await_own(block, k)

            @pl.when(onward)
            def _():
                line_copy(part(block, k), block, k, down, dist).start()

            @pl.when(there)
            def _():
                pair_copy(part(block, k), block, k, down * line + dist).start()
                send_tp(part(block, k), block, k, down * line + dist)

    def from_pair(dist, k):
        for down, node, there, _ in ways(dist):
            block = node * 2 + (1 - b)
            if down:
                there = jnp.logical_and(there, dist > 0)

            @pl.when(there)
            def _():
                await_own(block, k)
                send_tp(part(block, k), block, k, (2 + down) * line + dist)

    def work(block, k):
        for shift in range(1, pack.tp_size):
            piece = pack.region(buf, block, k, t ^ shift)
            remote(
                piece,
                piece,
                tp_sems.at[0],
                sib_sems.at[((shift - 1) * ctx_size + block) * CHUNKS + k],
                pack.sibling(shift),
            ).wait_recv()
        compute(pack.row0(block, k), block * CHUNKS + k)

    def step(s):
        dist, k = s // CHUNKS, s % CHUNKS

        @pl.when(dist + 1 < line)
        def _():
            from_line(dist + 1, k)

        @pl.when(s < pack.steps)
        def _():
            from_pair(dist, k)

        def side(i):
            late = s - i
            node, late_k = a ^ (late // CHUNKS), late % CHUNKS

            @pl.when(jnp.logical_and(late >= 0, late < pack.steps))
            def _():
                work(node * 2 + jnp.where(i == 0, b, 1 - b), late_k)

        loop(2, side)

    loop(pack.steps + 1, step)

    def drain(s):
        dist, k = s // CHUNKS, s % CHUNKS
        piece = part(0, 0)
        for down, _, there, onward in ways(dist):

            @pl.when(jnp.logical_and(onward, dist < line - 1))
            def _():
                line_copy(piece, 0, k, down, dist).wait_send()

            if down:
                there = jnp.logical_and(there, dist > 0)

            @pl.when(there)
            def _():
                pair_copy(piece, 0, k, down * line + dist).wait_send()
                for shift in range(1, pack.tp_size):
                    tp_copy(piece, 0, k, down * line + dist, shift).wait_send()
                    tp_copy(piece, 0, k, (2 + down) * line + dist, shift).wait_send()

    loop(pack.steps, drain)


def scatter_scratch(ctx_size, tp_size, rows, cols):
    line, dma = ctx_size // 2, pltpu.SemaphoreType.DMA
    low = jnp.bfloat16
    return [
        pltpu.VMEM((ctx_size * rows, tp_size * cols), low),
        pltpu.VMEM(((tp_size - 1) * ctx_size * rows, cols), low),
        pltpu.VMEM((line * rows, cols), low),
        pltpu.VMEM((2 * line * rows, cols), low),
        dma(((tp_size - 1) * ctx_size * CHUNKS,)),
        dma((line * CHUNKS,)),
        dma((line * CHUNKS,)),
        dma(((tp_size - 1) * ctx_size * CHUNKS,)),
        dma((line * CHUNKS,)),
        dma((2 * line * CHUNKS,)),
    ]


def scatter_steps(pack, scratch, before, compute, finish):
    (full, sib_buf, pair_buf, line_buf, tp_send, pair_send, line_send, tp_recv, pair_recv, line_recv) = scratch
    line, t, a, b = pack.line, pack.t, pack.a, pack.b
    ctx_size = 2 * line
    wide, low = jnp.float32, jnp.bfloat16
    table = [
        sorted(range(line), key=lambda o, node=node: (-abs(o - node), o)) for node in range(line)
    ]

    def owner(i):
        result = jnp.int32(0)
        for node in range(line):
            for place in range(line):
                here = jnp.logical_and(a == node, i == place)
                result = jnp.where(here, table[node][place], result)
        return result

    def tp_copy(block, k, shift):
        return remote(
            pack.region(full, block, k, t ^ shift),
            sib_buf.at[
                pl.ds(pack.row0((shift - 1) * ctx_size + block, k), pack.chunk), :
            ],
            tp_send.at[((shift - 1) * ctx_size + block) * CHUNKS + k],
            tp_recv.at[((shift - 1) * ctx_size + block) * CHUNKS + k],
            pack.sibling(shift),
        )

    def pair_copy(node, k):
        return remote(
            pack.region(full, node * 2 + (1 - b), k, t),
            pair_buf.at[pl.ds(pack.row0(node, k), pack.chunk), :],
            pair_send.at[node * CHUNKS + k],
            pair_recv.at[node * CHUNKS + k],
            pack.pair(),
        )

    def line_copy(node, k, down):
        return remote(
            pack.region(full, node * 2 + b, k, t),
            line_buf.at[pl.ds(pack.row0(down * line + node, k), pack.chunk), :],
            line_send.at[node * CHUNKS + k],
            line_recv.at[(down * line + node) * CHUNKS + k],
            pack.down() if down else pack.up(),
        )

    def own_part(block, k):
        return full[
            pl.ds(pack.row0(block, k), pack.chunk),
            pl.ds(pl.multiple_of(t * pack.cols, pack.cols), pack.cols),
        ].astype(wide)

    def put_part(block, k, value):
        full[
            pl.ds(pack.row0(block, k), pack.chunk),
            pl.ds(pl.multiple_of(t * pack.cols, pack.cols), pack.cols),
        ] = value.astype(low)

    def landed(ref, block, k):
        return ref[pl.ds(pack.row0(block, k), pack.chunk), :].astype(wide)

    def fill(block, k):
        row0 = pack.row0(block, k)
        full[pl.ds(row0, pack.chunk), :] = compute(row0, block * CHUNKS + k)
        for shift in range(1, pack.tp_size):
            tp_copy(block, k, shift).start()

    def join(block, k):
        total = own_part(block, k)
        for shift in range(1, pack.tp_size):
            tp_copy(block, k, shift).wait_recv()
            total = total + landed(sib_buf, (shift - 1) * ctx_size + block, k)
        put_part(block, k, total)

    pack.meet()
    before()

    def step(s):
        @pl.when(s < pack.steps)
        def _():
            node, k = owner(s // CHUNKS), s % CHUNKS

            def side(i):
                fill(node * 2 + jnp.where(i == 0, 1 - b, b), k)

            loop(2, side)

        late = s - 1

        @pl.when(jnp.logical_and(late >= 0, late < pack.steps))
        def _():
            node, k = owner(late // CHUNKS), late % CHUNKS

            def side(i):
                join(node * 2 + jnp.where(i == 0, 1 - b, b), k)

                @pl.when(i == 0)
                def _():
                    pair_copy(node, k).start()

            loop(2, side)

        later = s - 2

        @pl.when(later >= 0)
        def _():
            node, k = owner(later // CHUNKS), later % CHUNKS
            pair_copy(node, k).wait_recv()
            put_part(
                node * 2 + b, k, own_part(node * 2 + b, k) + landed(pair_buf, node, k)
            )
            from_below = jnp.logical_and(pack.has_down, node >= a)
            from_above = jnp.logical_and(pack.has_up, node <= a)
            for down, there in ((0, from_below), (1, from_above)):

                @pl.when(there)
                def _():
                    line_copy(node, k, down).wait_recv()
                    put_part(
                        node * 2 + b,
                        k,
                        own_part(node * 2 + b, k) + landed(line_buf, down * line + node, k),
                    )

            @pl.when(node > a)
            def _():
                line_copy(node, k, 0).start()

            @pl.when(node < a)
            def _():
                line_copy(node, k, 1).start()

            @pl.when(node == a)
            def _():
                finish(k, own_part(node * 2 + b, k))

    loop(pack.steps + 2, step)

    def drain(s):
        node, k = s // CHUNKS, s % CHUNKS
        pair_copy(node, k).wait_send()
        for shift in range(1, pack.tp_size):
            tp_copy(node * 2, k, shift).wait_send()
            tp_copy(node * 2 + 1, k, shift).wait_send()

        @pl.when(node > a)
        def _():
            line_copy(node, k, 0).wait_send()

        @pl.when(node < a)
        def _():
            line_copy(node, k, 1).wait_send()

    loop(pack.steps, drain)


ANY = pl.BlockSpec(memory_space=pl.ANY)


def nn_dot(left, right):
    return lax.dot_general(
        left, right, (((1,), (0,)), ((), ())), preferred_element_type=jnp.float32
    )


def nt_dot(left, right):
    return lax.dot_general(
        left, right, (((1,), (1,)), ((), ())), preferred_element_type=jnp.float32
    )


def pack_gather_call(sizes, tensor, resident, outs, piece, collective_id, keep, flops):
    ctx_size, tp_size = sizes
    rows, cols = tensor.shape
    full = (ctx_size * rows, tp_size * cols)
    count = len(outs)
    pieces = ctx_size * CHUNKS
    dma = pltpu.SemaphoreType.DMA
    base = gather_scratch(ctx_size, tp_size, rows, cols, tensor.dtype)

    def kernel(*refs):
        src, refs = refs[0], refs[1:]
        held_hbm, refs = refs[: len(resident)], refs[len(resident) :]
        out_refs, refs = refs[: count + keep], refs[count + keep :]
        scratch, refs = refs[: len(base)], refs[len(base) :]
        held, refs = refs[: len(resident)], refs[len(resident) :]
        stage, refs = refs[:count], refs[count:]
        held_sem, out_sem = refs
        pack = Pack(ctx_size, tp_size, rows, cols)
        loads = [
            pltpu.make_async_copy(h, v, held_sem.at[i])
            for i, (h, v) in enumerate(zip(held_hbm, held))
        ]

        def before():
            for load in loads:
                load.wait()

        def stores(row0, index):
            window = pl.ds(row0, pack.chunk)
            pairs = list(zip(stage, out_refs))
            if keep:
                pairs.append((scratch[0], out_refs[count]))
            return [
                pltpu.make_async_copy(
                    here.at[window, :], there.at[window, :], out_sem.at[i * pieces + index]
                )
                for i, (here, there) in enumerate(pairs)
            ]

        def compute(row0, index):
            window = pl.ds(row0, pack.chunk)
            for ref, value in zip(stage, piece(scratch[0][window, :], window, held)):
                ref[window, :] = value.astype(ref.dtype)
            for store in stores(row0, index):
                store.start()

        for load in loads:
            load.start()
        gather_steps(pack, src, scratch, before, compute)

        def finish(index):
            for store in stores(pl.multiple_of(index * pack.chunk, pack.chunk), index):
                store.wait()

        loop(pieces, finish)

    shapes = [jax.ShapeDtypeStruct((full[0], width), dtype) for width, dtype in outs]
    if keep:
        shapes.append(jax.ShapeDtypeStruct(full, tensor.dtype))
    return pl.pallas_call(
        kernel,
        out_shape=tuple(shapes),
        in_specs=[ANY] * (1 + len(resident)),
        out_specs=tuple([ANY] * len(shapes)),
        scratch_shapes=base
        + [pltpu.VMEM(r.shape, r.dtype) for r in resident]
        + [pltpu.VMEM((full[0], width), dtype) for width, dtype in outs]
        + [dma((len(resident),)), dma((max(1, len(shapes)) * pieces,))],
        compiler_params=pltpu.CompilerParams(
            collective_id=collective_id, has_side_effects=True, vmem_limit_bytes=VMEM_LIMIT
        ),
        cost_estimate=pl.CostEstimate(
            flops=flops, bytes_accessed=4 * full[0] * full[1] * 2, transcendentals=0
        ),
    )(tensor, *resident)


def pack_scatter_call(sizes, shape, resident, piece, collective_id, flops):
    ctx_size, tp_size = sizes
    rows, cols = shape
    dma = pltpu.SemaphoreType.DMA
    base = scatter_scratch(ctx_size, tp_size, rows, cols)

    def kernel(*refs):
        held_hbm, refs = refs[: len(resident)], refs[len(resident) :]
        out_ref, refs = refs[0], refs[1:]
        scratch, refs = refs[: len(base)], refs[len(base) :]
        held, held_sem = refs[: len(resident)], refs[len(resident)]
        pack = Pack(ctx_size, tp_size, rows, cols)
        loads = [
            pltpu.make_async_copy(h, v, held_sem.at[i])
            for i, (h, v) in enumerate(zip(held_hbm, held))
        ]

        def before():
            for load in loads:
                load.wait()

        def compute(row0, index):
            return piece(pl.ds(row0, pack.chunk), held).astype(jnp.bfloat16)

        def finish(k, total):
            out_ref[pl.ds(pl.multiple_of(k * pack.chunk, pack.chunk), pack.chunk), :] = total

        for load in loads:
            load.start()
        scatter_steps(pack, scratch, before, compute, finish)

    return pl.pallas_call(
        kernel,
        out_shape=jax.ShapeDtypeStruct(shape, jnp.float32),
        in_specs=[ANY] * len(resident),
        out_specs=pl.BlockSpec(memory_space=pltpu.VMEM),
        scratch_shapes=base
        + [pltpu.VMEM(r.shape, r.dtype) for r in resident]
        + [dma((len(resident),))],
        compiler_params=pltpu.CompilerParams(
            collective_id=collective_id, has_side_effects=True, vmem_limit_bytes=VMEM_LIMIT
        ),
        cost_estimate=pl.CostEstimate(
            flops=flops,
            bytes_accessed=4 * ctx_size * rows * tp_size * cols * 2,
            transcendentals=0,
        ),
    )(*resident)


def on_device(
    hidden_in,
    cotangent,
    positions,
    seq_lengths,
    expert_ids,
    attn_norm,
    ffn_norm,
    query_norm,
    key_norm,
    w_query,
    w_key,
    w_value,
    w_out,
    w_router,
    w_gate,
    w_up,
    w_down,
):
    tok_rows, col_count = hidden_in.shape
    ctx_size, tp_size = lax.axis_size("ctx"), lax.axis_size("tp")
    sizes = (ctx_size, tp_size)
    ctx_place, tp_place = lax.axis_index("ctx"), lax.axis_index("tp")
    width_all = col_count * tp_size
    pack_rows = tok_rows * ctx_size
    head_dim = query_norm.shape[0]
    local_heads = w_query.shape[1] // head_dim
    expert_count, hidden_units = w_gate.shape[0], w_gate.shape[2]
    own_experts = expert_count // ctx_size
    sharers = ctx_size // local_heads
    shared_rows = pack_rows // sharers
    score_scale = head_dim ** (-0.5)
    wide = jnp.float32
    slim = jnp.bfloat16
    lanes = 128

    def row_total(tensor):
        return lax.psum(tensor, "tp")

    def dot(left, right, dims):
        return lax.dot_general(
            left, right, ((dims[:1], dims[1:]), ((), ())), preferred_element_type=wide
        )

    head_place = ctx_place % local_heads

    def head_slice(weight, axis):
        return lax.dynamic_slice_in_dim(weight, head_place * head_dim, head_dim, axis)

    def expert_slice(weight):
        return lax.dynamic_slice_in_dim(weight, ctx_place * own_experts, own_experts, 0)

    qkv_weight = lax.all_gather(
        jnp.concatenate([head_slice(w, 1) for w in (w_query, w_key, w_value)], axis=1),
        "fsdp",
        axis=0,
        tiled=True,
    )
    out_weight = lax.all_gather(head_slice(w_out, 0), "fsdp", axis=1, tiled=True)
    router_full = lax.all_gather(w_router, "fsdp", axis=1, tiled=True)
    router_pad = jnp.pad(router_full, ((0, lanes - expert_count), (0, 0)))
    gate_weight, up_weight, down_weight = (
        lax.all_gather(expert_slice(w), "fsdp", axis=1, tiled=True)
        for w in (w_gate, w_up, w_down)
    )
    gain_first_all = lax.all_gather(attn_norm, "tp", axis=0, tiled=True).astype(wide)[None, :]

    segment, place = locate(positions[0], seq_lengths[0])
    cosine, sine = rope_tables(place, head_dim)
    ids_all = lax.all_gather(expert_ids, "ctx", axis=0, tiled=True)
    chosen = jnp.sum(
        (ids_all[:, :, None] == jnp.arange(lanes, dtype=jnp.int32)[None, None, :]).astype(wide),
        axis=1,
    ).astype(slim)

    share = ctx_place // local_heads

    def query_rows(tensor):
        if sharers == 1:
            return tensor
        return lax.dynamic_slice_in_dim(tensor, share * shared_rows, shared_rows, 0)

    def all_rows(tensor):
        if sharers == 1:
            return tensor
        return lax.dynamic_update_slice_in_dim(
            jnp.zeros((pack_rows,) + tensor.shape[1:], tensor.dtype),
            tensor,
            share * shared_rows,
            0,
        )

    def project(rows, window, held):
        weight, gain, cos_table, sin_table, gain_q, gain_k = held
        hidden = rows.astype(wide)
        inverse = lax.rsqrt(jnp.mean(hidden * hidden, axis=1, keepdims=True) + norm_eps)
        normed = (hidden * inverse * gain[...]).astype(slim)
        raw = nn_dot(normed, weight[...])
        cos_rows, sin_rows = cos_table[window, :], sin_table[window, :]

        def prepare(raw_proj, gain_vec):
            inv = lax.rsqrt(jnp.mean(raw_proj * raw_proj, axis=1, keepdims=True) + norm_eps)
            scaled = raw_proj * inv * gain_vec[...]
            return scaled * cos_rows + pltpu.roll(scaled, head_dim // 2, 1) * sin_rows

        query_raw = raw[:, :head_dim]
        key_raw = raw[:, head_dim : 2 * head_dim]
        return (
            normed,
            jnp.broadcast_to(inverse, (rows.shape[0], lanes)),
            query_raw,
            key_raw,
            prepare(query_raw, gain_q),
            prepare(key_raw, gain_k),
            raw[:, 2 * head_dim :],
        )

    gain_query = query_norm.astype(wide)[None, :]
    gain_key = key_norm.astype(wide)[None, :]
    normed_first, inv_all, query_raw, key_raw, query_low, key_low, value_low = pack_gather_call(
        sizes,
        hidden_in,
        (qkv_weight, gain_first_all, cosine, sine, gain_query, gain_key),
        (
            (width_all, slim),
            (lanes, wide),
            (head_dim, wide),
            (head_dim, wide),
            (head_dim, slim),
            (head_dim, slim),
            (head_dim, slim),
        ),
        project,
        1,
        False,
        6 * pack_rows * width_all * head_dim,
    )
    (cotangent_all,) = pack_gather_call(
        sizes, cotangent, (gain_query,), (), lambda rows, window, held: (), 2, True, 0
    )

    query_raw, query_low = query_rows(query_raw), query_rows(query_low)
    query_turn = (query_rows(cosine), query_rows(sine))
    same_seq = query_rows(segment)[:, None] == segment[None, :]

    def scores_of():
        return jnp.where(same_seq, dot(query_low, key_low, (1, 1)) * score_scale, -1e30)

    scores = scores_of()
    row_peak = jnp.max(scores, axis=1, keepdims=True)
    row_exp = jnp.exp(scores - row_peak)
    row_sum = jnp.sum(row_exp, axis=1, keepdims=True)
    log_total = row_peak + jnp.log(row_sum)
    probs_low = (row_exp / row_sum).astype(slim)
    attended_low = all_rows(dot(probs_low, value_low, (1, 0)).astype(slim))
    attn_branch = pack_scatter_call(
        sizes,
        (tok_rows, col_count),
        (attended_low, out_weight),
        lambda window, held: nn_dot(held[0][window, :], held[1][...]),
        3,
        2 * pack_rows * width_all * head_dim,
    )

    resid_in = hidden_in.astype(wide)
    middle = resid_in + attn_branch
    gain_second = ffn_norm.astype(wide)
    inv_second = lax.rsqrt(row_total(jnp.sum(middle * middle, axis=1)) / width_all + norm_eps)[
        :, None
    ]

    def experts(rows, window, held):
        gate_w, up_w, down_w, router_w, chosen_ref, cotangent_ref = held
        lane = lax.broadcasted_iota(jnp.int32, (rows.shape[0], lanes), 1)
        logits = jnp.where(lane < expert_count, nt_dot(rows, router_w[...]), -1e30)
        logit_exp = jnp.exp(logits - jnp.max(logits, axis=1, keepdims=True))
        route_probs = logit_exp / jnp.sum(logit_exp, axis=1, keepdims=True)
        gate_weights = route_probs * chosen_ref[window, :].astype(wide)
        first_expert = lax.axis_index("ctx") * own_experts
        rows_grad = cotangent_ref[window, :]
        grad_logits = jnp.zeros((rows.shape[0], lanes), wide)
        mixed_list, gate_list, up_list = [], [], []
        for slot in range(own_experts):
            mine = (lane == first_expert + slot).astype(wide)
            gates = jnp.sum(gate_weights * mine, axis=1, keepdims=True)
            gate_proj = nn_dot(rows, gate_w[slot])
            up_proj = nn_dot(rows, up_w[slot])
            grad_mixed = nn_dot(rows_grad, down_w[slot]).astype(slim).astype(wide)
            gate_sigmoid = jax.nn.sigmoid(gate_proj)
            silu = gate_proj * gate_sigmoid
            activity = silu * up_proj
            mixed_list.append((gates * activity).astype(slim))
            grad_gates = jnp.sum(grad_mixed * activity, axis=1, keepdims=True)
            grad_activity = grad_mixed * gates
            gate_list.append(
                (
                    grad_activity * up_proj * (gate_sigmoid + silu * (1.0 - gate_sigmoid))
                ).astype(slim)
            )
            up_list.append((grad_activity * silu).astype(slim))
            grad_logits = grad_logits + gates * grad_gates * (mine - route_probs)
        return (
            jnp.concatenate(mixed_list, axis=1),
            jnp.concatenate(gate_list, axis=1),
            jnp.concatenate(up_list, axis=1),
            grad_logits,
        )

    own_units = own_experts * hidden_units
    mixed_low, grad_gate_low, grad_up_low, grad_logits_low, normed_second = pack_gather_call(
        sizes,
        (middle * inv_second * gain_second).astype(slim),
        (gate_weight, up_weight, down_weight, router_pad, chosen, cotangent_all),
        ((own_units, slim), (own_units, slim), (own_units, slim), (lanes, slim)),
        experts,
        4,
        True,
        6 * pack_rows * width_all * own_units,
    )

    def back(window, held):
        gate_grad, up_grad, logit_grad, gate_w, up_w, router_w = held
        total = nn_dot(logit_grad[window, :], router_w[...])
        for slot in range(own_experts):
            units = pl.ds(slot * hidden_units, hidden_units)
            total = total + nt_dot(gate_grad[window, units], gate_w[slot])
            total = total + nt_dot(up_grad[window, units], up_w[slot])
        return total

    grad_second = pack_scatter_call(
        sizes,
        (tok_rows, col_count),
        (grad_gate_low, grad_up_low, grad_logits_low, gate_weight, up_weight, router_pad),
        back,
        5,
        4 * pack_rows * width_all * own_units,
    )

    def units_of(tensor, slot):
        return tensor[:, slot * hidden_units : (slot + 1) * hidden_units]

    def spread_experts(left, right):
        parts = jnp.stack(
            [dot(left, units_of(right, slot), (0, 0)).astype(slim) for slot in range(own_experts)]
        )
        mine = lax.psum_scatter(parts, "fsdp", scatter_dimension=1, tiled=True)
        return lax.all_to_all(mine, "ctx", split_axis=1, concat_axis=0, tiled=True).astype(wide)

    grad_gate = spread_experts(normed_second, grad_gate_low)
    grad_up = spread_experts(normed_second, grad_up_low)
    grad_down = spread_experts(cotangent_all, mixed_low)
    grad_router = row_total(
        lax.psum_scatter(
            dot(grad_logits_low[:, :expert_count], normed_second, (0, 0)).astype(slim),
            ("fsdp", "ctx"),
            scatter_dimension=1,
            tiled=True,
        ).astype(wide)
    )

    gain_two_grad = jnp.sum(grad_second * middle * inv_second, axis=0)
    second_scaled = grad_second * gain_second
    second_inner = row_total(jnp.sum(second_scaled * middle, axis=1))[:, None]
    grad_middle = (
        cotangent.astype(wide)
        + inv_second * second_scaled
        - middle * inv_second**3 * second_inner / width_all
    )

    grad_attended, grad_middle_all = pack_gather_call(
        sizes,
        grad_middle.astype(slim),
        (out_weight,),
        ((head_dim, slim),),
        lambda rows, window, held: (nt_dot(rows, held[0][...]),),
        6,
        True,
        2 * pack_rows * width_all * head_dim,
    )
    grad_out_part = dot(attended_low, grad_middle_all, (0, 0))
    probs_back = jnp.exp(scores_of() - log_total)
    grad_att_rows = query_rows(grad_attended)
    grad_probs = dot(grad_att_rows, value_low, (1, 1))
    grad_scores = (
        probs_back * (grad_probs - jnp.sum(probs_back * grad_probs, axis=1, keepdims=True))
    ).astype(slim)
    grad_query_rot = dot(grad_scores, key_low, (1, 0)) * score_scale
    grad_key_rot = dot(grad_scores, query_low, (0, 0)) * score_scale
    grad_value_low = dot(probs_back.astype(slim), grad_att_rows, (0, 0)).astype(slim)

    expert_branch = pack_scatter_call(
        sizes,
        (tok_rows, col_count),
        (mixed_low, down_weight),
        lambda window, held: sum(
            nt_dot(held[0][window, pl.ds(slot * hidden_units, hidden_units)], held[1][slot])
            for slot in range(own_experts)
        ),
        7,
        2 * pack_rows * width_all * own_units,
    )
    hidden_out = (middle + expert_branch).astype(slim)

    def prepare_back(grad_rot, raw_proj, gain_vec, turn):
        inverse = lax.rsqrt(jnp.mean(raw_proj * raw_proj, axis=1, keepdims=True) + norm_eps)
        grad_normed = unrotate(grad_rot, *turn)
        weighted = grad_normed * gain_vec
        grad_raw = inverse * weighted - raw_proj * inverse**3 * jnp.mean(
            weighted * raw_proj, axis=1, keepdims=True
        )
        gain_grad = jnp.sum(grad_normed * raw_proj * inverse, axis=0)
        return grad_raw.astype(slim), gain_grad

    grad_query_low, query_gain_grad = prepare_back(
        grad_query_rot, query_raw, gain_query, query_turn
    )
    grad_key_low, key_gain_grad = prepare_back(grad_key_rot, key_raw, gain_key, (cosine, sine))
    grad_qkv_low = jnp.concatenate(
        [all_rows(grad_query_low), grad_key_low, grad_value_low], axis=1
    )
    grad_first = pack_scatter_call(
        sizes,
        (tok_rows, col_count),
        (grad_qkv_low, qkv_weight),
        lambda window, held: nt_dot(held[0][window, :], held[1][...]),
        8,
        6 * pack_rows * width_all * head_dim,
    )
    grad_qkv_part = dot(normed_first, grad_qkv_low, (0, 0))

    def over_sharers(tensor):
        if sharers == 1:
            return tensor.astype(wide)
        return jnp.sum(
            tensor.reshape((sharers, local_heads) + tensor.shape[1:]).astype(wide), axis=0
        )

    qkv_mine = lax.psum_scatter(
        grad_qkv_part.astype(slim), "fsdp", scatter_dimension=0, tiled=True
    )
    qkv_rows = qkv_mine.shape[0] // ctx_size
    qkv_mine = over_sharers(
        lax.all_to_all(
            qkv_mine.reshape(ctx_size, qkv_rows, 3 * head_dim), "ctx", split_axis=0, concat_axis=0
        )
    )
    grad_query, grad_key, grad_value = (
        jnp.swapaxes(qkv_mine[:, :, i * head_dim : (i + 1) * head_dim], 0, 1).reshape(qkv_rows, -1)
        for i in range(3)
    )
    out_mine = lax.psum_scatter(
        grad_out_part.astype(slim), "fsdp", scatter_dimension=1, tiled=True
    )
    out_cols = out_mine.shape[1] // ctx_size
    out_mine = jnp.swapaxes(out_mine.reshape(head_dim, ctx_size, out_cols), 0, 1)
    grad_out = over_sharers(
        lax.all_to_all(out_mine, "ctx", split_axis=0, concat_axis=0)
    ).reshape(-1, out_cols)

    gain_first = attn_norm.astype(wide)
    inv_first = lax.dynamic_slice_in_dim(inv_all, ctx_place * tok_rows, tok_rows, 0)[:, :1]
    gain_one_grad = jnp.sum(grad_first * resid_in * inv_first, axis=0)
    first_scaled = grad_first * gain_first
    first_inner = row_total(jnp.sum(first_scaled * resid_in, axis=1))[:, None]
    grad_hidden = (
        grad_middle + inv_first * first_scaled - resid_in * inv_first**3 * first_inner / width_all
    )
    gains_part = lax.dynamic_update_slice(
        jnp.zeros((2, width_all), wide),
        jnp.stack([gain_one_grad, gain_two_grad]),
        (0, tp_place * col_count),
    )
    stream_part = jnp.stack(
        [
            jnp.sum(middle * middle),
            jnp.sum(attn_branch * attn_branch),
            jnp.sum(expert_branch * expert_branch),
        ]
    )
    stream_sums, gains_sum, query_gain_sum, key_gain_sum = lax.psum(
        (stream_part, gains_part, query_gain_grad, key_gain_grad), ("fsdp", "ctx", "tp")
    )
    token_count = tok_rows * lax.axis_size("fsdp") * ctx_size
    stream_rms = jnp.sqrt(stream_sums / (token_count * width_all))
    return (
        hidden_out,
        grad_hidden,
        gains_sum[0],
        gains_sum[1],
        query_gain_sum,
        key_gain_sum,
        grad_query,
        grad_key,
        grad_value,
        grad_out,
        grad_router,
        grad_gate,
        grad_up,
        grad_down,
        stream_rms,
    )


def solution(mesh):
    return jax.shard_map(
        on_device,
        mesh=mesh,
        in_specs=(
            P(("fsdp", "ctx"), "tp"),
            P(("fsdp", "ctx"), "tp"),
            P("fsdp", None),
            P("fsdp", None),
            P(("fsdp", "ctx"), None),
            P("tp"),
            P("tp"),
            P(),
            P(),
            P("fsdp", "tp"),
            P("fsdp", "tp"),
            P("fsdp", "tp"),
            P("tp", "fsdp"),
            P(None, "fsdp"),
            P(None, "fsdp", "tp"),
            P(None, "fsdp", "tp"),
            P(None, "fsdp", "tp"),
        ),
        out_specs=(
            P(("fsdp", "ctx"), "tp"),
            P(("fsdp", "ctx"), "tp"),
            P(),
            P(),
            P(),
            P(),
            P(("fsdp", "ctx"), "tp"),
            P(("fsdp", "ctx"), "tp"),
            P(("fsdp", "ctx"), "tp"),
            P("tp", ("fsdp", "ctx")),
            P(None, ("fsdp", "ctx")),
            P(None, ("fsdp", "ctx"), "tp"),
            P(None, ("fsdp", "ctx"), "tp"),
            P(None, ("fsdp", "ctx"), "tp"),
            P(),
        ),
        check_vma=False,
    )
```

```python
import jax
import jax.numpy as jnp
from jax import lax
from jax.experimental import pallas as pl
from jax.experimental.pallas import tpu as pltpu
from jax.sharding import PartitionSpec as P

norm_eps = 1e-06
rope_base = 10000.0


def locate(pack_spots, lengths_row):
    seq_ends = jnp.cumsum(lengths_row)
    starts = seq_ends - lengths_row
    segment = jnp.sum((pack_spots[:, None] >= seq_ends[None, :]).astype(jnp.int32), axis=1)
    slot_ids = jnp.arange(lengths_row.shape[0], dtype=jnp.int32)
    seq_begin = jnp.sum(
        jnp.where(segment[:, None] == slot_ids[None, :], starts[None, :], 0), axis=1
    )
    return (segment, pack_spots - seq_begin)


def rope_tables(pack_spots, head_dim):
    half_dim = head_dim // 2
    inv_freq = rope_base ** (-(jnp.arange(half_dim, dtype=jnp.float32) * 2.0 / head_dim))
    angle_grid = pack_spots.astype(jnp.float32)[:, None] * inv_freq[None, :]
    cosine, sine = jnp.cos(angle_grid), jnp.sin(angle_grid)
    return jnp.concatenate([cosine, cosine], axis=1), jnp.concatenate([-sine, sine], axis=1)


def unrotate(grad_rot, cosine, sine):
    return grad_rot * cosine + jnp.roll(grad_rot * sine, grad_rot.shape[1] // 2, axis=1)


CHUNKS = 2
MESH_ID = pl.DeviceIdType.MESH
VMEM_LIMIT = 64 * 1000 * 1000


class Pack:
    def __init__(self, ctx_size, tp_size, rows, cols, packs=1):
        self.line = ctx_size // 2
        self.packs = packs
        self.tp_size, self.rows, self.cols = tp_size, rows, cols
        self.chunk = rows // CHUNKS
        self.steps = self.line * CHUNKS
        place = lax.axis_index("ctx")
        self.a, self.b = place // 2, place % 2
        self.t = lax.axis_index("tp")
        self.has_up, self.has_down = self.a < self.line - 1, self.a > 0

    def up(self):
        return {"ctx": (self.a + 1) * 2 + self.b}

    def down(self):
        return {"ctx": (self.a - 1) * 2 + self.b}

    def pair(self):
        return {"ctx": self.a * 2 + (1 - self.b)}

    def sibling(self, shift):
        return {"tp": self.t ^ shift}

    def ctx_peer(self, shift):
        return {"ctx": lax.axis_index("ctx") ^ shift}

    def other_pack(self, shift):
        return {"fsdp": lax.axis_index("fsdp") ^ shift}

    def meet(self, everyone):
        barrier = pltpu.get_barrier_semaphore()

        def greet(device):
            pl.semaphore_signal(barrier, inc=1, device_id=device, device_id_type=MESH_ID)

        if everyone:
            near = 2 * self.line - 1
            for shift in range(1, 2 * self.line):
                greet(self.ctx_peer(shift))
        else:
            near = 1 + jnp.where(self.has_up, 1, 0) + jnp.where(self.has_down, 1, 0)

            @pl.when(self.has_up)
            def _():
                greet(self.up())

            @pl.when(self.has_down)
            def _():
                greet(self.down())

            greet(self.pair())
        for shift in range(1, self.tp_size):
            greet(self.sibling(shift))
        for shift in range(1, self.packs):
            greet(self.other_pack(shift))
        pl.semaphore_wait(barrier, near + self.tp_size + self.packs - 2)

    def row0(self, block, k):
        return pl.multiple_of(block * self.rows + k * self.chunk, self.chunk)

    def region(self, ref, block, k, part):
        return ref.at[
            pl.ds(self.row0(block, k), self.chunk),
            pl.ds(pl.multiple_of(part * self.cols, self.cols), self.cols),
        ]


def remote(src, dst, send_sem, recv_sem, device):
    return pltpu.make_async_remote_copy(
        src_ref=src,
        dst_ref=dst,
        send_sem=send_sem,
        recv_sem=recv_sem,
        device_id=device,
        device_id_type=MESH_ID,
    )


def loop(count, body):
    lax.fori_loop(0, count, lambda i, carry: (body(i), carry)[1], 0)


def gather_scratch(ctx_size, tp_size, rows, cols, dtype):
    line, dma = ctx_size // 2, pltpu.SemaphoreType.DMA
    return [
        pltpu.VMEM((ctx_size * rows, tp_size * cols), dtype),
        dma((2 * line * CHUNKS,)),
        dma((2 * line * CHUNKS,)),
        dma((4 * line * (tp_size - 1) * CHUNKS,)),
        dma((ctx_size * CHUNKS,)),
        dma(((tp_size - 1) * ctx_size * CHUNKS,)),
        dma,
    ]


def gather_steps(pack, src, scratch, everyone, lag, begin, before, compute):
    buf, line_sems, pair_sems, tp_sems, own_sems, sib_sems, local_sem = scratch
    line, t, a, b = pack.line, pack.t, pack.a, pack.b
    ctx_size = 2 * line

    def part(block, k):
        return pack.region(buf, block, k, t)

    def line_copy(piece, block, k, down, dist):
        return remote(
            piece,
            part(block, k),
            line_sems.at[(down * line + dist) * CHUNKS + k],
            own_sems.at[block * CHUNKS + k],
            pack.down() if down else pack.up(),
        )

    def pair_copy(piece, block, k, slot):
        return remote(
            piece,
            part(block, k),
            pair_sems.at[slot * CHUNKS + k],
            own_sems.at[block * CHUNKS + k],
            pack.pair(),
        )

    def tp_copy(piece, block, k, slot, shift):
        return remote(
            piece,
            part(block, k),
            tp_sems.at[(slot * (pack.tp_size - 1) + shift - 1) * CHUNKS + k],
            sib_sems.at[((shift - 1) * ctx_size + block) * CHUNKS + k],
            pack.sibling(shift),
        )

    def send_tp(piece, block, k, slot):
        for shift in range(1, pack.tp_size):
            tp_copy(piece, block, k, slot, shift).start()

    def await_own(block, k):
        piece = part(block, k)
        pair_copy(piece, block, k, 0).wait_recv()

    pack.meet(everyone)
    mine = a * 2 + b
    own_copy = pltpu.make_async_copy(
        src,
        buf.at[
            pl.ds(pl.multiple_of(mine * pack.rows, pack.rows), pack.rows),
            pl.ds(pl.multiple_of(t * pack.cols, pack.cols), pack.cols),
        ],
        local_sem,
    )
    own_copy.start()
    for k in range(CHUNKS):
        piece = src.at[pl.ds(k * pack.chunk, pack.chunk), :]

        @pl.when(pack.has_up)
        def _():
            line_copy(piece, mine, k, 0, 0).start()

        @pl.when(pack.has_down)
        def _():
            line_copy(piece, mine, k, 1, 0).start()

        pair_copy(piece, mine, k, 0).start()
    for k in range(CHUNKS):
        send_tp(src.at[pl.ds(k * pack.chunk, pack.chunk), :], mine, k, 0)
    begin()
    own_copy.wait()

    def ways(dist):
        below, above = a - dist, a + dist
        return (
            (0, below, below >= 0, jnp.logical_and(below >= 0, pack.has_up)),
            (1, above, above < line, jnp.logical_and(above < line, pack.has_down)),
        )

    def from_line(dist, k):
        for down, node, there, onward in ways(dist):
            block = node * 2 + b

            @pl.when(there)
            def _():
                await_own(block, k)

            @pl.when(onward)
            def _():
                line_copy(part(block, k), block, k, down, dist).start()

            @pl.when(there)
            def _():
                pair_copy(part(block, k), block, k, down * line + dist).start()
                send_tp(part(block, k), block, k, down * line + dist)

    def from_pair(dist, k):
        for down, node, there, _ in ways(dist):
            block = node * 2 + (1 - b)
            if down:
                there = jnp.logical_and(there, dist > 0)

            @pl.when(there)
            def _():
                await_own(block, k)
                send_tp(part(block, k), block, k, (2 + down) * line + dist)

    def work(block, k, order):
        for shift in range(1, pack.tp_size):
            piece = pack.region(buf, block, k, t ^ shift)
            remote(
                piece,
                piece,
                tp_sems.at[0],
                sib_sems.at[((shift - 1) * ctx_size + block) * CHUNKS + k],
                pack.sibling(shift),
            ).wait_recv()
        compute(pack.row0(block, k), block * CHUNKS + k, order)

    def step(s):
        dist, k = s // CHUNKS, s % CHUNKS

        @pl.when(dist + 1 < line)
        def _():
            from_line(dist + 1, k)

        @pl.when(s < pack.steps)
        def _():
            from_pair(dist, k)

        @pl.when(s == lag)
        def _():
            before()

        turn = s - lag

        def side(i):
            late = turn - i
            node, late_k = a ^ (late // CHUNKS), late % CHUNKS

            @pl.when(jnp.logical_and(late >= 0, late < pack.steps))
            def _():
                order = jnp.where(
                    i == 0,
                    jnp.maximum(2 * turn - 1, 0),
                    jnp.minimum(2 * turn, 2 * pack.steps - 1),
                )
                work(node * 2 + jnp.where(i == 0, b, 1 - b), late_k, order)

        loop(2, side)

    loop(pack.steps + 1 + lag, step)

    def drain(s):
        dist, k = s // CHUNKS, s % CHUNKS
        piece = part(0, 0)
        for down, _, there, onward in ways(dist):

            @pl.when(jnp.logical_and(onward, dist < line - 1))
            def _():
                line_copy(piece, 0, k, down, dist).wait_send()

            if down:
                there = jnp.logical_and(there, dist > 0)

            @pl.when(there)
            def _():
                pair_copy(piece, 0, k, down * line + dist).wait_send()
                for shift in range(1, pack.tp_size):
                    tp_copy(piece, 0, k, down * line + dist, shift).wait_send()
                    tp_copy(piece, 0, k, (2 + down) * line + dist, shift).wait_send()

    loop(pack.steps, drain)


def scatter_scratch(ctx_size, tp_size, rows, cols):
    line, dma = ctx_size // 2, pltpu.SemaphoreType.DMA
    low = jnp.bfloat16
    return [
        pltpu.VMEM((ctx_size * rows, tp_size * cols), low),
        pltpu.VMEM(((tp_size - 1) * ctx_size * rows, cols), low),
        pltpu.VMEM((line * rows, cols), low),
        pltpu.VMEM((2 * line * rows, cols), low),
        dma(((tp_size - 1) * ctx_size * CHUNKS,)),
        dma((line * CHUNKS,)),
        dma((line * CHUNKS,)),
        dma(((tp_size - 1) * ctx_size * CHUNKS,)),
        dma((line * CHUNKS,)),
        dma((2 * line * CHUNKS,)),
    ]


def scatter_steps(pack, scratch, everyone, begin, before, compute, finish):
    (full, sib_buf, pair_buf, line_buf, tp_send, pair_send, line_send, tp_recv, pair_recv, line_recv) = scratch
    line, t, a, b = pack.line, pack.t, pack.a, pack.b
    ctx_size = 2 * line
    wide, low = jnp.float32, jnp.bfloat16
    table = [
        sorted(range(line), key=lambda o, node=node: (-abs(o - node), o)) for node in range(line)
    ]

    def owner(i):
        result = jnp.int32(0)
        for node in range(line):
            for place in range(line):
                here = jnp.logical_and(a == node, i == place)
                result = jnp.where(here, table[node][place], result)
        return result

    def tp_copy(block, k, shift):
        return remote(
            pack.region(full, block, k, t ^ shift),
            sib_buf.at[
                pl.ds(pack.row0((shift - 1) * ctx_size + block, k), pack.chunk), :
            ],
            tp_send.at[((shift - 1) * ctx_size + block) * CHUNKS + k],
            tp_recv.at[((shift - 1) * ctx_size + block) * CHUNKS + k],
            pack.sibling(shift),
        )

    def pair_copy(node, k):
        return remote(
            pack.region(full, node * 2 + (1 - b), k, t),
            pair_buf.at[pl.ds(pack.row0(node, k), pack.chunk), :],
            pair_send.at[node * CHUNKS + k],
            pair_recv.at[node * CHUNKS + k],
            pack.pair(),
        )

    def line_copy(node, k, down):
        return remote(
            pack.region(full, node * 2 + b, k, t),
            line_buf.at[pl.ds(pack.row0(down * line + node, k), pack.chunk), :],
            line_send.at[node * CHUNKS + k],
            line_recv.at[(down * line + node) * CHUNKS + k],
            pack.down() if down else pack.up(),
        )

    def own_part(block, k):
        return full[
            pl.ds(pack.row0(block, k), pack.chunk),
            pl.ds(pl.multiple_of(t * pack.cols, pack.cols), pack.cols),
        ].astype(wide)

    def put_part(block, k, value):
        full[
            pl.ds(pack.row0(block, k), pack.chunk),
            pl.ds(pl.multiple_of(t * pack.cols, pack.cols), pack.cols),
        ] = value.astype(low)

    def landed(ref, block, k):
        return ref[pl.ds(pack.row0(block, k), pack.chunk), :].astype(wide)

    def fill(block, k, order):
        row0 = pack.row0(block, k)
        full[pl.ds(row0, pack.chunk), :] = compute(row0, block * CHUNKS + k, order)
        for shift in range(1, pack.tp_size):
            tp_copy(block, k, shift).start()

    def join(block, k):
        total = own_part(block, k)
        for shift in range(1, pack.tp_size):
            tp_copy(block, k, shift).wait_recv()
            total = total + landed(sib_buf, (shift - 1) * ctx_size + block, k)
        put_part(block, k, total)

    pack.meet(everyone)
    begin()
    before()

    def step(s):
        @pl.when(s < pack.steps)
        def _():
            node, k = owner(s // CHUNKS), s % CHUNKS

            def side(i):
                fill(node * 2 + jnp.where(i == 0, 1 - b, b), k, 2 * s + i)

            loop(2, side)

        late = s - 1

        @pl.when(jnp.logical_and(late >= 0, late < pack.steps))
        def _():
            node, k = owner(late // CHUNKS), late % CHUNKS

            def side(i):
                join(node * 2 + jnp.where(i == 0, 1 - b, b), k)

                @pl.when(i == 0)
                def _():
                    pair_copy(node, k).start()

            loop(2, side)

        later = s - 2

        @pl.when(later >= 0)
        def _():
            node, k = owner(later // CHUNKS), later % CHUNKS
            pair_copy(node, k).wait_recv()
            put_part(
                node * 2 + b, k, own_part(node * 2 + b, k) + landed(pair_buf, node, k)
            )
            from_below = jnp.logical_and(pack.has_down, node >= a)
            from_above = jnp.logical_and(pack.has_up, node <= a)
            for down, there in ((0, from_below), (1, from_above)):

                @pl.when(there)
                def _():
                    line_copy(node, k, down).wait_recv()
                    put_part(
                        node * 2 + b,
                        k,
                        own_part(node * 2 + b, k) + landed(line_buf, down * line + node, k),
                    )

            @pl.when(node > a)
            def _():
                line_copy(node, k, 0).start()

            @pl.when(node < a)
            def _():
                line_copy(node, k, 1).start()

            @pl.when(node == a)
            def _():
                finish(k, own_part(node * 2 + b, k))

    loop(pack.steps + 2, step)

    def drain(s):
        node, k = s // CHUNKS, s % CHUNKS
        pair_copy(node, k).wait_send()
        for shift in range(1, pack.tp_size):
            tp_copy(node * 2, k, shift).wait_send()
            tp_copy(node * 2 + 1, k, shift).wait_send()

        @pl.when(node > a)
        def _():
            line_copy(node, k, 0).wait_send()

        @pl.when(node < a)
        def _():
            line_copy(node, k, 1).wait_send()

    loop(pack.steps, drain)


ANY = pl.BlockSpec(memory_space=pl.ANY)


def nn_dot(left, right):
    return lax.dot_general(
        left, right, (((1,), (0,)), ((), ())), preferred_element_type=jnp.float32
    )


def nt_dot(left, right):
    return lax.dot_general(
        left, right, (((1,), (1,)), ((), ())), preferred_element_type=jnp.float32
    )


def tn_dot(left, right):
    return lax.dot_general(
        left, right, (((0,), (0,)), ((), ())), preferred_element_type=jnp.float32
    )


class Out:
    def __init__(self, width, dtype, flip=False, late=False):
        self.width, self.dtype, self.flip, self.late = width, dtype, flip, late

    def shape(self, rows):
        return (self.width, rows) if self.flip else (rows, self.width)

    def window(self, ref, window):
        return ref.at[:, window] if self.flip else ref.at[window, :]


class Parts:
    def __init__(self, shape, pieces):
        self.shape, self.pieces = shape, pieces


class Swap:
    def __init__(self, axis, shape, pieces, keep):
        self.axis, self.shape, self.pieces, self.keep = axis, shape, pieces, keep


class Ship:
    def __init__(self, axis, array, source, shape):
        self.axis, self.array, self.source, self.shape = axis, array, source, shape


class Make:
    def __init__(self, width, features, tile, send):
        self.width, self.features, self.tile, self.send = width, features, tile, send


class Deal:
    def __init__(self, own, far):
        self.own, self.far = own, far


class Tiles:
    def __init__(self, width, features, tile):
        self.width, self.features, self.tile = width, features, tile


def whole(ref):
    return ref


def pack_call(
    sizes,
    shape,
    piece,
    collective_id,
    flops,
    gathered=None,
    resident=(),
    outs=(),
    totals=(),
    last=None,
    keep=False,
    swaps=(),
    ships=(),
    tiles=None,
    makes=(),
    deals=(),
    lag=1,
):
    packs, ctx_size, tp_size = sizes
    rows, cols = shape
    all_rows, all_cols = ctx_size * rows, tp_size * cols
    pieces = ctx_size * CHUNKS
    dma = pltpu.SemaphoreType.DMA
    gather = gathered is not None
    if gather:
        base = gather_scratch(ctx_size, tp_size, rows, cols, gathered.dtype)
    else:
        base = scatter_scratch(ctx_size, tp_size, rows, cols)
    axis_size = {"fsdp": packs, "ctx": ctx_size, "tp": tp_size}
    inputs = []

    def enlist(array):
        for i, known in enumerate(inputs):
            if known is array:
                return i
        inputs.append(array)
        return len(inputs) - 1

    if gather:
        enlist(gathered)
    resident = list(resident)
    first_deal = len(resident)
    for deal in deals:
        resident += [deal.own, deal.far]
    parts = [
        r if isinstance(r, Parts) else Parts(r.shape, [(r, whole, whole)]) for r in resident
    ]
    part_list = [[(enlist(x), src, dst) for x, src, dst in p.pieces] for p in parts]
    swap_list = [[(enlist(x), src, dst) for x, src, dst in w.pieces] for w in swaps]
    ship_list = [enlist(ship.array) for ship in ships]
    swap_count = sum(len(w.pieces) * axis_size[w.axis] for w in swaps)
    ship_count = sum(axis_size[ship.axis] for ship in ships)
    kept_swaps = [i for i, w in enumerate(swaps) if w.keep]
    n_out = len(outs) + len(totals) + keep + len(kept_swaps) + len(ships)
    tile_rows = 128
    features = all_cols
    own_features = features // (packs * ctx_size)
    splits = tile_rows // own_features
    own_tiles = features // packs // tile_rows
    far_tiles = (packs - 1) * own_tiles
    assert own_tiles + far_tiles == pieces
    stride = pieces // own_tiles

    def kernel(*refs):
        refs = list(refs)

        def take(count):
            taken = refs[:count]
            del refs[:count]
            return taken

        given = take(len(inputs))
        sum_ref = None if gather else take(1)[0]
        out_refs = take(n_out)
        blocks_ref = None if tiles is None else take(1)[0]
        make_outs = [take(2) for _ in makes]
        deal_outs = take(len(deals))
        scratch = take(len(base))
        held = take(len(resident))
        stage = take(len(outs))
        total_refs = take(len(totals))
        swap_bufs = take(len(swaps))
        (held_sem, out_sem, late_sem, swap_local, swap_send, swap_recv, ship_send, ship_recv) = take(8)
        if tiles is not None:
            tile_stage, tile_far, tile_send, far_recv, block_recv = take(5)
        make_stages = take(len(makes))
        make_send, make_recv, deal_send, deal_recv = take(4)
        over_packs = swaps or ships or tiles is not None or any(make.send for make in makes)
        everyone = tiles is not None or deals or any(ship.axis == "ctx" for ship in ships)
        pack = Pack(ctx_size, tp_size, rows, cols, packs if over_packs else 1)
        mine = {axis: lax.axis_index(axis) for axis in axis_size}
        loads = []
        for target_ref, copies in zip(held, part_list):
            for which, source, target in copies:
                loads.append(
                    pltpu.make_async_copy(
                        source(given[which]), target(target_ref), held_sem.at[len(loads)]
                    )
                )
        swap_copies, swap_sends = [], []
        index = 0
        for swap, buf, copies in zip(swaps, swap_bufs, swap_list):
            for which, source, target in copies:
                here = source(given[which])
                there = target(buf, mine[swap.axis])
                swap_copies.append(pltpu.make_async_copy(here, there, swap_local.at[index]))
                for shift in range(1, axis_size[swap.axis]):
                    slot = index + shift
                    device = {swap.axis: mine[swap.axis] ^ shift}
                    theirs = target(buf, mine[swap.axis] ^ shift)
                    swap_sends.append(
                        (
                            remote(here, there, swap_send.at[slot], swap_recv.at[slot], device),
                            remote(theirs, theirs, swap_send.at[slot], swap_recv.at[slot], device),
                        )
                    )
                index += axis_size[swap.axis]
        late = []
        for i, where in enumerate(kept_swaps):
            late.append((swap_bufs[where], out_refs[len(outs) + len(totals) + keep + i]))
        late_copies = [
            pltpu.make_async_copy(here, there, late_sem.at[i])
            for i, (here, there) in enumerate(late)
        ]
        ship_local, ship_copies = [], []
        index = 0
        for ship, which, landing in zip(ships, ship_list, out_refs[n_out - len(ships) :]):
            place = mine[ship.axis]
            if ship.axis == "ctx":
                here = ship.source(given[which], 0)
                ship_local.append(
                    pltpu.make_async_copy(here, landing.at[place], ship_send.at[index])
                )
            for shift in range(1, axis_size[ship.axis]):
                here = ship.source(given[which], shift)
                there = landing.at[place] if ship.axis == "ctx" else landing.at[shift - 1]
                theirs = landing.at[place ^ shift] if ship.axis == "ctx" else there
                device = {ship.axis: place ^ shift}
                sems = ship_send.at[index + shift], ship_recv.at[index + shift]
                ship_copies.append(
                    (remote(here, there, *sems, device), remote(theirs, theirs, *sems, device))
                )
            index += axis_size[ship.axis]

        def begin():
            for copy in swap_copies + ship_local:
                copy.start()
            for send, _ in swap_sends + ship_copies:
                send.start()

        def before():
            for ref in total_refs:
                ref[...] = jnp.zeros_like(ref)
            for load in loads:
                load.wait()
            for copy in swap_copies:
                copy.wait()
            for send, receive in swap_sends:
                receive.wait_recv()
            for copy in late_copies:
                copy.start()

        def stores(row0, index):
            window = pl.ds(row0, pack.chunk)
            copies = []
            for i, out in enumerate(outs):
                if not out.late:
                    copies.append((out.window(stage[i], window), out.window(out_refs[i], window), i))
            if keep:
                i = len(outs)
                copies.append(
                    (scratch[0].at[window, :], out_refs[i + len(totals)].at[window, :], i)
                )
            return [
                pltpu.make_async_copy(here, there, out_sem.at[i * pieces + index])
                for here, there, i in copies
            ]

        def put(window, values):
            early = [i for i, out in enumerate(outs) if not out.late]
            for i, value in zip(early, values):
                out = outs[i]
                if out.flip:
                    stage[i][:, window] = value.astype(out.dtype)
                else:
                    stage[i][window, :] = value.astype(out.dtype)

        ahead = 3

        def is_far(order):
            if far_tiles != own_tiles:
                return order < far_tiles
            middle = jnp.logical_and(order >= ahead, order < pieces - ahead)
            return jnp.where(middle, (order - ahead) % 2 == 1, order < ahead)

        def rank(order):
            if far_tiles != own_tiles:
                return jnp.where(order < far_tiles, order, order - far_tiles)
            middle = (order - ahead) // 2
            return jnp.where(
                order < ahead,
                order,
                jnp.where(
                    order >= pieces - ahead,
                    order - far_tiles,
                    jnp.where(is_far(order), ahead + middle, middle),
                ),
            )

        def tile_copy(order, which, shift):
            return remote(
                tile_stage.at[order],
                tile_far.at[which],
                tile_send.at[order * splits],
                far_recv.at[which],
                {"fsdp": mine["fsdp"] ^ shift},
            )

        def block_copy(order, split, owner):
            return remote(
                tile_stage.at[order, pl.ds(split * own_features, own_features), :],
                blocks_ref.at[mine["ctx"]],
                tile_send.at[order * splits + split],
                block_recv.at[mine["ctx"]],
                {"ctx": owner},
            )

        def block_store(order, split):
            return pltpu.make_async_copy(
                tile_stage.at[order, pl.ds(split * own_features, own_features), :],
                blocks_ref.at[mine["ctx"]],
                tile_send.at[order * splits + split],
            )

        def each_block(order, go_away, stay):
            for split in range(splits):
                owner = ((mine["ctx"] // splits) ^ rank(order)) * splits + split

                @pl.when(owner != mine["ctx"])
                def _():
                    go_away(order, split, owner)

                @pl.when(owner == mine["ctx"])
                def _():
                    stay(order, split)

        def make_tile(order):
            if tiles is None:
                return
            far, which = is_far(order), rank(order)
            shift = jnp.where(far, which // own_tiles + 1, 0)
            place = (mine["ctx"] // splits) ^ (which % own_tiles)
            first = ((mine["fsdp"] ^ shift) * own_tiles + place) * tile_rows
            value = tiles.tile(pl.ds(pl.multiple_of(first, tile_rows), tile_rows), held)

            @pl.when(far)
            def _():
                tile_stage[order] = value.astype(jnp.bfloat16)
                tile_copy(order, which, shift).start()

            @pl.when(jnp.logical_not(far))
            def _():
                total = value
                for other in range(packs - 1):
                    slot = other * own_tiles + which
                    tile_copy(order, slot, 1).wait_recv()
                    total = total + tile_far[slot].astype(jnp.float32)
                tile_stage[order] = total.astype(jnp.bfloat16)
                each_block(
                    order,
                    lambda *where: block_copy(*where).start(),
                    lambda *where: block_store(*where).start(),
                )

        def finish_tiles():
            if tiles is None:
                return

            def sent(order):
                @pl.when(is_far(order))
                def _():
                    tile_copy(order, 0, 1).wait_send()

                @pl.when(jnp.logical_not(is_far(order)))
                def _():
                    each_block(
                        order,
                        lambda *where: block_copy(*where).wait_send(),
                        lambda *where: block_store(*where).wait(),
                    )

            loop(pieces, sent)
            for shift in range(1, ctx_size):
                landed = blocks_ref.at[mine["ctx"] ^ shift]
                remote(
                    landed,
                    landed,
                    tile_send.at[0],
                    block_recv.at[mine["ctx"] ^ shift],
                    {"ctx": mine["ctx"] ^ shift},
                ).wait_recv()

        def make_copies(i, order):
            far = order < far_tiles
            which = jnp.where(far, order, order - far_tiles)
            shift = jnp.where(far, which // own_tiles + 1, 0)
            window = pl.ds(
                pl.multiple_of(which % own_tiles * tile_rows, tile_rows), tile_rows
            )
            here = make_stages[i].at[order]
            sem = make_send.at[i * pieces + order]
            own_out, far_out = make_outs[i]
            slot = jnp.maximum(shift - 1, 0)
            send = remote(
                here,
                far_out.at[slot, window, :],
                sem,
                make_recv.at[i * pieces + order],
                {"fsdp": mine["fsdp"] ^ shift},
            )
            away = pltpu.make_async_copy(here, far_out.at[slot, window, :], sem)
            stay = pltpu.make_async_copy(here, own_out.at[window, :], sem)
            return far, shift, which % own_tiles, send, away, stay

        def make_parts(order):
            for i, make in enumerate(makes):
                far, shift, place, send, away, stay = make_copies(i, order)
                first = ((mine["fsdp"] ^ shift) * own_tiles + place) * tile_rows
                value = make.tile(pl.ds(pl.multiple_of(first, tile_rows), tile_rows), held)
                make_stages[i][order] = value.astype(jnp.bfloat16)

                @pl.when(far)
                def _():
                    (send if make.send else away).start()

                @pl.when(jnp.logical_not(far))
                def _():
                    stay.start()

        def finish_parts():
            def sent(order):
                for i, make in enumerate(makes):
                    far, _, _, send, away, stay = make_copies(i, order)

                    @pl.when(far)
                    def _():
                        if make.send:
                            send.wait_send()
                            send.wait_recv()
                        else:
                            away.wait()

                    @pl.when(jnp.logical_not(far))
                    def _():
                        stay.wait()

            loop(pieces, sent)

        def deal_blocks(i, turn, go_away, stay):
            own_buf, landing = held[first_deal + 2 * i], deal_outs[i]
            for split in range(splits):
                owner = ((mine["ctx"] // splits) ^ turn) * splits + split
                here = own_buf.at[
                    pl.ds(pl.multiple_of(owner * own_features, own_features), own_features), :
                ]
                there = landing.at[mine["ctx"]]
                sem = deal_send.at[(i * own_tiles + turn) * splits + split]

                @pl.when(owner != mine["ctx"])
                def _():
                    go_away(
                        remote(
                            here,
                            there,
                            sem,
                            deal_recv.at[i * ctx_size + mine["ctx"]],
                            {"ctx": owner},
                        )
                    )

                @pl.when(owner == mine["ctx"])
                def _():
                    stay(pltpu.make_async_copy(here, there, sem))

        def deal_out(order):
            if not deals:
                return

            @pl.when(order % stride == 0)
            def _():
                turn = order // stride
                place = (mine["ctx"] // splits) ^ turn
                window = pl.ds(pl.multiple_of(place * tile_rows, tile_rows), tile_rows)
                for i in range(len(deals)):
                    own_buf, far_buf = held[first_deal + 2 * i], held[first_deal + 2 * i + 1]
                    total = own_buf[window, :].astype(jnp.float32)
                    for other in range(packs - 1):
                        total = total + far_buf[other, window, :].astype(jnp.float32)
                    own_buf[window, :] = total.astype(jnp.bfloat16)
                    deal_blocks(i, turn, lambda copy: copy.start(), lambda copy: copy.start())

        def finish_deals():
            if not deals:
                return

            def sent(turn):
                for i in range(len(deals)):
                    deal_blocks(i, turn, lambda copy: copy.wait_send(), lambda copy: copy.wait())

            loop(own_tiles, sent)
            for i in range(len(deals)):
                for shift in range(1, ctx_size):
                    place = mine["ctx"] ^ shift
                    landed = deal_outs[i].at[place]
                    sem = deal_recv.at[i * ctx_size + place]
                    remote(landed, landed, deal_send.at[0], sem, {"ctx": place}).wait_recv()

        for load in loads:
            load.start()
        if gather:

            def compute(row0, index, order):
                window = pl.ds(row0, pack.chunk)
                put(window, piece(scratch[0][window, :], window, held + swap_bufs, total_refs))
                for store in stores(row0, index):
                    store.start()
                deal_out(order)
                make_tile(order)
                make_parts(order)

            gather_steps(pack, given[0], scratch, everyone, lag, begin, before, compute)
        else:

            def compute(row0, index, order):
                window = pl.ds(row0, pack.chunk)
                deal_out(order)
                make_tile(order)
                make_parts(order)
                rows_value, values = piece(window, held + swap_bufs, total_refs)
                put(window, values)
                for store in stores(row0, index):
                    store.start()
                return rows_value.astype(jnp.bfloat16)

            def finish(k, total):
                sum_ref[pl.ds(pl.multiple_of(k * pack.chunk, pack.chunk), pack.chunk), :] = total

            scatter_steps(pack, scratch, everyone, begin, before, compute, finish)
        if last is not None:
            last(held + swap_bufs, stage, total_refs, pack.chunk)
        ends = []
        for i, out in enumerate(outs):
            if out.late:
                ends.append((stage[i], out_refs[i]))
        for i, ref in enumerate(total_refs):
            ends.append((ref, out_refs[len(outs) + i]))
        end_copies = [
            pltpu.make_async_copy(here, there, late_sem.at[len(late) + i])
            for i, (here, there) in enumerate(ends)
        ]
        for copy in end_copies:
            copy.start()

        def drain(index):
            for store in stores(pl.multiple_of(index * pack.chunk, pack.chunk), index):
                store.wait()

        loop(pieces, drain)
        finish_tiles()
        finish_parts()
        finish_deals()
        for copy in late_copies + end_copies + ship_local:
            copy.wait()
        for send, _ in swap_sends:
            send.wait_send()
        for send, receive in ship_copies:
            send.wait_send()
            receive.wait_recv()

    low = jnp.bfloat16
    shapes = [jax.ShapeDtypeStruct(out.shape(all_rows), out.dtype) for out in outs]
    shapes += [jax.ShapeDtypeStruct(dims, dtype) for dims, dtype in totals]
    if keep:
        shapes.append(jax.ShapeDtypeStruct((all_rows, all_cols), gathered.dtype))
    shapes += [jax.ShapeDtypeStruct(swaps[i].shape, low) for i in kept_swaps]
    for ship in ships:
        slots = ctx_size if ship.axis == "ctx" else packs - 1
        shapes.append(jax.ShapeDtypeStruct((slots,) + ship.shape, ship.array.dtype))
    if tiles is not None:
        shapes.append(jax.ShapeDtypeStruct((ctx_size, own_features, tiles.width), low))
    part_features = features // packs
    for make in makes:
        shapes.append(jax.ShapeDtypeStruct((part_features, make.width), low))
        shapes.append(jax.ShapeDtypeStruct((packs - 1, part_features, make.width), low))
    for deal in deals:
        shapes.append(jax.ShapeDtypeStruct((ctx_size, own_features, deal.own.shape[1]), low))
    out_specs = [ANY] * len(shapes)
    if not gather:
        shapes = [jax.ShapeDtypeStruct(shape, jnp.float32)] + shapes
        out_specs = [pl.BlockSpec(memory_space=pltpu.VMEM)] + out_specs
    tile_scratch = []
    if tiles is not None:
        tile_scratch = [
            pltpu.VMEM((pieces, tile_rows, tiles.width), low),
            pltpu.VMEM((far_tiles, tile_rows, tiles.width), low),
            dma((pieces * splits,)),
            dma((far_tiles,)),
            dma((ctx_size,)),
        ]
    return pl.pallas_call(
        kernel,
        out_shape=tuple(shapes),
        in_specs=[ANY] * len(inputs),
        out_specs=tuple(out_specs),
        scratch_shapes=base
        + [pltpu.VMEM(p.shape, p.pieces[0][0].dtype) for p in parts]
        + [pltpu.VMEM(out.shape(all_rows), out.dtype) for out in outs]
        + [pltpu.VMEM(dims, dtype) for dims, dtype in totals]
        + [pltpu.VMEM(swap.shape, low) for swap in swaps]
        + [
            dma((max(1, sum(len(p.pieces) for p in parts)),)),
            dma(((len(outs) + 1) * pieces,)),
            dma((len(kept_swaps) + len(outs) + len(totals) + 1,)),
            dma((max(1, swap_count),)),
            dma((max(1, swap_count),)),
            dma((max(1, swap_count),)),
            dma((max(1, ship_count),)),
            dma((max(1, ship_count),)),
        ]
        + tile_scratch
        + [pltpu.VMEM((pieces, tile_rows, make.width), low) for make in makes]
        + [
            dma((max(1, len(makes)) * pieces,)),
            dma((max(1, len(makes)) * pieces,)),
            dma((max(1, len(deals)) * own_tiles * splits,)),
            dma((max(1, len(deals)) * ctx_size,)),
        ],
        compiler_params=pltpu.CompilerParams(
            collective_id=collective_id, has_side_effects=True, vmem_limit_bytes=VMEM_LIMIT
        ),
        cost_estimate=pl.CostEstimate(
            flops=flops, bytes_accessed=8 * all_rows * all_cols, transcendentals=0
        ),
    )(*inputs)


def small_sums(sizes, tensor, collective_id):
    packs, ctx_size, tp_size = sizes
    dma = pltpu.SemaphoreType.DMA
    count = tensor.shape[0]

    def kernel(src, out_ref, ctx_buf, mid, rest_buf, send_sems, recv_sems):
        f, c, t = (lax.axis_index(axis) for axis in ("fsdp", "ctx", "tp"))
        ctx_peers = [(shift, {"ctx": c ^ shift}) for shift in range(1, ctx_size)]
        rest_peers = [
            (shift * tp_size + turn, {"fsdp": f ^ shift, "tp": t ^ turn})
            for shift in range(packs)
            for turn in range(tp_size)
            if shift or turn
        ]
        barrier = pltpu.get_barrier_semaphore()
        for _, device in ctx_peers + rest_peers:
            pl.semaphore_signal(barrier, inc=1, device_id=device, device_id_type=MESH_ID)
        pl.semaphore_wait(barrier, len(ctx_peers) + len(rest_peers))

        def exchange(source, buf, peers, offset):
            copies = [
                remote(
                    source,
                    buf.at[slot],
                    send_sems.at[offset + slot],
                    recv_sems.at[offset + slot],
                    device,
                )
                for slot, device in peers
            ]
            for copy in copies:
                copy.start()
            for copy in copies:
                copy.wait()

        exchange(src, ctx_buf, ctx_peers, 0)
        total = src[...]
        for slot, _ in ctx_peers:
            total = total + ctx_buf[slot]
        mid[...] = total
        exchange(mid, rest_buf, rest_peers, ctx_size)
        rest_buf[0] = total
        for turn in range(tp_size):
            part = rest_buf[turn]
            for shift in range(1, packs):
                part = part + rest_buf[shift * tp_size + turn]
            out_ref[t ^ turn] = part

    return pl.pallas_call(
        kernel,
        out_shape=jax.ShapeDtypeStruct((tp_size, count, tensor.shape[1]), jnp.float32),
        in_specs=[pl.BlockSpec(memory_space=pltpu.VMEM)],
        out_specs=pl.BlockSpec(memory_space=pltpu.VMEM),
        scratch_shapes=[
            pltpu.VMEM((ctx_size,) + tensor.shape, jnp.float32),
            pltpu.VMEM(tensor.shape, jnp.float32),
            pltpu.VMEM((packs * tp_size,) + tensor.shape, jnp.float32),
            dma((ctx_size + packs * tp_size,)),
            dma((ctx_size + packs * tp_size,)),
        ],
        compiler_params=pltpu.CompilerParams(collective_id=collective_id, has_side_effects=True),
    )(tensor)

def on_device(
    hidden_in,
    cotangent,
    positions,
    seq_lengths,
    expert_ids,
    attn_norm,
    ffn_norm,
    query_norm,
    key_norm,
    w_query,
    w_key,
    w_value,
    w_out,
    w_router,
    w_gate,
    w_up,
    w_down,
):
    tok_rows, col_count = hidden_in.shape
    packs, ctx_size, tp_size = (lax.axis_size(axis) for axis in ("fsdp", "ctx", "tp"))
    sizes = (packs, ctx_size, tp_size)
    own_shape = (tok_rows, col_count)
    ctx_place = lax.axis_index("ctx")
    width_all = col_count * tp_size
    part_width = width_all // packs
    pack_rows = tok_rows * ctx_size
    head_dim = query_norm.shape[0]
    local_heads = w_query.shape[1] // head_dim
    expert_count, hidden_units = w_gate.shape[0], w_gate.shape[2]
    own_experts = expert_count // ctx_size
    own_units = own_experts * hidden_units
    top_count = expert_ids.shape[1]
    sharers = ctx_size // local_heads
    score_scale = head_dim ** (-0.5)
    wide = jnp.float32
    slim = jnp.bfloat16
    lanes = 128

    def row_total(tensor):
        return lax.psum(tensor, "tp")

    def units_of(ref, window, slot):
        return ref[window, pl.ds(slot * hidden_units, hidden_units)]

    def own_queries(window, value):
        if sharers == 1:
            return value
        share = window.start // (pack_rows // sharers)
        return jnp.where(share == lax.axis_index("ctx") // local_heads, value, 0.0)

    def head_window():
        return pl.ds(
            pl.multiple_of(lax.axis_index("ctx") % local_heads * head_dim, head_dim), head_dim
        )

    def part_of(place, size):
        return pl.ds(pl.multiple_of(place * size, size), size)

    half_rows = part_width // 2

    def half_ship(weight, slot, half):
        return Ship(
            "fsdp",
            weight,
            lambda ref, shift: ref.at[
                lax.axis_index("ctx") * own_experts + slot,
                pl.ds(half * half_rows, half_rows),
                :,
            ],
            (half_rows, hidden_units),
        )

    halves = [(slot, half) for slot in range(own_experts) for half in range(2)]
    expert_ships = [half_ship(w, *which) for w in (w_gate, w_up, w_down) for which in halves]
    first_ships = len(expert_ships) // 6
    second_ships = first_ships + (len(expert_ships) - first_ships) // 2

    def expert_weight(weight, far):
        pieces = [
            (
                weight,
                lambda ref: ref.at[pl.ds(lax.axis_index("ctx") * own_experts, own_experts), :, :],
                lambda buf: buf.at[:, part_of(lax.axis_index("fsdp"), part_width), :],
            )
        ]
        for (slot, half), array in zip(halves, far):
            for shift in range(1, packs):
                pieces.append(
                    (
                        array,
                        lambda ref, shift=shift: ref.at[shift - 1],
                        lambda buf, slot=slot, half=half, shift=shift: buf.at[
                            slot,
                            part_of((lax.axis_index("fsdp") ^ shift) * 2 + half, half_rows),
                            :,
                        ],
                    )
                )
        return Parts((own_experts, width_all, hidden_units), pieces)

    segment, place = locate(positions[0], seq_lengths[0])
    cosine, sine = rope_tables(place, head_dim)
    segment_rows = jnp.broadcast_to(segment[:, None], (pack_rows, lanes))
    segment_cols = jnp.broadcast_to(segment[None, :], (8, pack_rows))

    def project(rows, window, held, totals):
        cos_table, sin_table, gain_q, gain_k, weight, _, gain, _ = held
        hidden = rows.astype(wide)
        inverse = lax.rsqrt(jnp.mean(hidden * hidden, axis=1, keepdims=True) + norm_eps)
        normed = (hidden * inverse * gain[...].astype(wide)).astype(slim)
        raw = nn_dot(normed, weight[...])
        cos_rows, sin_rows = cos_table[window, :], sin_table[window, :]

        def prepare(raw_proj, gain_vec):
            inv = lax.rsqrt(jnp.mean(raw_proj * raw_proj, axis=1, keepdims=True) + norm_eps)
            scaled = raw_proj * inv * gain_vec[...]
            return scaled * cos_rows + pltpu.roll(scaled, head_dim // 2, 1) * sin_rows

        query_raw = raw[:, :head_dim]
        key_raw = raw[:, head_dim : 2 * head_dim]
        key_turned = prepare(key_raw, gain_k)
        return (
            normed,
            jnp.broadcast_to(inverse, (rows.shape[0], lanes)),
            query_raw,
            key_raw,
            prepare(query_raw, gain_q),
            key_turned,
            key_turned.T,
            raw[:, 2 * head_dim :],
        )

    gain_query = query_norm.astype(wide)[None, :]
    gain_key = key_norm.astype(wide)[None, :]
    (
        normed_first,
        inv_all,
        query_raw,
        key_raw,
        query_low,
        key_low,
        key_flip,
        value_low,
        qkv_weight,
        out_weight,
        router_full,
        *first_halves,
        ids_all,
    ) = pack_call(
        sizes,
        own_shape,
        project,
        1,
        6 * pack_rows * width_all * head_dim,
        gathered=hidden_in,
        resident=(cosine, sine, gain_query, gain_key),
        outs=(
            Out(width_all, slim),
            Out(lanes, wide),
            Out(head_dim, wide),
            Out(head_dim, wide),
            Out(head_dim, slim),
            Out(head_dim, slim),
            Out(head_dim, slim, flip=True),
            Out(head_dim, slim),
        ),
        swaps=(
            Swap(
                "fsdp",
                (width_all, 3 * head_dim),
                [
                    (
                        w,
                        lambda ref: ref.at[:, head_window()],
                        lambda buf, place, i=i: buf.at[
                            part_of(place, part_width), pl.ds(i * head_dim, head_dim)
                        ],
                    )
                    for i, w in enumerate((w_query, w_key, w_value))
                ],
                True,
            ),
            Swap(
                "fsdp",
                (head_dim, width_all),
                [
                    (
                        w_out,
                        lambda ref: ref.at[head_window(), :],
                        lambda buf, place: buf.at[:, part_of(place, part_width)],
                    )
                ],
                True,
            ),
            Swap(
                "tp",
                (1, width_all),
                [
                    (
                        attn_norm[None, :],
                        whole,
                        lambda buf, place: buf.at[:, part_of(place, col_count)],
                    )
                ],
                False,
            ),
            Swap(
                "fsdp",
                (expert_count, width_all),
                [(w_router, whole, lambda buf, place: buf.at[:, part_of(place, part_width)])],
                True,
            ),
        ),
        ships=expert_ships[:first_ships]
        + [Ship("ctx", expert_ids.T, lambda ref, shift: ref, (top_count, tok_rows))],
        lag=3,
    )
    router_pad = jnp.pad(router_full, ((0, lanes - expert_count), (0, 0)))

    def attend(rows, window, held, totals):
        query, key, value, seg_rows, seg_cols = held
        scores = nt_dot(query[window, :], key[...]) * score_scale
        same_seq = seg_rows[window, :][:, :1] == seg_cols[0:1, :]
        scores = jnp.where(same_seq, scores, -1e30)
        row_peak = jnp.max(scores, axis=1, keepdims=True)
        row_exp = jnp.exp(scores - row_peak)
        row_sum = jnp.sum(row_exp, axis=1, keepdims=True)
        probs_low = (row_exp * (1.0 / row_sum)).astype(slim)
        log_total = jnp.broadcast_to(row_peak + jnp.log(row_sum), (scores.shape[0], lanes))
        return own_queries(window, nn_dot(probs_low, value[...])), log_total.T[:8, :]

    attended_low, log_total, cotangent_all, *second_halves = pack_call(
        sizes,
        own_shape,
        attend,
        2,
        4 * pack_rows * pack_rows * head_dim,
        gathered=cotangent,
        resident=(query_low, key_low, value_low, segment_rows, segment_cols),
        outs=(Out(head_dim, slim), Out(8, wide, flip=True)),
        keep=True,
        ships=expert_ships[first_ships:second_ships],
    )
    attn_branch, *third_halves = pack_call(
        sizes,
        own_shape,
        lambda window, held, totals: (nn_dot(held[0][window, :], held[1][...]), ()),
        3,
        2 * pack_rows * width_all * head_dim,
        resident=(attended_low, out_weight),
        ships=expert_ships[second_ships:],
    )
    far_halves = first_halves + second_halves + third_halves
    gate_weight, up_weight, down_weight = (
        expert_weight(w, far_halves[i * len(halves) : (i + 1) * len(halves)])
        for i, w in enumerate((w_gate, w_up, w_down))
    )

    resid_in = hidden_in.astype(wide)
    middle = resid_in + attn_branch
    gain_second = ffn_norm.astype(wide)
    inv_second = lax.rsqrt(row_total(jnp.sum(middle * middle, axis=1)) / width_all + norm_eps)[
        :, None
    ]

    def experts(rows, window, held, totals):
        gate_w, up_w, down_w, router_w, ids_ref, cotangent_ref = held
        lane = lax.broadcasted_iota(jnp.int32, (rows.shape[0], lanes), 1)
        logits = jnp.where(lane < expert_count, nt_dot(rows, router_w[...]), -1e30)
        logit_exp = jnp.exp(logits - jnp.max(logits, axis=1, keepdims=True))
        route_probs = logit_exp / jnp.sum(logit_exp, axis=1, keepdims=True)
        block = window.start // tok_rows
        within = pl.multiple_of(window.start - block * tok_rows, rows.shape[0])
        ids = ids_ref[block, :, pl.ds(within, rows.shape[0])].T
        chosen = jnp.zeros((rows.shape[0], lanes), wide)
        for pick in range(ids.shape[1]):
            chosen = chosen + (ids[:, pick : pick + 1] == lane).astype(wide)
        gate_weights = route_probs * chosen
        first_expert = lax.axis_index("ctx") * own_experts
        rows_grad = cotangent_ref[window, :]
        grad_logits = jnp.zeros((rows.shape[0], lanes), wide)
        mixed_list, gate_list, up_list = [], [], []
        for slot in range(own_experts):
            mine = (lane == first_expert + slot).astype(wide)
            gates = jnp.sum(gate_weights * mine, axis=1, keepdims=True)
            gate_proj = nn_dot(rows, gate_w[slot])
            up_proj = nn_dot(rows, up_w[slot])
            grad_mixed = nn_dot(rows_grad, down_w[slot]).astype(slim).astype(wide)
            gate_sigmoid = jax.nn.sigmoid(gate_proj)
            silu = gate_proj * gate_sigmoid
            activity = silu * up_proj
            mixed_list.append((gates * activity).astype(slim))
            grad_gates = jnp.sum(grad_mixed * activity, axis=1, keepdims=True)
            grad_activity = grad_mixed * gates
            gate_list.append(
                (
                    grad_activity * up_proj * (gate_sigmoid + silu * (1.0 - gate_sigmoid))
                ).astype(slim)
            )
            up_list.append((grad_activity * silu).astype(slim))
            grad_logits = grad_logits + gates * grad_gates * (mine - route_probs)
        return (
            jnp.concatenate(mixed_list, axis=1),
            jnp.concatenate(gate_list, axis=1),
            jnp.concatenate(up_list, axis=1),
            grad_logits,
        )

    mixed_low, grad_gate_low, grad_up_low, grad_logits_low, normed_second = pack_call(
        sizes,
        own_shape,
        experts,
        4,
        6 * pack_rows * width_all * own_units,
        gathered=(middle * inv_second * gain_second).astype(slim),
        resident=(gate_weight, up_weight, down_weight, router_pad, ids_all, cotangent_all),
        outs=(
            Out(own_units, slim),
            Out(own_units, slim),
            Out(own_units, slim),
            Out(lanes, slim),
        ),
        keep=True,
    )

    def back(window, held, totals):
        gate_grad, up_grad, logit_grad, gate_w, up_w, router_w, _ = held
        total = nn_dot(logit_grad[window, :], router_w[...])
        for slot in range(own_experts):
            total = total + nt_dot(units_of(gate_grad, window, slot), gate_w[slot])
            total = total + nt_dot(units_of(up_grad, window, slot), up_w[slot])
        return total, ()

    def gate_tile(window, held):
        features = held[6][:, window]
        return jnp.concatenate(
            [tn_dot(features, held[0][...]), tn_dot(features, held[2][...])], axis=1
        )

    grad_second, gate_own, gate_far = pack_call(
        sizes,
        own_shape,
        back,
        5,
        6 * pack_rows * width_all * own_units,
        resident=(
            grad_gate_low,
            grad_up_low,
            grad_logits_low,
            gate_weight,
            up_weight,
            router_pad,
            normed_second,
        ),
        makes=(Make(own_units + lanes, width_all, gate_tile, True),),
    )

    def by_expert(blocks):
        count, rows = blocks.shape[:2]
        return (
            jnp.swapaxes(blocks.reshape(count, rows, own_experts, hidden_units), 1, 2)
            .reshape(expert_count, rows, hidden_units)
            .astype(wide)
        )

    def by_head(blocks):
        rows = blocks.shape[1]
        summed = jnp.sum(
            blocks.reshape(sharers, local_heads, rows, head_dim).astype(wide), axis=0
        )
        return jnp.swapaxes(summed, 0, 1).reshape(rows, local_heads * head_dim)

    gain_two_grad = jnp.sum(grad_second * middle * inv_second, axis=0)
    second_scaled = grad_second * gain_second
    second_inner = row_total(jnp.sum(second_scaled * middle, axis=1))[:, None]
    grad_middle = (
        cotangent.astype(wide)
        + inv_second * second_scaled
        - middle * inv_second**3 * second_inner / width_all
    )

    (
        grad_attended,
        grad_middle_all,
        up_own,
        up_far,
        down_own,
        down_away,
        gate_blocks,
    ) = pack_call(
        sizes,
        own_shape,
        lambda rows, window, held, totals: (own_queries(window, nt_dot(rows, held[0][...])),),
        6,
        2 * pack_rows * width_all * (head_dim + own_units),
        gathered=grad_middle.astype(slim),
        resident=(out_weight, normed_second, grad_up_low, cotangent_all, mixed_low),
        outs=(Out(head_dim, slim),),
        keep=True,
        makes=(
            Make(
                own_units,
                width_all,
                lambda window, held: tn_dot(held[1][:, window], held[2][...]),
                True,
            ),
            Make(
                own_units,
                width_all,
                lambda window, held: tn_dot(held[3][:, window], held[4][...]),
                False,
            ),
        ),
        deals=(Deal(gate_own, gate_far),),
    )
    grad_gate = by_expert(gate_blocks[:, :, :own_units])
    grad_router = row_total(
        jnp.sum(gate_blocks[:, :, own_units : own_units + expert_count].astype(wide), axis=0).T
    )


    def attend_back(window, held, totals):
        mixed_ref, down_w, query, key, key_t, value, grad_att = held[:7]
        seg_rows, seg_cols, log_ref = held[7:10]
        grad_query_rot, grad_key_rot, grad_value, _ = totals
        query_chunk, grad_chunk = query[window, :], grad_att[window, :]
        scores = nt_dot(key[...], query_chunk) * score_scale
        same_seq = seg_rows[...] == seg_cols[0:1, window]
        probs = jnp.exp(jnp.where(same_seq, scores, -1e30) - log_ref[0:1, window])
        grad_probs = nt_dot(value[...], grad_chunk)
        inner = jnp.sum(probs * grad_probs, axis=0, keepdims=True)
        grad_scores = (probs * (grad_probs - inner)).astype(slim)
        grad_value[...] += nn_dot(probs.astype(slim), grad_chunk)
        grad_key_rot[...] += nn_dot(grad_scores, query_chunk)
        grad_query_rot[window, :] = nn_dot(key_t[...], grad_scores).T
        total = sum(
            nt_dot(units_of(mixed_ref, window, slot), down_w[slot]) for slot in range(own_experts)
        )
        return total, ()

    def unturn_all(held, stage, totals, chunk):
        raws, cos_table, sin_table, gains = held[10:12], held[12], held[13], held[14:16]
        grad_rots, grad_value, gain_sums = totals[:2], totals[2], totals[3]

        def unturn(i):
            window = pl.ds(pl.multiple_of(i * chunk, chunk), chunk)
            cos_rows, sin_rows = cos_table[window, :], sin_table[window, :]
            for which in range(2):
                grad_rot = grad_rots[which][window, :] * score_scale
                raw = raws[which][window, :]
                inverse = lax.rsqrt(jnp.mean(raw * raw, axis=1, keepdims=True) + norm_eps)
                grad_normed = grad_rot * cos_rows + pltpu.roll(
                    grad_rot * sin_rows, head_dim // 2, 1
                )
                weighted = grad_normed * gains[which][...]
                grad_raw = inverse * weighted - raw * inverse**3 * jnp.mean(
                    weighted * raw, axis=1, keepdims=True
                )
                stage[0][window, pl.ds(which * head_dim, head_dim)] = grad_raw.astype(slim)
                gain_sums[pl.ds(which, 1), :] += jnp.sum(
                    grad_normed * raw * inverse, axis=0, keepdims=True
                )
            stage[0][window, pl.ds(2 * head_dim, head_dim)] = grad_value[window, :].astype(slim)

        loop(pack_rows // chunk, unturn)

    expert_branch, grad_qkv_low, _, _, _, gain_sums, down_far, up_blocks = pack_call(
        sizes,
        own_shape,
        attend_back,
        7,
        2 * pack_rows * width_all * own_units + 10 * pack_rows * pack_rows * head_dim,
        resident=(
            mixed_low,
            down_weight,
            query_low,
            key_low,
            key_flip,
            value_low,
            grad_attended,
            segment_rows,
            segment_cols,
            log_total,
            query_raw,
            key_raw,
            cosine,
            sine,
            gain_query,
            gain_key,
        ),
        outs=(Out(3 * head_dim, slim, late=True),),
        totals=(
            ((pack_rows, head_dim), wide),
            ((pack_rows, head_dim), wide),
            ((pack_rows, head_dim), wide),
            ((8, head_dim), wide),
        ),
        last=unturn_all,
        ships=(
            Ship(
                "fsdp",
                down_away,
                lambda ref, shift: ref.at[shift - 1],
                (part_width, own_units),
            ),
        ),
        deals=(Deal(up_own, up_far),),
    )
    hidden_out = (middle + expert_branch).astype(slim)
    grad_up = by_expert(up_blocks)

    def last_tile(window, held):
        return jnp.concatenate(
            [
                tn_dot(held[2][:, window], held[0][...]),
                tn_dot(held[3][:, window], held[4][...]),
            ],
            axis=1,
        )

    grad_first, last_blocks, down_blocks = pack_call(
        sizes,
        own_shape,
        lambda window, held, totals: (nt_dot(held[0][window, :], held[1][...]), ()),
        8,
        2 * pack_rows * width_all * 7 * head_dim,
        resident=(grad_qkv_low, qkv_weight, normed_first, grad_middle_all, attended_low),
        tiles=Tiles(4 * head_dim, width_all, last_tile),
        deals=(Deal(down_own, down_far),),
    )
    grad_down = by_expert(down_blocks)
    grad_query, grad_key, grad_value, grad_out = (
        by_head(last_blocks[:, :, i * head_dim : (i + 1) * head_dim]) for i in range(4)
    )
    grad_out = grad_out.T

    gain_first = attn_norm.astype(wide)
    inv_first = lax.dynamic_slice_in_dim(inv_all, ctx_place * tok_rows, tok_rows, 0)[:, :1]
    gain_one_grad = jnp.sum(grad_first * resid_in * inv_first, axis=0)
    first_scaled = grad_first * gain_first
    first_inner = row_total(jnp.sum(first_scaled * resid_in, axis=1))[:, None]
    grad_hidden = (
        grad_middle + inv_first * first_scaled - resid_in * inv_first**3 * first_inner / width_all
    )

    stream_part = jnp.stack(
        [
            jnp.sum(middle * middle),
            jnp.sum(attn_branch * attn_branch),
            jnp.sum(expert_branch * expert_branch),
        ]
    )
    gain_rows = col_count // lanes
    sums = small_sums(
        sizes,
        jnp.concatenate(
            [
                gain_one_grad.reshape(gain_rows, lanes),
                gain_two_grad.reshape(gain_rows, lanes),
                gain_sums,
                jnp.pad(stream_part[None, :], ((0, 7), (0, lanes - 3))),
            ],
            axis=0,
        ),
        9,
    )
    tp_sums = jnp.sum(sums[:, 2 * gain_rows :], axis=0)
    token_count = tok_rows * packs * ctx_size
    stream_rms = jnp.sqrt(tp_sums[8, :3] / (token_count * width_all))
    return (
        hidden_out,
        grad_hidden,
        sums[:, :gain_rows].reshape(width_all),
        sums[:, gain_rows : 2 * gain_rows].reshape(width_all),
        tp_sums[0],
        tp_sums[1],
        grad_query,
        grad_key,
        grad_value,
        grad_out,
        grad_router,
        grad_gate,
        grad_up,
        grad_down,
        stream_rms,
    )


def solution(mesh):
    return jax.shard_map(
        on_device,
        mesh=mesh,
        in_specs=(
            P(("fsdp", "ctx"), "tp"),
            P(("fsdp", "ctx"), "tp"),
            P("fsdp", None),
            P("fsdp", None),
            P(("fsdp", "ctx"), None),
            P("tp"),
            P("tp"),
            P(),
            P(),
            P("fsdp", "tp"),
            P("fsdp", "tp"),
            P("fsdp", "tp"),
            P("tp", "fsdp"),
            P(None, "fsdp"),
            P(None, "fsdp", "tp"),
            P(None, "fsdp", "tp"),
            P(None, "fsdp", "tp"),
        ),
        out_specs=(
            P(("fsdp", "ctx"), "tp"),
            P(("fsdp", "ctx"), "tp"),
            P(),
            P(),
            P(),
            P(),
            P(("fsdp", "ctx"), "tp"),
            P(("fsdp", "ctx"), "tp"),
            P(("fsdp", "ctx"), "tp"),
            P("tp", ("fsdp", "ctx")),
            P(None, ("fsdp", "ctx")),
            P(None, ("fsdp", "ctx"), "tp"),
            P(None, ("fsdp", "ctx"), "tp"),
            P(None, ("fsdp", "ctx"), "tp"),
            P(),
        ),
        check_vma=False,
    )
```

```python
import jax
import jax.numpy as jnp
from jax import lax
from jax.experimental import pallas as pl
from jax.experimental.pallas import tpu as pltpu
from jax.sharding import PartitionSpec as P

norm_eps = 1e-06
rope_base = 10000.0


def locate(pack_spots, lengths_row):
    seq_ends = jnp.cumsum(lengths_row)
    starts = seq_ends - lengths_row
    segment = jnp.sum((pack_spots[:, None] >= seq_ends[None, :]).astype(jnp.int32), axis=1)
    slot_ids = jnp.arange(lengths_row.shape[0], dtype=jnp.int32)
    seq_begin = jnp.sum(
        jnp.where(segment[:, None] == slot_ids[None, :], starts[None, :], 0), axis=1
    )
    return (segment, pack_spots - seq_begin)


def rope_tables(pack_spots, head_dim):
    half_dim = head_dim // 2
    inv_freq = rope_base ** (-(jnp.arange(half_dim, dtype=jnp.float32) * 2.0 / head_dim))
    angle_grid = pack_spots.astype(jnp.float32)[:, None] * inv_freq[None, :]
    cosine, sine = jnp.cos(angle_grid), jnp.sin(angle_grid)
    return jnp.concatenate([cosine, cosine], axis=1), jnp.concatenate([-sine, sine], axis=1)


def unrotate(grad_rot, cosine, sine):
    return grad_rot * cosine + jnp.roll(grad_rot * sine, grad_rot.shape[1] // 2, axis=1)


CHUNKS = 2
MESH_ID = pl.DeviceIdType.MESH
VMEM_LIMIT = 64 * 1000 * 1000


class Pack:
    def __init__(self, ctx_size, tp_size, rows, cols, packs=1):
        self.line = ctx_size // 2
        self.packs = packs
        self.tp_size, self.rows, self.cols = tp_size, rows, cols
        self.chunk = rows // CHUNKS
        self.steps = self.line * CHUNKS
        place = lax.axis_index("ctx")
        self.a, self.b = place // 2, place % 2
        self.t = lax.axis_index("tp")
        self.has_up, self.has_down = self.a < self.line - 1, self.a > 0

    def up(self):
        return {"ctx": (self.a + 1) * 2 + self.b}

    def down(self):
        return {"ctx": (self.a - 1) * 2 + self.b}

    def pair(self):
        return {"ctx": self.a * 2 + (1 - self.b)}

    def sibling(self, shift):
        return {"tp": self.t ^ shift}

    def ctx_peer(self, shift):
        return {"ctx": lax.axis_index("ctx") ^ shift}

    def other_pack(self, shift):
        return {"fsdp": lax.axis_index("fsdp") ^ shift}

    def meet(self, everyone):
        barrier = pltpu.get_barrier_semaphore()

        def greet(device):
            pl.semaphore_signal(barrier, inc=1, device_id=device, device_id_type=MESH_ID)

        if everyone:
            near = 2 * self.line - 1
            for shift in range(1, 2 * self.line):
                greet(self.ctx_peer(shift))
        else:
            near = 1 + jnp.where(self.has_up, 1, 0) + jnp.where(self.has_down, 1, 0)

            @pl.when(self.has_up)
            def _():
                greet(self.up())

            @pl.when(self.has_down)
            def _():
                greet(self.down())

            greet(self.pair())
        for shift in range(1, self.tp_size):
            greet(self.sibling(shift))
        for shift in range(1, self.packs):
            greet(self.other_pack(shift))
        pl.semaphore_wait(barrier, near + self.tp_size + self.packs - 2)

    def row0(self, block, k):
        return pl.multiple_of(block * self.rows + k * self.chunk, self.chunk)

    def region(self, ref, block, k, part):
        return ref.at[
            pl.ds(self.row0(block, k), self.chunk),
            pl.ds(pl.multiple_of(part * self.cols, self.cols), self.cols),
        ]


def pick(table, i):
    result = jnp.int32(table[-1])
    for at, value in enumerate(table[:-1]):
        result = jnp.where(i == at, value, result)
    return result


def remote(src, dst, send_sem, recv_sem, device):
    return pltpu.make_async_remote_copy(
        src_ref=src,
        dst_ref=dst,
        send_sem=send_sem,
        recv_sem=recv_sem,
        device_id=device,
        device_id_type=MESH_ID,
    )


def loop(count, body):
    lax.fori_loop(0, count, lambda i, carry: (body(i), carry)[1], 0)


def gather_scratch(ctx_size, tp_size, rows, cols, dtype):
    line, dma = ctx_size // 2, pltpu.SemaphoreType.DMA
    return [
        pltpu.VMEM((ctx_size * rows, tp_size * cols), dtype),
        dma((2 * line * CHUNKS,)),
        dma((2 * line * CHUNKS,)),
        dma((4 * line * (tp_size - 1) * CHUNKS,)),
        dma((ctx_size * CHUNKS,)),
        dma(((tp_size - 1) * ctx_size * CHUNKS,)),
        dma,
    ]


def gather_steps(pack, src, scratch, everyone, lag, begin, before, compute):
    buf, line_sems, pair_sems, tp_sems, own_sems, sib_sems, local_sem = scratch
    line, t, a, b = pack.line, pack.t, pack.a, pack.b
    ctx_size = 2 * line

    def part(block, k):
        return pack.region(buf, block, k, t)

    def line_copy(piece, block, k, down, dist):
        return remote(
            piece,
            part(block, k),
            line_sems.at[(down * line + dist) * CHUNKS + k],
            own_sems.at[block * CHUNKS + k],
            pack.down() if down else pack.up(),
        )

    def pair_copy(piece, block, k, slot):
        return remote(
            piece,
            part(block, k),
            pair_sems.at[slot * CHUNKS + k],
            own_sems.at[block * CHUNKS + k],
            pack.pair(),
        )

    def tp_copy(piece, block, k, slot, shift):
        return remote(
            piece,
            part(block, k),
            tp_sems.at[(slot * (pack.tp_size - 1) + shift - 1) * CHUNKS + k],
            sib_sems.at[((shift - 1) * ctx_size + block) * CHUNKS + k],
            pack.sibling(shift),
        )

    def send_tp(piece, block, k, slot):
        for shift in range(1, pack.tp_size):
            tp_copy(piece, block, k, slot, shift).start()

    def await_own(block, k):
        piece = part(block, k)
        pair_copy(piece, block, k, 0).wait_recv()

    pack.meet(everyone)
    mine = a * 2 + b
    own_copy = pltpu.make_async_copy(
        src,
        buf.at[
            pl.ds(pl.multiple_of(mine * pack.rows, pack.rows), pack.rows),
            pl.ds(pl.multiple_of(t * pack.cols, pack.cols), pack.cols),
        ],
        local_sem,
    )
    own_copy.start()
    for k in range(CHUNKS):
        piece = src.at[pl.ds(k * pack.chunk, pack.chunk), :]

        @pl.when(pack.has_up)
        def _():
            line_copy(piece, mine, k, 0, 0).start()

        @pl.when(pack.has_down)
        def _():
            line_copy(piece, mine, k, 1, 0).start()

        pair_copy(piece, mine, k, 0).start()
    for k in range(CHUNKS):
        send_tp(src.at[pl.ds(k * pack.chunk, pack.chunk), :], mine, k, 0)
    begin()
    own_copy.wait()

    def ways(dist):
        below, above = a - dist, a + dist
        return (
            (0, below, below >= 0, jnp.logical_and(below >= 0, pack.has_up)),
            (1, above, above < line, jnp.logical_and(above < line, pack.has_down)),
        )

    def from_line(dist, k):
        for down, node, there, onward in ways(dist):
            block = node * 2 + b

            @pl.when(there)
            def _():
                await_own(block, k)

            @pl.when(onward)
            def _():
                line_copy(part(block, k), block, k, down, dist).start()

            @pl.when(there)
            def _():
                pair_copy(part(block, k), block, k, down * line + dist).start()
                send_tp(part(block, k), block, k, down * line + dist)

    def from_pair(dist, k):
        for down, node, there, _ in ways(dist):
            block = node * 2 + (1 - b)
            if down:
                there = jnp.logical_and(there, dist > 0)

            @pl.when(there)
            def _():
                await_own(block, k)
                send_tp(part(block, k), block, k, (2 + down) * line + dist)

    def work(block, k, order):
        for shift in range(1, pack.tp_size):
            piece = pack.region(buf, block, k, t ^ shift)
            remote(
                piece,
                piece,
                tp_sems.at[0],
                sib_sems.at[((shift - 1) * ctx_size + block) * CHUNKS + k],
                pack.sibling(shift),
            ).wait_recv()
        compute(pack.row0(block, k), block * CHUNKS + k, order)

    def step(s):
        dist, k = s // CHUNKS, s % CHUNKS

        @pl.when(dist + 1 < line)
        def _():
            from_line(dist + 1, k)

        @pl.when(s < pack.steps)
        def _():
            from_pair(dist, k)

        @pl.when(s == lag)
        def _():
            before()

        turn = s - lag

        def side(i):
            late = turn - i
            node, late_k = a ^ (late // CHUNKS), late % CHUNKS

            @pl.when(jnp.logical_and(late >= 0, late < pack.steps))
            def _():
                order = jnp.where(
                    i == 0,
                    jnp.maximum(2 * turn - 1, 0),
                    jnp.minimum(2 * turn, 2 * pack.steps - 1),
                )
                work(node * 2 + jnp.where(i == 0, b, 1 - b), late_k, order)

        loop(2, side)

    loop(pack.steps + 1 + lag, step)

    def drain(s):
        dist, k = s // CHUNKS, s % CHUNKS
        piece = part(0, 0)
        for down, _, there, onward in ways(dist):

            @pl.when(jnp.logical_and(onward, dist < line - 1))
            def _():
                line_copy(piece, 0, k, down, dist).wait_send()

            if down:
                there = jnp.logical_and(there, dist > 0)

            @pl.when(there)
            def _():
                pair_copy(piece, 0, k, down * line + dist).wait_send()
                for shift in range(1, pack.tp_size):
                    tp_copy(piece, 0, k, down * line + dist, shift).wait_send()
                    tp_copy(piece, 0, k, (2 + down) * line + dist, shift).wait_send()

    loop(pack.steps, drain)


def scatter_scratch(ctx_size, tp_size, rows, cols):
    line, dma = ctx_size // 2, pltpu.SemaphoreType.DMA
    low = jnp.bfloat16
    return [
        pltpu.VMEM((ctx_size * rows, tp_size * cols), low),
        pltpu.VMEM(((tp_size - 1) * ctx_size * rows, cols), low),
        pltpu.VMEM((line * rows, cols), low),
        pltpu.VMEM((2 * line * rows, cols), low),
        dma(((tp_size - 1) * ctx_size * CHUNKS,)),
        dma((line * CHUNKS,)),
        dma((line * CHUNKS,)),
        dma(((tp_size - 1) * ctx_size * CHUNKS,)),
        dma((line * CHUNKS,)),
        dma((2 * line * CHUNKS,)),
    ]


def scatter_steps(pack, scratch, everyone, begin, before, compute, jobs, finish):
    (full, sib_buf, pair_buf, line_buf, tp_send, pair_send, line_send, tp_recv, pair_recv, line_recv) = scratch
    line, t, a, b = pack.line, pack.t, pack.a, pack.b
    ctx_size = 2 * line
    wide, low = jnp.float32, jnp.bfloat16
    table = [
        sorted(range(line), key=lambda o, node=node: (-abs(o - node), o)) for node in range(line)
    ]

    def owner(i):
        result = jnp.int32(0)
        for node in range(line):
            for place in range(line):
                here = jnp.logical_and(a == node, i == place)
                result = jnp.where(here, table[node][place], result)
        return result

    def tp_copy(block, k, shift):
        return remote(
            pack.region(full, block, k, t ^ shift),
            sib_buf.at[
                pl.ds(pack.row0((shift - 1) * ctx_size + block, k), pack.chunk), :
            ],
            tp_send.at[((shift - 1) * ctx_size + block) * CHUNKS + k],
            tp_recv.at[((shift - 1) * ctx_size + block) * CHUNKS + k],
            pack.sibling(shift),
        )

    def pair_copy(node, k):
        return remote(
            pack.region(full, node * 2 + (1 - b), k, t),
            pair_buf.at[pl.ds(pack.row0(node, k), pack.chunk), :],
            pair_send.at[node * CHUNKS + k],
            pair_recv.at[node * CHUNKS + k],
            pack.pair(),
        )

    def line_copy(node, k, down):
        return remote(
            pack.region(full, node * 2 + b, k, t),
            line_buf.at[pl.ds(pack.row0(down * line + node, k), pack.chunk), :],
            line_send.at[node * CHUNKS + k],
            line_recv.at[(down * line + node) * CHUNKS + k],
            pack.down() if down else pack.up(),
        )

    def own_part(block, k):
        return full[
            pl.ds(pack.row0(block, k), pack.chunk),
            pl.ds(pl.multiple_of(t * pack.cols, pack.cols), pack.cols),
        ].astype(wide)

    def put_part(block, k, value):
        full[
            pl.ds(pack.row0(block, k), pack.chunk),
            pl.ds(pl.multiple_of(t * pack.cols, pack.cols), pack.cols),
        ] = value.astype(low)

    def landed(ref, block, k):
        return ref[pl.ds(pack.row0(block, k), pack.chunk), :].astype(wide)

    def fill(block):
        row0 = pl.multiple_of(block * pack.rows, pack.rows)
        full[pl.ds(row0, pack.rows), :] = compute(row0)
        for k in range(CHUNKS):
            for shift in range(1, pack.tp_size):
                tp_copy(block, k, shift).start()

    def join(block, k):
        total = own_part(block, k)
        for shift in range(1, pack.tp_size):
            tp_copy(block, k, shift).wait_recv()
            total = total + landed(sib_buf, (shift - 1) * ctx_size + block, k)
        put_part(block, k, total)

    pack.meet(everyone)
    begin()
    before()

    def step(s):
        @pl.when(s < pack.steps)
        def _():
            node, k = owner(s // CHUNKS), s % CHUNKS

            def side(i):
                @pl.when(k == 0)
                def _():
                    fill(node * 2 + jnp.where(i == 0, 1 - b, b))

                jobs(2 * s + i)

            loop(2, side)

        late = s - 1

        @pl.when(jnp.logical_and(late >= 0, late < pack.steps))
        def _():
            node, k = owner(late // CHUNKS), late % CHUNKS

            def side(i):
                join(node * 2 + jnp.where(i == 0, 1 - b, b), k)

                @pl.when(i == 0)
                def _():
                    pair_copy(node, k).start()

            loop(2, side)

        later = s - 4

        @pl.when(later >= 0)
        def _():
            node, k = owner(later // CHUNKS), later % CHUNKS
            pair_copy(node, k).wait_recv()
            put_part(
                node * 2 + b, k, own_part(node * 2 + b, k) + landed(pair_buf, node, k)
            )
            from_below = jnp.logical_and(pack.has_down, node >= a)
            from_above = jnp.logical_and(pack.has_up, node <= a)
            for down, there in ((0, from_below), (1, from_above)):

                @pl.when(there)
                def _():
                    line_copy(node, k, down).wait_recv()
                    put_part(
                        node * 2 + b,
                        k,
                        own_part(node * 2 + b, k) + landed(line_buf, down * line + node, k),
                    )

            @pl.when(node > a)
            def _():
                line_copy(node, k, 0).start()

            @pl.when(node < a)
            def _():
                line_copy(node, k, 1).start()

            @pl.when(node == a)
            def _():
                finish(k, own_part(node * 2 + b, k))

    loop(pack.steps + 4, step)

    def drain(s):
        node, k = s // CHUNKS, s % CHUNKS
        pair_copy(node, k).wait_send()
        for shift in range(1, pack.tp_size):
            tp_copy(node * 2, k, shift).wait_send()
            tp_copy(node * 2 + 1, k, shift).wait_send()

        @pl.when(node > a)
        def _():
            line_copy(node, k, 0).wait_send()

        @pl.when(node < a)
        def _():
            line_copy(node, k, 1).wait_send()

    loop(pack.steps, drain)


ANY = pl.BlockSpec(memory_space=pl.ANY)


def nn_dot(left, right):
    return lax.dot_general(
        left, right, (((1,), (0,)), ((), ())), preferred_element_type=jnp.float32
    )


def nt_dot(left, right):
    return lax.dot_general(
        left, right, (((1,), (1,)), ((), ())), preferred_element_type=jnp.float32
    )


def tn_dot(left, right):
    return lax.dot_general(
        left, right, (((0,), (0,)), ((), ())), preferred_element_type=jnp.float32
    )


class Out:
    def __init__(self, width, dtype, flip=False, late=False):
        self.width, self.dtype, self.flip, self.late = width, dtype, flip, late

    def shape(self, rows):
        return (self.width, rows) if self.flip else (rows, self.width)

    def window(self, ref, window):
        return ref.at[:, window] if self.flip else ref.at[window, :]


class Parts:
    def __init__(self, shape, pieces):
        self.shape, self.pieces = shape, pieces


class Swap:
    def __init__(self, axis, shape, pieces, keep):
        self.axis, self.shape, self.pieces, self.keep = axis, shape, pieces, keep


class Ship:
    def __init__(self, axis, array, source, shape):
        self.axis, self.array, self.source, self.shape = axis, array, source, shape


class Make:
    def __init__(self, width, features, tile, send):
        self.width, self.features, self.tile, self.send = width, features, tile, send


class Deal:
    def __init__(self, own, far):
        self.own, self.far = own, far


class Tiles:
    def __init__(self, width, features, tile):
        self.width, self.features, self.tile = width, features, tile


def whole(ref):
    return ref


def pack_call(
    sizes,
    shape,
    piece,
    collective_id,
    flops,
    gathered=None,
    resident=(),
    outs=(),
    totals=(),
    last=None,
    keep=False,
    swaps=(),
    ships=(),
    tiles=None,
    makes=(),
    deals=(),
    lag=1,
):
    packs, ctx_size, tp_size = sizes
    rows, cols = shape
    all_rows, all_cols = ctx_size * rows, tp_size * cols
    pieces = ctx_size * CHUNKS
    dma = pltpu.SemaphoreType.DMA
    gather = gathered is not None
    if gather:
        base = gather_scratch(ctx_size, tp_size, rows, cols, gathered.dtype)
    else:
        base = scatter_scratch(ctx_size, tp_size, rows, cols)
    axis_size = {"fsdp": packs, "ctx": ctx_size, "tp": tp_size}
    inputs = []

    def enlist(array):
        for i, known in enumerate(inputs):
            if known is array:
                return i
        inputs.append(array)
        return len(inputs) - 1

    if gather:
        enlist(gathered)
    resident = list(resident)
    first_deal = len(resident)
    for deal in deals:
        resident += [deal.own, deal.far]
    parts = [
        r if isinstance(r, Parts) else Parts(r.shape, [(r, whole, whole)]) for r in resident
    ]
    part_list = [[(enlist(x), src, dst) for x, src, dst in p.pieces] for p in parts]
    swap_list = [[(enlist(x), src, dst) for x, src, dst in w.pieces] for w in swaps]
    ship_list = [enlist(ship.array) for ship in ships]
    swap_count = sum(len(w.pieces) * axis_size[w.axis] for w in swaps)
    ship_count = sum(axis_size[ship.axis] for ship in ships)
    kept_swaps = [i for i, w in enumerate(swaps) if w.keep]
    n_out = len(outs) + len(totals) + keep + len(kept_swaps) + len(ships)
    tile_rows = 128
    features = all_cols
    own_features = features // (packs * ctx_size)
    splits = tile_rows // own_features
    own_tiles = features // packs // tile_rows
    far_tiles = (packs - 1) * own_tiles
    assert own_tiles + far_tiles == pieces
    stride = pieces // own_tiles
    deal_order = (4, 1, 6, 2, 5, 3, 7, 0) if own_tiles == 8 else tuple(range(own_tiles))

    def kernel(*refs):
        refs = list(refs)

        def take(count):
            taken = refs[:count]
            del refs[:count]
            return taken

        given = take(len(inputs))
        sum_ref = None if gather else take(1)[0]
        out_refs = take(n_out)
        blocks_ref = None if tiles is None else take(1)[0]
        make_outs = [take(2) for _ in makes]
        deal_outs = take(len(deals))
        scratch = take(len(base))
        held = take(len(resident))
        stage = take(len(outs))
        total_refs = take(len(totals))
        swap_bufs = take(len(swaps))
        (held_sem, out_sem, late_sem, swap_local, swap_send, swap_recv, ship_send, ship_recv) = take(8)
        if tiles is not None:
            tile_stage, tile_far, tile_send, far_recv, block_recv = take(5)
        make_stages = take(len(makes))
        make_send, make_recv, deal_send, deal_recv = take(4)
        over_packs = swaps or ships or tiles is not None or any(make.send for make in makes)
        everyone = tiles is not None or deals or any(ship.axis == "ctx" for ship in ships)
        pack = Pack(ctx_size, tp_size, rows, cols, packs if over_packs else 1)
        mine = {axis: lax.axis_index(axis) for axis in axis_size}
        loads = []
        for target_ref, copies in zip(held, part_list):
            for which, source, target in copies:
                loads.append(
                    pltpu.make_async_copy(
                        source(given[which]), target(target_ref), held_sem.at[len(loads)]
                    )
                )
        swap_copies, swap_sends = [], []
        index = 0
        for swap, buf, copies in zip(swaps, swap_bufs, swap_list):
            for which, source, target in copies:
                here = source(given[which])
                there = target(buf, mine[swap.axis])
                swap_copies.append(pltpu.make_async_copy(here, there, swap_local.at[index]))
                for shift in range(1, axis_size[swap.axis]):
                    slot = index + shift
                    device = {swap.axis: mine[swap.axis] ^ shift}
                    theirs = target(buf, mine[swap.axis] ^ shift)
                    swap_sends.append(
                        (
                            remote(here, there, swap_send.at[slot], swap_recv.at[slot], device),
                            remote(theirs, theirs, swap_send.at[slot], swap_recv.at[slot], device),
                        )
                    )
                index += axis_size[swap.axis]
        late = []
        for i, where in enumerate(kept_swaps):
            late.append((swap_bufs[where], out_refs[len(outs) + len(totals) + keep + i]))
        late_copies = [
            pltpu.make_async_copy(here, there, late_sem.at[i])
            for i, (here, there) in enumerate(late)
        ]
        ship_local, ship_copies = [], []
        index = 0
        for ship, which, landing in zip(ships, ship_list, out_refs[n_out - len(ships) :]):
            place = mine[ship.axis]
            if ship.axis == "ctx":
                here = ship.source(given[which], 0)
                ship_local.append(
                    pltpu.make_async_copy(here, landing.at[place], ship_send.at[index])
                )
            for shift in range(1, axis_size[ship.axis]):
                here = ship.source(given[which], shift)
                there = landing.at[place] if ship.axis == "ctx" else landing.at[shift - 1]
                theirs = landing.at[place ^ shift] if ship.axis == "ctx" else there
                device = {ship.axis: place ^ shift}
                sems = ship_send.at[index + shift], ship_recv.at[index + shift]
                ship_copies.append(
                    (remote(here, there, *sems, device), remote(theirs, theirs, *sems, device))
                )
            index += axis_size[ship.axis]

        def begin():
            for copy in swap_copies + ship_local:
                copy.start()
            for send, _ in swap_sends + ship_copies:
                send.start()

        def before():
            for ref in total_refs:
                ref[...] = jnp.zeros_like(ref)
            for load in loads:
                load.wait()
            for copy in swap_copies:
                copy.wait()
            for send, receive in swap_sends:
                receive.wait_recv()
            for copy in late_copies:
                copy.start()

        def stores(row0, index):
            window = pl.ds(row0, pack.chunk)
            copies = []
            for i, out in enumerate(outs):
                if not out.late:
                    copies.append((out.window(stage[i], window), out.window(out_refs[i], window), i))
            if keep:
                i = len(outs)
                copies.append(
                    (scratch[0].at[window, :], out_refs[i + len(totals)].at[window, :], i)
                )
            return [
                pltpu.make_async_copy(here, there, out_sem.at[i * pieces + index])
                for here, there, i in copies
            ]

        def put(window, values):
            early = [i for i, out in enumerate(outs) if not out.late]
            for i, value in zip(early, values):
                out = outs[i]
                if out.flip:
                    stage[i][:, window] = value.astype(out.dtype)
                else:
                    stage[i][window, :] = value.astype(out.dtype)

        ahead = 3

        def is_far(order):
            if far_tiles != own_tiles:
                return order < far_tiles
            middle = jnp.logical_and(order >= ahead, order < pieces - ahead)
            return jnp.where(middle, (order - ahead) % 2 == 1, order < ahead)

        def rank(order):
            if far_tiles != own_tiles:
                return jnp.where(order < far_tiles, order, order - far_tiles)
            middle = (order - ahead) // 2
            return jnp.where(
                order < ahead,
                order,
                jnp.where(
                    order >= pieces - ahead,
                    order - far_tiles,
                    jnp.where(is_far(order), ahead + middle, middle),
                ),
            )

        def tile_copy(order, which, shift):
            return remote(
                tile_stage.at[order],
                tile_far.at[which],
                tile_send.at[order * splits],
                far_recv.at[which],
                {"fsdp": mine["fsdp"] ^ shift},
            )

        def block_copy(order, split, owner):
            return remote(
                tile_stage.at[order, pl.ds(split * own_features, own_features), :],
                blocks_ref.at[mine["ctx"]],
                tile_send.at[order * splits + split],
                block_recv.at[mine["ctx"]],
                {"ctx": owner},
            )

        def block_store(order, split):
            return pltpu.make_async_copy(
                tile_stage.at[order, pl.ds(split * own_features, own_features), :],
                blocks_ref.at[mine["ctx"]],
                tile_send.at[order * splits + split],
            )

        def each_block(order, go_away, stay):
            for split in range(splits):
                owner = ((mine["ctx"] // splits) ^ pick(deal_order, rank(order))) * splits + split

                @pl.when(owner != mine["ctx"])
                def _():
                    go_away(order, split, owner)

                @pl.when(owner == mine["ctx"])
                def _():
                    stay(order, split)

        def make_tile(order):
            if tiles is None:
                return
            far, which = is_far(order), rank(order)
            shift = jnp.where(far, which // own_tiles + 1, 0)
            place = (mine["ctx"] // splits) ^ pick(deal_order, which % own_tiles)
            first = ((mine["fsdp"] ^ shift) * own_tiles + place) * tile_rows
            value = tiles.tile(pl.ds(pl.multiple_of(first, tile_rows), tile_rows), held)

            @pl.when(far)
            def _():
                tile_stage[order] = value.astype(jnp.bfloat16)
                tile_copy(order, which, shift).start()

            @pl.when(jnp.logical_not(far))
            def _():
                total = value
                for other in range(packs - 1):
                    slot = other * own_tiles + which
                    tile_copy(order, slot, 1).wait_recv()
                    total = total + tile_far[slot].astype(jnp.float32)
                tile_stage[order] = total.astype(jnp.bfloat16)
                each_block(
                    order,
                    lambda *where: block_copy(*where).start(),
                    lambda *where: block_store(*where).start(),
                )

        def finish_tiles():
            if tiles is None:
                return

            def sent(order):
                @pl.when(is_far(order))
                def _():
                    tile_copy(order, 0, 1).wait_send()

                @pl.when(jnp.logical_not(is_far(order)))
                def _():
                    each_block(
                        order,
                        lambda *where: block_copy(*where).wait_send(),
                        lambda *where: block_store(*where).wait(),
                    )

            loop(pieces, sent)
            for shift in range(1, ctx_size):
                landed = blocks_ref.at[mine["ctx"] ^ shift]
                remote(
                    landed,
                    landed,
                    tile_send.at[0],
                    block_recv.at[mine["ctx"] ^ shift],
                    {"ctx": mine["ctx"] ^ shift},
                ).wait_recv()

        def make_copies(i, order):
            far = order < far_tiles
            which = jnp.where(far, order, order - far_tiles)
            shift = jnp.where(far, which // own_tiles + 1, 0)
            window = pl.ds(
                pl.multiple_of(which % own_tiles * tile_rows, tile_rows), tile_rows
            )
            here = make_stages[i].at[order]
            sem = make_send.at[i * pieces + order]
            own_out, far_out = make_outs[i]
            slot = jnp.maximum(shift - 1, 0)
            send = remote(
                here,
                far_out.at[slot, window, :],
                sem,
                make_recv.at[i * pieces + order],
                {"fsdp": mine["fsdp"] ^ shift},
            )
            away = pltpu.make_async_copy(here, far_out.at[slot, window, :], sem)
            stay = pltpu.make_async_copy(here, own_out.at[window, :], sem)
            return far, shift, which % own_tiles, send, away, stay

        def make_parts(order):
            for i, make in enumerate(makes):
                far, shift, place, send, away, stay = make_copies(i, order)
                first = ((mine["fsdp"] ^ shift) * own_tiles + place) * tile_rows
                value = make.tile(pl.ds(pl.multiple_of(first, tile_rows), tile_rows), held)
                make_stages[i][order] = value.astype(jnp.bfloat16)

                @pl.when(far)
                def _():
                    (send if make.send else away).start()

                @pl.when(jnp.logical_not(far))
                def _():
                    stay.start()

        def finish_parts():
            def sent(order):
                for i, make in enumerate(makes):
                    far, _, _, send, away, stay = make_copies(i, order)

                    @pl.when(far)
                    def _():
                        if make.send:
                            send.wait_send()
                            send.wait_recv()
                        else:
                            away.wait()

                    @pl.when(jnp.logical_not(far))
                    def _():
                        stay.wait()

            loop(pieces, sent)

        def deal_blocks(i, turn, go_away, stay):
            own_buf, landing = held[first_deal + 2 * i], deal_outs[i]
            for split in range(splits):
                owner = ((mine["ctx"] // splits) ^ pick(deal_order, turn)) * splits + split
                here = own_buf.at[
                    pl.ds(pl.multiple_of(owner * own_features, own_features), own_features), :
                ]
                there = landing.at[mine["ctx"]]
                sem = deal_send.at[(i * own_tiles + turn) * splits + split]

                @pl.when(owner != mine["ctx"])
                def _():
                    go_away(
                        remote(
                            here,
                            there,
                            sem,
                            deal_recv.at[i * ctx_size + mine["ctx"]],
                            {"ctx": owner},
                        )
                    )

                @pl.when(owner == mine["ctx"])
                def _():
                    stay(pltpu.make_async_copy(here, there, sem))

        def deal_out(order):
            if not deals:
                return

            @pl.when(order % stride == 0)
            def _():
                turn = order // stride
                place = (mine["ctx"] // splits) ^ pick(deal_order, turn)
                window = pl.ds(pl.multiple_of(place * tile_rows, tile_rows), tile_rows)
                for i in range(len(deals)):
                    own_buf, far_buf = held[first_deal + 2 * i], held[first_deal + 2 * i + 1]
                    total = own_buf[window, :].astype(jnp.float32)
                    for other in range(packs - 1):
                        total = total + far_buf[other, window, :].astype(jnp.float32)
                    own_buf[window, :] = total.astype(jnp.bfloat16)
                    deal_blocks(i, turn, lambda copy: copy.start(), lambda copy: copy.start())

        def finish_deals():
            if not deals:
                return

            def sent(turn):
                for i in range(len(deals)):
                    deal_blocks(i, turn, lambda copy: copy.wait_send(), lambda copy: copy.wait())

            loop(own_tiles, sent)
            for i in range(len(deals)):
                for shift in range(1, ctx_size):
                    place = mine["ctx"] ^ shift
                    landed = deal_outs[i].at[place]
                    sem = deal_recv.at[i * ctx_size + place]
                    remote(landed, landed, deal_send.at[0], sem, {"ctx": place}).wait_recv()

        for load in loads:
            load.start()
        if gather:

            def compute(row0, index, order):
                window = pl.ds(row0, pack.chunk)
                put(window, piece(scratch[0][window, :], window, held + swap_bufs, total_refs))
                for store in stores(row0, index):
                    store.start()
                deal_out(order)
                make_tile(order)
                make_parts(order)

            gather_steps(pack, given[0], scratch, everyone, lag, begin, before, compute)
        else:

            def compute(row0):
                window = pl.ds(row0, pack.rows)
                rows_value, values = piece(window, held + swap_bufs, total_refs)
                put(window, values)
                return rows_value.astype(jnp.bfloat16)

            def jobs(order):
                deal_out(order)
                make_tile(order)
                make_parts(order)

            def finish(k, total):
                sum_ref[pl.ds(pl.multiple_of(k * pack.chunk, pack.chunk), pack.chunk), :] = total

            scatter_steps(pack, scratch, everyone, begin, before, compute, jobs, finish)
        if last is not None:
            last(held + swap_bufs, stage, total_refs, pack.chunk)
        ends = []
        for i, out in enumerate(outs):
            if out.late:
                ends.append((stage[i], out_refs[i]))
        for i, ref in enumerate(total_refs):
            ends.append((ref, out_refs[len(outs) + i]))
        end_copies = [
            pltpu.make_async_copy(here, there, late_sem.at[len(late) + i])
            for i, (here, there) in enumerate(ends)
        ]
        for copy in end_copies:
            copy.start()

        def drain(index):
            for store in stores(pl.multiple_of(index * pack.chunk, pack.chunk), index):
                store.wait()

        loop(pieces, drain)
        finish_tiles()
        finish_parts()
        finish_deals()
        for copy in late_copies + end_copies + ship_local:
            copy.wait()
        for send, _ in swap_sends:
            send.wait_send()
        for send, receive in ship_copies:
            send.wait_send()
            receive.wait_recv()

    low = jnp.bfloat16
    shapes = [jax.ShapeDtypeStruct(out.shape(all_rows), out.dtype) for out in outs]
    shapes += [jax.ShapeDtypeStruct(dims, dtype) for dims, dtype in totals]
    if keep:
        shapes.append(jax.ShapeDtypeStruct((all_rows, all_cols), gathered.dtype))
    shapes += [jax.ShapeDtypeStruct(swaps[i].shape, low) for i in kept_swaps]
    for ship in ships:
        slots = ctx_size if ship.axis == "ctx" else packs - 1
        shapes.append(jax.ShapeDtypeStruct((slots,) + ship.shape, ship.array.dtype))
    if tiles is not None:
        shapes.append(jax.ShapeDtypeStruct((ctx_size, own_features, tiles.width), low))
    part_features = features // packs
    for make in makes:
        shapes.append(jax.ShapeDtypeStruct((part_features, make.width), low))
        shapes.append(jax.ShapeDtypeStruct((packs - 1, part_features, make.width), low))
    for deal in deals:
        shapes.append(jax.ShapeDtypeStruct((ctx_size, own_features, deal.own.shape[1]), low))
    out_specs = [ANY] * len(shapes)
    if not gather:
        shapes = [jax.ShapeDtypeStruct(shape, jnp.float32)] + shapes
        out_specs = [pl.BlockSpec(memory_space=pltpu.VMEM)] + out_specs
    tile_scratch = []
    if tiles is not None:
        tile_scratch = [
            pltpu.VMEM((pieces, tile_rows, tiles.width), low),
            pltpu.VMEM((far_tiles, tile_rows, tiles.width), low),
            dma((pieces * splits,)),
            dma((far_tiles,)),
            dma((ctx_size,)),
        ]
    return pl.pallas_call(
        kernel,
        out_shape=tuple(shapes),
        in_specs=[ANY] * len(inputs),
        out_specs=tuple(out_specs),
        scratch_shapes=base
        + [pltpu.VMEM(p.shape, p.pieces[0][0].dtype) for p in parts]
        + [pltpu.VMEM(out.shape(all_rows), out.dtype) for out in outs]
        + [pltpu.VMEM(dims, dtype) for dims, dtype in totals]
        + [pltpu.VMEM(swap.shape, low) for swap in swaps]
        + [
            dma((max(1, sum(len(p.pieces) for p in parts)),)),
            dma(((len(outs) + 1) * pieces,)),
            dma((len(kept_swaps) + len(outs) + len(totals) + 1,)),
            dma((max(1, swap_count),)),
            dma((max(1, swap_count),)),
            dma((max(1, swap_count),)),
            dma((max(1, ship_count),)),
            dma((max(1, ship_count),)),
        ]
        + tile_scratch
        + [pltpu.VMEM((pieces, tile_rows, make.width), low) for make in makes]
        + [
            dma((max(1, len(makes)) * pieces,)),
            dma((max(1, len(makes)) * pieces,)),
            dma((max(1, len(deals)) * own_tiles * splits,)),
            dma((max(1, len(deals)) * ctx_size,)),
        ],
        compiler_params=pltpu.CompilerParams(
            collective_id=collective_id, has_side_effects=True, vmem_limit_bytes=VMEM_LIMIT
        ),
        cost_estimate=pl.CostEstimate(
            flops=flops, bytes_accessed=8 * all_rows * all_cols, transcendentals=0
        ),
    )(*inputs)


def small_sums(sizes, tensor, collective_id):
    packs, ctx_size, tp_size = sizes
    dma = pltpu.SemaphoreType.DMA
    count = tensor.shape[0]

    def kernel(src, out_ref, ctx_buf, mid, rest_buf, send_sems, recv_sems):
        f, c, t = (lax.axis_index(axis) for axis in ("fsdp", "ctx", "tp"))
        ctx_peers = [(shift, {"ctx": c ^ shift}) for shift in range(1, ctx_size)]
        rest_peers = [
            (shift * tp_size + turn, {"fsdp": f ^ shift, "tp": t ^ turn})
            for shift in range(packs)
            for turn in range(tp_size)
            if shift or turn
        ]
        barrier = pltpu.get_barrier_semaphore()
        for _, device in ctx_peers + rest_peers:
            pl.semaphore_signal(barrier, inc=1, device_id=device, device_id_type=MESH_ID)
        pl.semaphore_wait(barrier, len(ctx_peers) + len(rest_peers))

        def exchange(source, buf, peers, offset):
            copies = [
                remote(
                    source,
                    buf.at[slot],
                    send_sems.at[offset + slot],
                    recv_sems.at[offset + slot],
                    device,
                )
                for slot, device in peers
            ]
            for copy in copies:
                copy.start()
            for copy in copies:
                copy.wait()

        exchange(src, ctx_buf, ctx_peers, 0)
        total = src[...]
        for slot, _ in ctx_peers:
            total = total + ctx_buf[slot]
        mid[...] = total
        exchange(mid, rest_buf, rest_peers, ctx_size)
        rest_buf[0] = total
        for turn in range(tp_size):
            part = rest_buf[turn]
            for shift in range(1, packs):
                part = part + rest_buf[shift * tp_size + turn]
            out_ref[t ^ turn] = part

    return pl.pallas_call(
        kernel,
        out_shape=jax.ShapeDtypeStruct((tp_size, count, tensor.shape[1]), jnp.float32),
        in_specs=[pl.BlockSpec(memory_space=pltpu.VMEM)],
        out_specs=pl.BlockSpec(memory_space=pltpu.VMEM),
        scratch_shapes=[
            pltpu.VMEM((ctx_size,) + tensor.shape, jnp.float32),
            pltpu.VMEM(tensor.shape, jnp.float32),
            pltpu.VMEM((packs * tp_size,) + tensor.shape, jnp.float32),
            dma((ctx_size + packs * tp_size,)),
            dma((ctx_size + packs * tp_size,)),
        ],
        compiler_params=pltpu.CompilerParams(collective_id=collective_id, has_side_effects=True),
    )(tensor)

def on_device(
    hidden_in,
    cotangent,
    positions,
    seq_lengths,
    expert_ids,
    attn_norm,
    ffn_norm,
    query_norm,
    key_norm,
    w_query,
    w_key,
    w_value,
    w_out,
    w_router,
    w_gate,
    w_up,
    w_down,
):
    tok_rows, col_count = hidden_in.shape
    packs, ctx_size, tp_size = (lax.axis_size(axis) for axis in ("fsdp", "ctx", "tp"))
    sizes = (packs, ctx_size, tp_size)
    own_shape = (tok_rows, col_count)
    ctx_place = lax.axis_index("ctx")
    width_all = col_count * tp_size
    part_width = width_all // packs
    pack_rows = tok_rows * ctx_size
    head_dim = query_norm.shape[0]
    local_heads = w_query.shape[1] // head_dim
    expert_count, hidden_units = w_gate.shape[0], w_gate.shape[2]
    own_experts = expert_count // ctx_size
    own_units = own_experts * hidden_units
    top_count = expert_ids.shape[1]
    sharers = ctx_size // local_heads
    score_scale = head_dim ** (-0.5)
    wide = jnp.float32
    slim = jnp.bfloat16
    lanes = 128

    def row_total(tensor):
        return lax.psum(tensor, "tp")

    def units_of(ref, window, slot):
        return ref[window, pl.ds(slot * hidden_units, hidden_units)]

    def own_queries(window, value):
        if sharers == 1:
            return value
        share = window.start // (pack_rows // sharers)
        return jnp.where(share == lax.axis_index("ctx") // local_heads, value, 0.0)

    def head_window():
        return pl.ds(
            pl.multiple_of(lax.axis_index("ctx") % local_heads * head_dim, head_dim), head_dim
        )

    def part_of(place, size):
        return pl.ds(pl.multiple_of(place * size, size), size)

    half_rows = part_width // 2

    def half_ship(weight, slot, half):
        return Ship(
            "fsdp",
            weight,
            lambda ref, shift: ref.at[
                lax.axis_index("ctx") * own_experts + slot,
                pl.ds(half * half_rows, half_rows),
                :,
            ],
            (half_rows, hidden_units),
        )

    halves = [(slot, half) for slot in range(own_experts) for half in range(2)]
    expert_ships = [half_ship(w, *which) for w in (w_gate, w_up, w_down) for which in halves]
    first_ships = len(expert_ships) // 6
    second_ships = first_ships + (len(expert_ships) - first_ships) // 2

    def expert_weight(weight, far):
        pieces = [
            (
                weight,
                lambda ref: ref.at[pl.ds(lax.axis_index("ctx") * own_experts, own_experts), :, :],
                lambda buf: buf.at[:, part_of(lax.axis_index("fsdp"), part_width), :],
            )
        ]
        for (slot, half), array in zip(halves, far):
            for shift in range(1, packs):
                pieces.append(
                    (
                        array,
                        lambda ref, shift=shift: ref.at[shift - 1],
                        lambda buf, slot=slot, half=half, shift=shift: buf.at[
                            slot,
                            part_of((lax.axis_index("fsdp") ^ shift) * 2 + half, half_rows),
                            :,
                        ],
                    )
                )
        return Parts((own_experts, width_all, hidden_units), pieces)

    segment, place = locate(positions[0], seq_lengths[0])
    cosine, sine = rope_tables(place, head_dim)
    segment_rows = jnp.broadcast_to(segment[:, None], (pack_rows, lanes))
    segment_cols = jnp.broadcast_to(segment[None, :], (8, pack_rows))

    def project(rows, window, held, totals):
        cos_table, sin_table, gain_q, gain_k, weight, _, gain, _ = held
        hidden = rows.astype(wide)
        inverse = lax.rsqrt(jnp.mean(hidden * hidden, axis=1, keepdims=True) + norm_eps)
        normed = (hidden * inverse * gain[...].astype(wide)).astype(slim)
        raw = nn_dot(normed, weight[...])
        cos_rows, sin_rows = cos_table[window, :], sin_table[window, :]

        def prepare(raw_proj, gain_vec):
            inv = lax.rsqrt(jnp.mean(raw_proj * raw_proj, axis=1, keepdims=True) + norm_eps)
            scaled = raw_proj * inv * gain_vec[...]
            return scaled * cos_rows + pltpu.roll(scaled, head_dim // 2, 1) * sin_rows

        query_raw = raw[:, :head_dim]
        key_raw = raw[:, head_dim : 2 * head_dim]
        key_turned = prepare(key_raw, gain_k)
        return (
            normed,
            jnp.broadcast_to(inverse, (rows.shape[0], lanes)),
            query_raw,
            key_raw,
            prepare(query_raw, gain_q),
            key_turned,
            key_turned.T,
            raw[:, 2 * head_dim :],
        )

    gain_query = query_norm.astype(wide)[None, :]
    gain_key = key_norm.astype(wide)[None, :]
    (
        normed_first,
        inv_all,
        query_raw,
        key_raw,
        query_low,
        key_low,
        key_flip,
        value_low,
        qkv_weight,
        out_weight,
        router_full,
        *first_halves,
        ids_all,
    ) = pack_call(
        sizes,
        own_shape,
        project,
        1,
        6 * pack_rows * width_all * head_dim,
        gathered=hidden_in,
        resident=(cosine, sine, gain_query, gain_key),
        outs=(
            Out(width_all, slim),
            Out(lanes, wide),
            Out(head_dim, wide),
            Out(head_dim, wide),
            Out(head_dim, slim),
            Out(head_dim, slim),
            Out(head_dim, slim, flip=True),
            Out(head_dim, slim),
        ),
        swaps=(
            Swap(
                "fsdp",
                (width_all, 3 * head_dim),
                [
                    (
                        w,
                        lambda ref: ref.at[:, head_window()],
                        lambda buf, place, i=i: buf.at[
                            part_of(place, part_width), pl.ds(i * head_dim, head_dim)
                        ],
                    )
                    for i, w in enumerate((w_query, w_key, w_value))
                ],
                True,
            ),
            Swap(
                "fsdp",
                (head_dim, width_all),
                [
                    (
                        w_out,
                        lambda ref: ref.at[head_window(), :],
                        lambda buf, place: buf.at[:, part_of(place, part_width)],
                    )
                ],
                True,
            ),
            Swap(
                "tp",
                (1, width_all),
                [
                    (
                        attn_norm[None, :],
                        whole,
                        lambda buf, place: buf.at[:, part_of(place, col_count)],
                    )
                ],
                False,
            ),
            Swap(
                "fsdp",
                (expert_count, width_all),
                [(w_router, whole, lambda buf, place: buf.at[:, part_of(place, part_width)])],
                True,
            ),
        ),
        ships=expert_ships[:first_ships]
        + [Ship("ctx", expert_ids.T, lambda ref, shift: ref, (top_count, tok_rows))],
        lag=3,
    )
    router_pad = jnp.pad(router_full, ((0, lanes - expert_count), (0, 0)))

    def attend(rows, window, held, totals):
        query, key_t, value, seg_rows, seg_cols = held
        scores = nn_dot(query[window, :], key_t[...]) * score_scale
        same_seq = seg_rows[window, :][:, :1] == seg_cols[0:1, :]
        scores = jnp.where(same_seq, scores, -1e30)
        row_peak = jnp.max(scores, axis=1, keepdims=True)
        row_exp = jnp.exp(scores - row_peak)
        row_sum = jnp.sum(row_exp, axis=1, keepdims=True)
        probs_low = (row_exp * (1.0 / row_sum)).astype(slim)
        log_total = jnp.broadcast_to(row_peak + jnp.log(row_sum), (scores.shape[0], lanes))
        return own_queries(window, nn_dot(probs_low, value[...])), log_total.T[:8, :]

    attended_low, log_total, cotangent_all, *second_halves = pack_call(
        sizes,
        own_shape,
        attend,
        2,
        4 * pack_rows * pack_rows * head_dim,
        gathered=cotangent,
        resident=(query_low, key_flip, value_low, segment_rows, segment_cols),
        outs=(Out(head_dim, slim), Out(8, wide, flip=True)),
        keep=True,
        ships=expert_ships[first_ships:second_ships],
    )
    attn_branch, *third_halves = pack_call(
        sizes,
        own_shape,
        lambda window, held, totals: (nn_dot(held[0][window, :], held[1][...]), ()),
        3,
        2 * pack_rows * width_all * head_dim,
        resident=(attended_low, out_weight),
        ships=expert_ships[second_ships:],
    )
    far_halves = first_halves + second_halves + third_halves
    gate_weight, up_weight, down_weight = (
        expert_weight(w, far_halves[i * len(halves) : (i + 1) * len(halves)])
        for i, w in enumerate((w_gate, w_up, w_down))
    )

    resid_in = hidden_in.astype(wide)
    middle = resid_in + attn_branch
    gain_second = ffn_norm.astype(wide)
    inv_second = lax.rsqrt(row_total(jnp.sum(middle * middle, axis=1)) / width_all + norm_eps)[
        :, None
    ]

    def experts(rows, window, held, totals):
        gate_w, up_w, down_w, router_w, ids_ref, cotangent_ref = held
        lane = lax.broadcasted_iota(jnp.int32, (rows.shape[0], lanes), 1)
        logits = jnp.where(lane < expert_count, nt_dot(rows, router_w[...]), -1e30)
        logit_exp = jnp.exp(logits - jnp.max(logits, axis=1, keepdims=True))
        route_probs = logit_exp / jnp.sum(logit_exp, axis=1, keepdims=True)
        block = window.start // tok_rows
        within = pl.multiple_of(window.start - block * tok_rows, rows.shape[0])
        ids = ids_ref[block, :, pl.ds(within, rows.shape[0])].T
        chosen = jnp.zeros((rows.shape[0], lanes), wide)
        for pick in range(ids.shape[1]):
            chosen = chosen + (ids[:, pick : pick + 1] == lane).astype(wide)
        gate_weights = route_probs * chosen
        first_expert = lax.axis_index("ctx") * own_experts
        rows_grad = cotangent_ref[window, :]
        grad_logits = jnp.zeros((rows.shape[0], lanes), wide)
        mixed_list, gate_list, up_list = [], [], []
        for slot in range(own_experts):
            mine = (lane == first_expert + slot).astype(wide)
            gates = jnp.sum(gate_weights * mine, axis=1, keepdims=True)
            gate_proj = nn_dot(rows, gate_w[slot])
            up_proj = nn_dot(rows, up_w[slot])
            grad_mixed = nn_dot(rows_grad, down_w[slot]).astype(slim).astype(wide)
            gate_sigmoid = jax.nn.sigmoid(gate_proj)
            silu = gate_proj * gate_sigmoid
            activity = silu * up_proj
            mixed_list.append((gates * activity).astype(slim))
            grad_gates = jnp.sum(grad_mixed * activity, axis=1, keepdims=True)
            grad_activity = grad_mixed * gates
            gate_list.append(
                (
                    grad_activity * up_proj * (gate_sigmoid + silu * (1.0 - gate_sigmoid))
                ).astype(slim)
            )
            up_list.append((grad_activity * silu).astype(slim))
            grad_logits = grad_logits + gates * grad_gates * (mine - route_probs)
        return (
            jnp.concatenate(mixed_list, axis=1),
            jnp.concatenate(gate_list, axis=1),
            jnp.concatenate(up_list, axis=1),
            grad_logits,
        )

    mixed_low, grad_gate_low, grad_up_low, grad_logits_low, normed_second = pack_call(
        sizes,
        own_shape,
        experts,
        4,
        6 * pack_rows * width_all * own_units,
        gathered=(middle * inv_second * gain_second).astype(slim),
        resident=(gate_weight, up_weight, down_weight, router_pad, ids_all, cotangent_all),
        outs=(
            Out(own_units, slim),
            Out(own_units, slim),
            Out(own_units, slim),
            Out(lanes, slim),
        ),
        keep=True,
    )

    def back(window, held, totals):
        gate_grad, up_grad, logit_grad, gate_w, up_w, router_w, _ = held
        total = nn_dot(logit_grad[window, :], router_w[...])
        for slot in range(own_experts):
            total = total + nt_dot(units_of(gate_grad, window, slot), gate_w[slot])
            total = total + nt_dot(units_of(up_grad, window, slot), up_w[slot])
        return total, ()

    def gate_tile(window, held):
        features = held[6][:, window]
        return jnp.concatenate(
            [tn_dot(features, held[0][...]), tn_dot(features, held[2][...])], axis=1
        )

    grad_second, gate_own, gate_far = pack_call(
        sizes,
        own_shape,
        back,
        5,
        6 * pack_rows * width_all * own_units,
        resident=(
            grad_gate_low,
            grad_up_low,
            grad_logits_low,
            gate_weight,
            up_weight,
            router_pad,
            normed_second,
        ),
        makes=(Make(own_units + lanes, width_all, gate_tile, True),),
    )

    def by_expert(blocks):
        count, rows = blocks.shape[:2]
        return (
            jnp.swapaxes(blocks.reshape(count, rows, own_experts, hidden_units), 1, 2)
            .reshape(expert_count, rows, hidden_units)
            .astype(wide)
        )

    def by_head(blocks):
        rows = blocks.shape[1]
        summed = jnp.sum(
            blocks.reshape(sharers, local_heads, rows, head_dim).astype(wide), axis=0
        )
        return jnp.swapaxes(summed, 0, 1).reshape(rows, local_heads * head_dim)

    gain_two_grad = jnp.sum(grad_second * middle * inv_second, axis=0)
    second_scaled = grad_second * gain_second
    second_inner = row_total(jnp.sum(second_scaled * middle, axis=1))[:, None]
    grad_middle = (
        cotangent.astype(wide)
        + inv_second * second_scaled
        - middle * inv_second**3 * second_inner / width_all
    )

    (
        grad_attended,
        grad_middle_all,
        up_own,
        up_far,
        down_own,
        down_away,
        gate_blocks,
    ) = pack_call(
        sizes,
        own_shape,
        lambda rows, window, held, totals: (own_queries(window, nt_dot(rows, held[0][...])),),
        6,
        2 * pack_rows * width_all * (head_dim + own_units),
        gathered=grad_middle.astype(slim),
        resident=(out_weight, normed_second, grad_up_low, cotangent_all, mixed_low),
        outs=(Out(head_dim, slim),),
        keep=True,
        makes=(
            Make(
                own_units,
                width_all,
                lambda window, held: tn_dot(held[1][:, window], held[2][...]),
                True,
            ),
            Make(
                own_units,
                width_all,
                lambda window, held: tn_dot(held[3][:, window], held[4][...]),
                False,
            ),
        ),
        deals=(Deal(gate_own, gate_far),),
    )
    grad_gate = by_expert(gate_blocks[:, :, :own_units])
    grad_router = row_total(
        jnp.sum(gate_blocks[:, :, own_units : own_units + expert_count].astype(wide), axis=0).T
    )


    def attend_back(window, held, totals):
        mixed_ref, down_w, query, key, key_t, value, grad_att = held[:7]
        seg_rows, seg_cols, log_ref = held[7:10]
        grad_query_rot, grad_key_rot, grad_value, _ = totals
        query_chunk, grad_chunk = query[window, :], grad_att[window, :]
        scores = nt_dot(key[...], query_chunk) * score_scale
        key_segments = jnp.concatenate([seg_rows[...]] * (tok_rows // lanes), axis=1)
        same_seq = key_segments == seg_cols[0:1, window]
        probs = jnp.exp(jnp.where(same_seq, scores, -1e30) - log_ref[0:1, window])
        grad_probs = nt_dot(value[...], grad_chunk)
        inner = jnp.sum(probs * grad_probs, axis=0, keepdims=True)
        grad_scores = (probs * (grad_probs - inner)).astype(slim)
        grad_value[...] += nn_dot(probs.astype(slim), grad_chunk)
        grad_key_rot[...] += nn_dot(grad_scores, query_chunk)
        grad_query_rot[window, :] = nn_dot(key_t[...], grad_scores).T
        total = sum(
            nt_dot(units_of(mixed_ref, window, slot), down_w[slot]) for slot in range(own_experts)
        )
        return total, ()

    def unturn_all(held, stage, totals, chunk):
        raws, cos_table, sin_table, gains = held[10:12], held[12], held[13], held[14:16]
        grad_rots, grad_value, gain_sums = totals[:2], totals[2], totals[3]

        def unturn(i):
            window = pl.ds(pl.multiple_of(i * chunk, chunk), chunk)
            cos_rows, sin_rows = cos_table[window, :], sin_table[window, :]
            for which in range(2):
                grad_rot = grad_rots[which][window, :] * score_scale
                raw = raws[which][window, :]
                inverse = lax.rsqrt(jnp.mean(raw * raw, axis=1, keepdims=True) + norm_eps)
                grad_normed = grad_rot * cos_rows + pltpu.roll(
                    grad_rot * sin_rows, head_dim // 2, 1
                )
                weighted = grad_normed * gains[which][...]
                grad_raw = inverse * weighted - raw * inverse**3 * jnp.mean(
                    weighted * raw, axis=1, keepdims=True
                )
                stage[0][window, pl.ds(which * head_dim, head_dim)] = grad_raw.astype(slim)
                gain_sums[pl.ds(which, 1), :] += jnp.sum(
                    grad_normed * raw * inverse, axis=0, keepdims=True
                )
            stage[0][window, pl.ds(2 * head_dim, head_dim)] = grad_value[window, :].astype(slim)

        loop(pack_rows // chunk, unturn)

    expert_branch, grad_qkv_low, _, _, _, gain_sums, down_far, up_blocks = pack_call(
        sizes,
        own_shape,
        attend_back,
        7,
        2 * pack_rows * width_all * own_units + 10 * pack_rows * pack_rows * head_dim,
        resident=(
            mixed_low,
            down_weight,
            query_low,
            key_low,
            key_flip,
            value_low,
            grad_attended,
            segment_rows,
            segment_cols,
            log_total,
            query_raw,
            key_raw,
            cosine,
            sine,
            gain_query,
            gain_key,
        ),
        outs=(Out(3 * head_dim, slim, late=True),),
        totals=(
            ((pack_rows, head_dim), wide),
            ((pack_rows, head_dim), wide),
            ((pack_rows, head_dim), wide),
            ((8, head_dim), wide),
        ),
        last=unturn_all,
        ships=(
            Ship(
                "fsdp",
                down_away,
                lambda ref, shift: ref.at[shift - 1],
                (part_width, own_units),
            ),
        ),
        deals=(Deal(up_own, up_far),),
    )
    hidden_out = (middle + expert_branch).astype(slim)
    grad_up = by_expert(up_blocks)

    def last_tile(window, held):
        return jnp.concatenate(
            [
                tn_dot(held[2][:, window], held[0][...]),
                tn_dot(held[3][:, window], held[4][...]),
            ],
            axis=1,
        )

    grad_first, last_blocks, down_blocks = pack_call(
        sizes,
        own_shape,
        lambda window, held, totals: (nt_dot(held[0][window, :], held[1][...]), ()),
        8,
        2 * pack_rows * width_all * 7 * head_dim,
        resident=(grad_qkv_low, qkv_weight, normed_first, grad_middle_all, attended_low),
        tiles=Tiles(4 * head_dim, width_all, last_tile),
        deals=(Deal(down_own, down_far),),
    )
    grad_down = by_expert(down_blocks)
    grad_query, grad_key, grad_value, grad_out = (
        by_head(last_blocks[:, :, i * head_dim : (i + 1) * head_dim]) for i in range(4)
    )
    grad_out = grad_out.T

    gain_first = attn_norm.astype(wide)
    inv_first = lax.dynamic_slice_in_dim(inv_all, ctx_place * tok_rows, tok_rows, 0)[:, :1]
    gain_one_grad = jnp.sum(grad_first * resid_in * inv_first, axis=0)
    first_scaled = grad_first * gain_first
    first_inner = row_total(jnp.sum(first_scaled * resid_in, axis=1))[:, None]
    grad_hidden = (
        grad_middle + inv_first * first_scaled - resid_in * inv_first**3 * first_inner / width_all
    )

    stream_part = jnp.stack(
        [
            jnp.sum(middle * middle),
            jnp.sum(attn_branch * attn_branch),
            jnp.sum(expert_branch * expert_branch),
        ]
    )
    gain_rows = col_count // lanes
    sums = small_sums(
        sizes,
        jnp.concatenate(
            [
                gain_one_grad.reshape(gain_rows, lanes),
                gain_two_grad.reshape(gain_rows, lanes),
                gain_sums,
                jnp.pad(stream_part[None, :], ((0, 7), (0, lanes - 3))),
            ],
            axis=0,
        ),
        9,
    )
    tp_sums = jnp.sum(sums[:, 2 * gain_rows :], axis=0)
    token_count = tok_rows * packs * ctx_size
    stream_rms = jnp.sqrt(tp_sums[8, :3] / (token_count * width_all))
    return (
        hidden_out,
        grad_hidden,
        sums[:, :gain_rows].reshape(width_all),
        sums[:, gain_rows : 2 * gain_rows].reshape(width_all),
        tp_sums[0],
        tp_sums[1],
        grad_query,
        grad_key,
        grad_value,
        grad_out,
        grad_router,
        grad_gate,
        grad_up,
        grad_down,
        stream_rms,
    )


def solution(mesh):
    return jax.shard_map(
        on_device,
        mesh=mesh,
        in_specs=(
            P(("fsdp", "ctx"), "tp"),
            P(("fsdp", "ctx"), "tp"),
            P("fsdp", None),
            P("fsdp", None),
            P(("fsdp", "ctx"), None),
            P("tp"),
            P("tp"),
            P(),
            P(),
            P("fsdp", "tp"),
            P("fsdp", "tp"),
            P("fsdp", "tp"),
            P("tp", "fsdp"),
            P(None, "fsdp"),
            P(None, "fsdp", "tp"),
            P(None, "fsdp", "tp"),
            P(None, "fsdp", "tp"),
        ),
        out_specs=(
            P(("fsdp", "ctx"), "tp"),
            P(("fsdp", "ctx"), "tp"),
            P(),
            P(),
            P(),
            P(),
            P(("fsdp", "ctx"), "tp"),
            P(("fsdp", "ctx"), "tp"),
            P(("fsdp", "ctx"), "tp"),
            P("tp", ("fsdp", "ctx")),
            P(None, ("fsdp", "ctx")),
            P(None, ("fsdp", "ctx"), "tp"),
            P(None, ("fsdp", "ctx"), "tp"),
            P(None, ("fsdp", "ctx"), "tp"),
            P(),
        ),
        check_vma=False,
    )
```

```python
import jax
import jax.numpy as jnp
from jax import lax
from jax.experimental import pallas as pl
from jax.experimental.pallas import tpu as pltpu
from jax.sharding import PartitionSpec as P

norm_eps = 1e-06
rope_base = 10000.0


def locate(pack_spots, lengths_row):
    seq_ends = jnp.cumsum(lengths_row)
    starts = seq_ends - lengths_row
    segment = jnp.sum((pack_spots[:, None] >= seq_ends[None, :]).astype(jnp.int32), axis=1)
    slot_ids = jnp.arange(lengths_row.shape[0], dtype=jnp.int32)
    seq_begin = jnp.sum(
        jnp.where(segment[:, None] == slot_ids[None, :], starts[None, :], 0), axis=1
    )
    return (segment, pack_spots - seq_begin)


def rope_tables(pack_spots, head_dim):
    half_dim = head_dim // 2
    inv_freq = rope_base ** (-(jnp.arange(half_dim, dtype=jnp.float32) * 2.0 / head_dim))
    angle_grid = pack_spots.astype(jnp.float32)[:, None] * inv_freq[None, :]
    cosine, sine = jnp.cos(angle_grid), jnp.sin(angle_grid)
    return jnp.concatenate([cosine, cosine], axis=1), jnp.concatenate([-sine, sine], axis=1)


def unrotate(grad_rot, cosine, sine):
    return grad_rot * cosine + jnp.roll(grad_rot * sine, grad_rot.shape[1] // 2, axis=1)


CHUNKS = 2
MESH_ID = pl.DeviceIdType.MESH
VMEM_LIMIT = 64 * 1000 * 1000


class Pack:
    def __init__(self, ctx_size, tp_size, rows, cols, packs=1):
        self.line = ctx_size // 2
        self.packs = packs
        self.tp_size, self.rows, self.cols = tp_size, rows, cols
        self.chunk = rows // CHUNKS
        self.steps = self.line * CHUNKS
        place = lax.axis_index("ctx")
        self.a, self.b = place // 2, place % 2
        self.t = lax.axis_index("tp")
        self.has_up, self.has_down = self.a < self.line - 1, self.a > 0

    def up(self):
        return {"ctx": (self.a + 1) * 2 + self.b}

    def down(self):
        return {"ctx": (self.a - 1) * 2 + self.b}

    def pair(self):
        return {"ctx": self.a * 2 + (1 - self.b)}

    def sibling(self, shift):
        return {"tp": self.t ^ shift}

    def ctx_peer(self, shift):
        return {"ctx": lax.axis_index("ctx") ^ shift}

    def other_pack(self, shift):
        return {"fsdp": lax.axis_index("fsdp") ^ shift}

    def meet(self, everyone):
        barrier = pltpu.get_barrier_semaphore()

        def greet(device):
            pl.semaphore_signal(barrier, inc=1, device_id=device, device_id_type=MESH_ID)

        if everyone:
            near = 2 * self.line - 1
            for shift in range(1, 2 * self.line):
                greet(self.ctx_peer(shift))
        else:
            near = 1 + jnp.where(self.has_up, 1, 0) + jnp.where(self.has_down, 1, 0)

            @pl.when(self.has_up)
            def _():
                greet(self.up())

            @pl.when(self.has_down)
            def _():
                greet(self.down())

            greet(self.pair())
        for shift in range(1, self.tp_size):
            greet(self.sibling(shift))
        for shift in range(1, self.packs):
            greet(self.other_pack(shift))
        pl.semaphore_wait(barrier, near + self.tp_size + self.packs - 2)

    def row0(self, block, k):
        return pl.multiple_of(block * self.rows + k * self.chunk, self.chunk)

    def region(self, ref, block, k, part):
        return ref.at[
            pl.ds(self.row0(block, k), self.chunk),
            pl.ds(pl.multiple_of(part * self.cols, self.cols), self.cols),
        ]


def pick(table, i):
    result = jnp.int32(table[-1])
    for at, value in enumerate(table[:-1]):
        result = jnp.where(i == at, value, result)
    return result


def remote(src, dst, send_sem, recv_sem, device):
    return pltpu.make_async_remote_copy(
        src_ref=src,
        dst_ref=dst,
        send_sem=send_sem,
        recv_sem=recv_sem,
        device_id=device,
        device_id_type=MESH_ID,
    )


def loop(count, body):
    lax.fori_loop(0, count, lambda i, carry: (body(i), carry)[1], 0)


def gather_scratch(ctx_size, tp_size, rows, cols, dtype):
    line, dma = ctx_size // 2, pltpu.SemaphoreType.DMA
    return [
        pltpu.VMEM((ctx_size * rows, tp_size * cols), dtype),
        dma((2 * line * CHUNKS,)),
        dma((2 * line * CHUNKS,)),
        dma((4 * line * (tp_size - 1) * CHUNKS,)),
        dma((ctx_size * CHUNKS,)),
        dma(((tp_size - 1) * ctx_size * CHUNKS,)),
        dma,
    ]


def gather_steps(pack, src, scratch, everyone, lag, begin, before, compute):
    buf, line_sems, pair_sems, tp_sems, own_sems, sib_sems, local_sem = scratch
    line, t, a, b = pack.line, pack.t, pack.a, pack.b
    ctx_size = 2 * line

    def part(block, k):
        return pack.region(buf, block, k, t)

    def line_copy(piece, block, k, down, dist):
        return remote(
            piece,
            part(block, k),
            line_sems.at[(down * line + dist) * CHUNKS + k],
            own_sems.at[block * CHUNKS + k],
            pack.down() if down else pack.up(),
        )

    def pair_copy(piece, block, k, slot):
        return remote(
            piece,
            part(block, k),
            pair_sems.at[slot * CHUNKS + k],
            own_sems.at[block * CHUNKS + k],
            pack.pair(),
        )

    def tp_copy(piece, block, k, slot, shift):
        return remote(
            piece,
            part(block, k),
            tp_sems.at[(slot * (pack.tp_size - 1) + shift - 1) * CHUNKS + k],
            sib_sems.at[((shift - 1) * ctx_size + block) * CHUNKS + k],
            pack.sibling(shift),
        )

    def send_tp(piece, block, k, slot):
        for shift in range(1, pack.tp_size):
            tp_copy(piece, block, k, slot, shift).start()

    def await_own(block, k):
        piece = part(block, k)
        pair_copy(piece, block, k, 0).wait_recv()

    pack.meet(everyone)
    mine = a * 2 + b
    own_copy = pltpu.make_async_copy(
        src,
        buf.at[
            pl.ds(pl.multiple_of(mine * pack.rows, pack.rows), pack.rows),
            pl.ds(pl.multiple_of(t * pack.cols, pack.cols), pack.cols),
        ],
        local_sem,
    )
    own_copy.start()
    for k in range(CHUNKS):
        piece = src.at[pl.ds(k * pack.chunk, pack.chunk), :]

        @pl.when(pack.has_up)
        def _():
            line_copy(piece, mine, k, 0, 0).start()

        @pl.when(pack.has_down)
        def _():
            line_copy(piece, mine, k, 1, 0).start()

        pair_copy(piece, mine, k, 0).start()
    for k in range(CHUNKS):
        send_tp(src.at[pl.ds(k * pack.chunk, pack.chunk), :], mine, k, 0)
    begin()
    own_copy.wait()

    def ways(dist):
        below, above = a - dist, a + dist
        return (
            (0, below, below >= 0, jnp.logical_and(below >= 0, pack.has_up)),
            (1, above, above < line, jnp.logical_and(above < line, pack.has_down)),
        )

    def from_line(dist, k):
        for down, node, there, onward in ways(dist):
            block = node * 2 + b

            @pl.when(there)
            def _():
                await_own(block, k)

            @pl.when(onward)
            def _():
                line_copy(part(block, k), block, k, down, dist).start()

            @pl.when(there)
            def _():
                pair_copy(part(block, k), block, k, down * line + dist).start()
                send_tp(part(block, k), block, k, down * line + dist)

    def from_pair(dist, k):
        for down, node, there, _ in ways(dist):
            block = node * 2 + (1 - b)
            if down:
                there = jnp.logical_and(there, dist > 0)

            @pl.when(there)
            def _():
                await_own(block, k)
                send_tp(part(block, k), block, k, (2 + down) * line + dist)

    def work(block, k, order):
        for shift in range(1, pack.tp_size):
            piece = pack.region(buf, block, k, t ^ shift)
            remote(
                piece,
                piece,
                tp_sems.at[0],
                sib_sems.at[((shift - 1) * ctx_size + block) * CHUNKS + k],
                pack.sibling(shift),
            ).wait_recv()
        compute(pack.row0(block, k), block * CHUNKS + k, order)

    def step(s):
        dist, k = s // CHUNKS, s % CHUNKS

        @pl.when(s == lag)
        def _():
            before()

        turn = s - lag

        def side(i):
            @pl.when(jnp.logical_and(i == 0, dist + 1 < line))
            def _():
                from_line(dist + 1, k)

            @pl.when(jnp.logical_and(i == 1, s < pack.steps))
            def _():
                from_pair(dist, k)

            late = turn - i
            node, late_k = a ^ (late // CHUNKS), late % CHUNKS

            @pl.when(jnp.logical_and(late >= 0, late < pack.steps))
            def _():
                order = jnp.where(
                    i == 0,
                    jnp.maximum(2 * turn - 1, 0),
                    jnp.minimum(2 * turn, 2 * pack.steps - 1),
                )
                work(node * 2 + jnp.where(i == 0, b, 1 - b), late_k, order)

        loop(2, side)

    loop(pack.steps + 1 + lag, step)

    def drain(s):
        dist, k = s // CHUNKS, s % CHUNKS
        piece = part(0, 0)
        for down, _, there, onward in ways(dist):

            @pl.when(jnp.logical_and(onward, dist < line - 1))
            def _():
                line_copy(piece, 0, k, down, dist).wait_send()

            if down:
                there = jnp.logical_and(there, dist > 0)

            @pl.when(there)
            def _():
                pair_copy(piece, 0, k, down * line + dist).wait_send()
                for shift in range(1, pack.tp_size):
                    tp_copy(piece, 0, k, down * line + dist, shift).wait_send()
                    tp_copy(piece, 0, k, (2 + down) * line + dist, shift).wait_send()

    loop(pack.steps, drain)


def scatter_scratch(ctx_size, tp_size, rows, cols):
    line, dma = ctx_size // 2, pltpu.SemaphoreType.DMA
    low = jnp.bfloat16
    return [
        pltpu.VMEM((ctx_size * rows, tp_size * cols), low),
        pltpu.VMEM(((tp_size - 1) * ctx_size * rows, cols), low),
        pltpu.VMEM((line * rows, cols), low),
        pltpu.VMEM((2 * line * rows, cols), low),
        dma(((tp_size - 1) * ctx_size * CHUNKS,)),
        dma((line * CHUNKS,)),
        dma((line * CHUNKS,)),
        dma(((tp_size - 1) * ctx_size * CHUNKS,)),
        dma((line * CHUNKS,)),
        dma((2 * line * CHUNKS,)),
    ]


def scatter_steps(pack, scratch, everyone, begin, before, compute, jobs, tail, finish):
    (full, sib_buf, pair_buf, line_buf, tp_send, pair_send, line_send, tp_recv, pair_recv, line_recv) = scratch
    line, t, a, b = pack.line, pack.t, pack.a, pack.b
    ctx_size = 2 * line
    wide, low = jnp.float32, jnp.bfloat16
    table = [
        sorted(range(line), key=lambda o, node=node: (-abs(o - node), o)) for node in range(line)
    ]

    def owner(i):
        result = jnp.int32(0)
        for node in range(line):
            for place in range(line):
                here = jnp.logical_and(a == node, i == place)
                result = jnp.where(here, table[node][place], result)
        return result

    def tp_copy(block, k, shift):
        return remote(
            pack.region(full, block, k, t ^ shift),
            sib_buf.at[
                pl.ds(pack.row0((shift - 1) * ctx_size + block, k), pack.chunk), :
            ],
            tp_send.at[((shift - 1) * ctx_size + block) * CHUNKS + k],
            tp_recv.at[((shift - 1) * ctx_size + block) * CHUNKS + k],
            pack.sibling(shift),
        )

    def pair_copy(node, k):
        return remote(
            pack.region(full, node * 2 + (1 - b), k, t),
            pair_buf.at[pl.ds(pack.row0(node, k), pack.chunk), :],
            pair_send.at[node * CHUNKS + k],
            pair_recv.at[node * CHUNKS + k],
            pack.pair(),
        )

    def line_copy(node, k, down):
        return remote(
            pack.region(full, node * 2 + b, k, t),
            line_buf.at[pl.ds(pack.row0(down * line + node, k), pack.chunk), :],
            line_send.at[node * CHUNKS + k],
            line_recv.at[(down * line + node) * CHUNKS + k],
            pack.down() if down else pack.up(),
        )

    def own_part(block, k):
        return full[
            pl.ds(pack.row0(block, k), pack.chunk),
            pl.ds(pl.multiple_of(t * pack.cols, pack.cols), pack.cols),
        ].astype(wide)

    def put_part(block, k, value):
        full[
            pl.ds(pack.row0(block, k), pack.chunk),
            pl.ds(pl.multiple_of(t * pack.cols, pack.cols), pack.cols),
        ] = value.astype(low)

    def landed(ref, block, k):
        return ref[pl.ds(pack.row0(block, k), pack.chunk), :].astype(wide)

    def fill(block):
        row0 = pl.multiple_of(block * pack.rows, pack.rows)
        full[pl.ds(row0, pack.rows), :] = compute(row0)
        for k in range(CHUNKS):
            for shift in range(1, pack.tp_size):
                tp_copy(block, k, shift).start()

    def join(block, k):
        total = own_part(block, k)
        for shift in range(1, pack.tp_size):
            tp_copy(block, k, shift).wait_recv()
            total = total + landed(sib_buf, (shift - 1) * ctx_size + block, k)
        put_part(block, k, total)

    pack.meet(everyone)
    begin()
    before()

    def step(s):
        @pl.when(s < pack.steps)
        def _():
            node, k = owner(s // CHUNKS), s % CHUNKS

            def side(i):
                @pl.when(k == 0)
                def _():
                    fill(node * 2 + jnp.where(i == 0, 1 - b, b))

                jobs(2 * s + i)

            loop(2, side)

        late = s - 1

        @pl.when(jnp.logical_and(late >= 0, late < pack.steps))
        def _():
            node, k = owner(late // CHUNKS), late % CHUNKS

            def side(i):
                join(node * 2 + jnp.where(i == 0, 1 - b, b), k)

                @pl.when(i == 0)
                def _():
                    pair_copy(node, k).start()

            loop(2, side)

        if tail is not None:
            turn = s - (pack.steps - 1)
            share = ctx_size * CHUNKS // 4

            @pl.when(jnp.logical_and(turn >= 0, turn < 4))
            def _():
                loop(share, lambda i: tail(turn * share + i))

        later = s - 4

        @pl.when(later >= 0)
        def _():
            node, k = owner(later // CHUNKS), later % CHUNKS
            pair_copy(node, k).wait_recv()
            put_part(
                node * 2 + b, k, own_part(node * 2 + b, k) + landed(pair_buf, node, k)
            )
            from_below = jnp.logical_and(pack.has_down, node >= a)
            from_above = jnp.logical_and(pack.has_up, node <= a)
            for down, there in ((0, from_below), (1, from_above)):

                @pl.when(there)
                def _():
                    line_copy(node, k, down).wait_recv()
                    put_part(
                        node * 2 + b,
                        k,
                        own_part(node * 2 + b, k) + landed(line_buf, down * line + node, k),
                    )

            @pl.when(node > a)
            def _():
                line_copy(node, k, 0).start()

            @pl.when(node < a)
            def _():
                line_copy(node, k, 1).start()

            @pl.when(node == a)
            def _():
                finish(k, own_part(node * 2 + b, k))

    loop(pack.steps + 4, step)

    def drain(s):
        node, k = s // CHUNKS, s % CHUNKS
        pair_copy(node, k).wait_send()
        for shift in range(1, pack.tp_size):
            tp_copy(node * 2, k, shift).wait_send()
            tp_copy(node * 2 + 1, k, shift).wait_send()

        @pl.when(node > a)
        def _():
            line_copy(node, k, 0).wait_send()

        @pl.when(node < a)
        def _():
            line_copy(node, k, 1).wait_send()

    loop(pack.steps, drain)


ANY = pl.BlockSpec(memory_space=pl.ANY)


def nn_dot(left, right):
    return lax.dot_general(
        left, right, (((1,), (0,)), ((), ())), preferred_element_type=jnp.float32
    )


def nt_dot(left, right):
    return lax.dot_general(
        left, right, (((1,), (1,)), ((), ())), preferred_element_type=jnp.float32
    )


def tn_dot(left, right):
    return lax.dot_general(
        left, right, (((0,), (0,)), ((), ())), preferred_element_type=jnp.float32
    )


class Out:
    def __init__(self, width, dtype, flip=False, late=False):
        self.width, self.dtype, self.flip, self.late = width, dtype, flip, late

    def shape(self, rows):
        return (self.width, rows) if self.flip else (rows, self.width)

    def window(self, ref, window):
        return ref.at[:, window] if self.flip else ref.at[window, :]


class Parts:
    def __init__(self, shape, pieces):
        self.shape, self.pieces = shape, pieces


class Swap:
    def __init__(self, axis, shape, pieces, keep):
        self.axis, self.shape, self.pieces, self.keep = axis, shape, pieces, keep


class Ship:
    def __init__(self, axis, array, source, shape):
        self.axis, self.array, self.source, self.shape = axis, array, source, shape


class Make:
    def __init__(self, width, features, tile, send):
        self.width, self.features, self.tile, self.send = width, features, tile, send


class Deal:
    def __init__(self, own, far, parts=1):
        self.own, self.far, self.parts = own, far, parts
        self.width = own.shape[1] // parts


class Tiles:
    def __init__(self, width, features, tile):
        self.width, self.features, self.tile = width, features, tile


def whole(ref):
    return ref


def pack_call(
    sizes,
    shape,
    piece,
    collective_id,
    flops,
    gathered=None,
    resident=(),
    outs=(),
    totals=(),
    last=None,
    keep=False,
    swaps=(),
    ships=(),
    tiles=None,
    makes=(),
    deals=(),
    lag=1,
):
    packs, ctx_size, tp_size = sizes
    rows, cols = shape
    all_rows, all_cols = ctx_size * rows, tp_size * cols
    pieces = ctx_size * CHUNKS
    dma = pltpu.SemaphoreType.DMA
    gather = gathered is not None
    if gather:
        base = gather_scratch(ctx_size, tp_size, rows, cols, gathered.dtype)
    else:
        base = scatter_scratch(ctx_size, tp_size, rows, cols)
    axis_size = {"fsdp": packs, "ctx": ctx_size, "tp": tp_size}
    inputs = []

    def enlist(array):
        for i, known in enumerate(inputs):
            if known is array:
                return i
        inputs.append(array)
        return len(inputs) - 1

    if gather:
        enlist(gathered)
    resident = list(resident)
    first_deal = len(resident)
    for deal in deals:
        resident += [deal.own, deal.far]
    parts = [
        r if isinstance(r, Parts) else Parts(r.shape, [(r, whole, whole)]) for r in resident
    ]
    part_list = [[(enlist(x), src, dst) for x, src, dst in p.pieces] for p in parts]
    swap_list = [[(enlist(x), src, dst) for x, src, dst in w.pieces] for w in swaps]
    ship_list = [enlist(ship.array) for ship in ships]
    swap_count = sum(len(w.pieces) * axis_size[w.axis] for w in swaps)
    ship_count = sum(axis_size[ship.axis] for ship in ships)
    kept_swaps = [i for i, w in enumerate(swaps) if w.keep]
    n_out = len(outs) + len(totals) + keep + len(kept_swaps) + len(ships)
    tile_rows = 128
    features = all_cols
    own_features = features // (packs * ctx_size)
    splits = tile_rows // own_features
    own_tiles = features // packs // tile_rows
    far_tiles = (packs - 1) * own_tiles
    assert own_tiles + far_tiles == pieces
    stride = pieces // own_tiles
    deal_order = (4, 1, 6, 2, 5, 3, 7, 0) if own_tiles == 8 else tuple(range(own_tiles))

    def kernel(*refs):
        refs = list(refs)

        def take(count):
            taken = refs[:count]
            del refs[:count]
            return taken

        given = take(len(inputs))
        sum_ref = None if gather else take(1)[0]
        out_refs = take(n_out)
        blocks_ref = None if tiles is None else take(1)[0]
        make_outs = [take(2) for _ in makes]
        deal_outs = take(len(deals))
        scratch = take(len(base))
        held = take(len(resident))
        stage = take(len(outs))
        total_refs = take(len(totals))
        swap_bufs = take(len(swaps))
        (held_sem, out_sem, late_sem, swap_local, swap_send, swap_recv, ship_send, ship_recv) = take(8)
        if tiles is not None:
            tile_stage, tile_far, tile_send, far_recv, block_recv = take(5)
        make_stages = take(len(makes))
        make_send, make_recv, deal_send, deal_recv = take(4)
        over_packs = swaps or ships or tiles is not None or any(make.send for make in makes)
        everyone = tiles is not None or deals or any(ship.axis == "ctx" for ship in ships)
        pack = Pack(ctx_size, tp_size, rows, cols, packs if over_packs else 1)
        mine = {axis: lax.axis_index(axis) for axis in axis_size}
        loads = []
        for target_ref, copies in zip(held, part_list):
            for which, source, target in copies:
                loads.append(
                    pltpu.make_async_copy(
                        source(given[which]), target(target_ref), held_sem.at[len(loads)]
                    )
                )
        swap_copies, swap_sends = [], []
        index = 0
        for swap, buf, copies in zip(swaps, swap_bufs, swap_list):
            for which, source, target in copies:
                here = source(given[which])
                there = target(buf, mine[swap.axis])
                swap_copies.append(pltpu.make_async_copy(here, there, swap_local.at[index]))
                for shift in range(1, axis_size[swap.axis]):
                    slot = index + shift
                    device = {swap.axis: mine[swap.axis] ^ shift}
                    theirs = target(buf, mine[swap.axis] ^ shift)
                    swap_sends.append(
                        (
                            remote(here, there, swap_send.at[slot], swap_recv.at[slot], device),
                            remote(theirs, theirs, swap_send.at[slot], swap_recv.at[slot], device),
                        )
                    )
                index += axis_size[swap.axis]
        late = []
        for i, where in enumerate(kept_swaps):
            late.append((swap_bufs[where], out_refs[len(outs) + len(totals) + keep + i]))
        late_copies = [
            pltpu.make_async_copy(here, there, late_sem.at[i])
            for i, (here, there) in enumerate(late)
        ]
        ship_local, ship_copies = [], []
        index = 0
        for ship, which, landing in zip(ships, ship_list, out_refs[n_out - len(ships) :]):
            place = mine[ship.axis]
            if ship.axis == "ctx":
                here = ship.source(given[which], 0)
                ship_local.append(
                    pltpu.make_async_copy(here, landing.at[place], ship_send.at[index])
                )
            for shift in range(1, axis_size[ship.axis]):
                here = ship.source(given[which], shift)
                there = landing.at[place] if ship.axis == "ctx" else landing.at[shift - 1]
                theirs = landing.at[place ^ shift] if ship.axis == "ctx" else there
                device = {ship.axis: place ^ shift}
                sems = ship_send.at[index + shift], ship_recv.at[index + shift]
                ship_copies.append(
                    (remote(here, there, *sems, device), remote(theirs, theirs, *sems, device))
                )
            index += axis_size[ship.axis]

        def begin():
            for copy in swap_copies + ship_local:
                copy.start()
            for send, _ in swap_sends + ship_copies:
                send.start()

        def before():
            for ref in total_refs:
                ref[...] = jnp.zeros_like(ref)
            for load in loads:
                load.wait()
            for copy in swap_copies:
                copy.wait()
            for send, receive in swap_sends:
                receive.wait_recv()
            for copy in late_copies:
                copy.start()

        def stores(row0, index):
            window = pl.ds(row0, pack.chunk)
            copies = []
            for i, out in enumerate(outs):
                if not out.late:
                    copies.append((out.window(stage[i], window), out.window(out_refs[i], window), i))
            if keep:
                i = len(outs)
                copies.append(
                    (scratch[0].at[window, :], out_refs[i + len(totals)].at[window, :], i)
                )
            return [
                pltpu.make_async_copy(here, there, out_sem.at[i * pieces + index])
                for here, there, i in copies
            ]

        def put(window, values):
            early = [i for i, out in enumerate(outs) if not out.late]
            for i, value in zip(early, values):
                out = outs[i]
                if out.flip:
                    stage[i][:, window] = value.astype(out.dtype)
                else:
                    stage[i][window, :] = value.astype(out.dtype)

        ahead = 3

        def is_far(order):
            if far_tiles != own_tiles:
                return order < far_tiles
            middle = jnp.logical_and(order >= ahead, order < pieces - ahead)
            return jnp.where(middle, (order - ahead) % 2 == 1, order < ahead)

        def rank(order):
            if far_tiles != own_tiles:
                return jnp.where(order < far_tiles, order, order - far_tiles)
            middle = (order - ahead) // 2
            return jnp.where(
                order < ahead,
                order,
                jnp.where(
                    order >= pieces - ahead,
                    order - far_tiles,
                    jnp.where(is_far(order), ahead + middle, middle),
                ),
            )

        def tile_copy(order, which, shift):
            return remote(
                tile_stage.at[order],
                tile_far.at[which],
                tile_send.at[order * splits],
                far_recv.at[which],
                {"fsdp": mine["fsdp"] ^ shift},
            )

        def block_copy(order, split, owner):
            return remote(
                tile_stage.at[order, pl.ds(split * own_features, own_features), :],
                blocks_ref.at[mine["ctx"]],
                tile_send.at[order * splits + split],
                block_recv.at[mine["ctx"]],
                {"ctx": owner},
            )

        def block_store(order, split):
            return pltpu.make_async_copy(
                tile_stage.at[order, pl.ds(split * own_features, own_features), :],
                blocks_ref.at[mine["ctx"]],
                tile_send.at[order * splits + split],
            )

        def each_block(order, go_away, stay):
            for split in range(splits):
                owner = ((mine["ctx"] // splits) ^ pick(deal_order, rank(order))) * splits + split

                @pl.when(owner != mine["ctx"])
                def _():
                    go_away(order, split, owner)

                @pl.when(owner == mine["ctx"])
                def _():
                    stay(order, split)

        def make_tile(order):
            if tiles is None:
                return
            far, which = is_far(order), rank(order)
            shift = jnp.where(far, which // own_tiles + 1, 0)
            place = (mine["ctx"] // splits) ^ pick(deal_order, which % own_tiles)
            first = ((mine["fsdp"] ^ shift) * own_tiles + place) * tile_rows
            value = tiles.tile(pl.ds(pl.multiple_of(first, tile_rows), tile_rows), held)

            @pl.when(far)
            def _():
                tile_stage[order] = value.astype(jnp.bfloat16)
                tile_copy(order, which, shift).start()

            @pl.when(jnp.logical_not(far))
            def _():
                total = value
                for other in range(packs - 1):
                    slot = other * own_tiles + which
                    tile_copy(order, slot, 1).wait_recv()
                    total = total + tile_far[slot].astype(jnp.float32)
                tile_stage[order] = total.astype(jnp.bfloat16)
                each_block(
                    order,
                    lambda *where: block_copy(*where).start(),
                    lambda *where: block_store(*where).start(),
                )

        def finish_tiles():
            if tiles is None:
                return

            def sent(order):
                @pl.when(is_far(order))
                def _():
                    tile_copy(order, 0, 1).wait_send()

                @pl.when(jnp.logical_not(is_far(order)))
                def _():
                    each_block(
                        order,
                        lambda *where: block_copy(*where).wait_send(),
                        lambda *where: block_store(*where).wait(),
                    )

            loop(pieces, sent)
            for shift in range(1, ctx_size):
                landed = blocks_ref.at[mine["ctx"] ^ shift]
                remote(
                    landed,
                    landed,
                    tile_send.at[0],
                    block_recv.at[mine["ctx"] ^ shift],
                    {"ctx": mine["ctx"] ^ shift},
                ).wait_recv()

        def make_copies(i, order):
            far = order < far_tiles
            which = jnp.where(far, order, order - far_tiles)
            shift = jnp.where(far, which // own_tiles + 1, 0)
            window = pl.ds(
                pl.multiple_of(which % own_tiles * tile_rows, tile_rows), tile_rows
            )
            here = make_stages[i].at[order]
            sem = make_send.at[i * pieces + order]
            own_out, far_out = make_outs[i]
            slot = jnp.maximum(shift - 1, 0)
            send = remote(
                here,
                far_out.at[slot, window, :],
                sem,
                make_recv.at[i * pieces + order],
                {"fsdp": mine["fsdp"] ^ shift},
            )
            away = pltpu.make_async_copy(here, far_out.at[slot, window, :], sem)
            stay = pltpu.make_async_copy(here, own_out.at[window, :], sem)
            return far, shift, which % own_tiles, send, away, stay

        def make_parts(order):
            for i, make in enumerate(makes):
                far, shift, place, send, away, stay = make_copies(i, order)
                first = ((mine["fsdp"] ^ shift) * own_tiles + place) * tile_rows
                value = make.tile(pl.ds(pl.multiple_of(first, tile_rows), tile_rows), held)
                make_stages[i][order] = value.astype(jnp.bfloat16)

                @pl.when(far)
                def _():
                    (send if make.send else away).start()

                @pl.when(jnp.logical_not(far))
                def _():
                    stay.start()

        def finish_parts():
            def sent(order):
                for i, make in enumerate(makes):
                    far, _, _, send, away, stay = make_copies(i, order)

                    @pl.when(far)
                    def _():
                        if make.send:
                            send.wait_send()
                            send.wait_recv()
                        else:
                            away.wait()

                    @pl.when(jnp.logical_not(far))
                    def _():
                        stay.wait()

            loop(pieces, sent)

        deal_first = [sum(d.parts for d in deals[:i]) for i in range(len(deals))]

        def deal_blocks(i, turn, go_away, stay):
            own_buf, landing = held[first_deal + 2 * i], deal_outs[i]
            parts, width = deals[i].parts, deals[i].width
            for split in range(splits):
                owner = ((mine["ctx"] // splits) ^ pick(deal_order, turn)) * splits + split
                window = pl.ds(pl.multiple_of(owner * own_features, own_features), own_features)
                copies = []
                for part in range(parts):
                    here = own_buf.at[window, pl.ds(part * width, width)]
                    there = landing.at[mine["ctx"] * parts + part]
                    sem = deal_send.at[
                        (deal_first[i] + part) * own_tiles * splits + turn * splits + split
                    ]
                    arrived = deal_recv.at[(deal_first[i] + part) * ctx_size + mine["ctx"]]
                    copies.append((here, there, sem, arrived))

                @pl.when(owner != mine["ctx"])
                def _():
                    for copy in copies:
                        go_away(remote(*copy, {"ctx": owner}))

                @pl.when(owner == mine["ctx"])
                def _():
                    for here, there, sem, _ in copies:
                        stay(pltpu.make_async_copy(here, there, sem))

        def deal_out(order):
            if not deals:
                return

            @pl.when(order % stride == 0)
            def _():
                turn = order // stride
                place = (mine["ctx"] // splits) ^ pick(deal_order, turn)
                window = pl.ds(pl.multiple_of(place * tile_rows, tile_rows), tile_rows)
                for i in range(len(deals)):
                    own_buf, far_buf = held[first_deal + 2 * i], held[first_deal + 2 * i + 1]
                    total = own_buf[window, :].astype(jnp.float32)
                    for other in range(packs - 1):
                        total = total + far_buf[other, window, :].astype(jnp.float32)
                    own_buf[window, :] = total.astype(jnp.bfloat16)
                    deal_blocks(i, turn, lambda copy: copy.start(), lambda copy: copy.start())

        def finish_deals():
            if not deals:
                return

            def sent(turn):
                for i in range(len(deals)):
                    deal_blocks(i, turn, lambda copy: copy.wait_send(), lambda copy: copy.wait())

            loop(own_tiles, sent)
            for i in range(len(deals)):
                for shift in range(1, ctx_size):
                    place = mine["ctx"] ^ shift
                    for part in range(deals[i].parts):
                        landed = deal_outs[i].at[place * deals[i].parts + part]
                        sem = deal_recv.at[(deal_first[i] + part) * ctx_size + place]
                        remote(landed, landed, deal_send.at[0], sem, {"ctx": place}).wait_recv()

        for load in loads:
            load.start()
        if gather:

            def compute(row0, index, order):
                window = pl.ds(row0, pack.chunk)
                put(window, piece(scratch[0][window, :], window, held + swap_bufs, total_refs))
                for store in stores(row0, index):
                    store.start()
                deal_out(order)
                make_tile(order)
                make_parts(order)

            gather_steps(pack, given[0], scratch, everyone, lag, begin, before, compute)
        else:

            def compute(row0):
                window = pl.ds(row0, pack.rows)
                rows_value, values = piece(window, held + swap_bufs, total_refs)
                put(window, values)
                return rows_value.astype(jnp.bfloat16)

            def jobs(order):
                deal_out(order)
                make_tile(order)
                make_parts(order)

            def finish(k, total):
                sum_ref[pl.ds(pl.multiple_of(k * pack.chunk, pack.chunk), pack.chunk), :] = total

            def tail(i):
                last(
                    pl.ds(pl.multiple_of(i * pack.chunk, pack.chunk), pack.chunk),
                    held + swap_bufs,
                    stage,
                    total_refs,
                )

            scatter_steps(
                pack, scratch, everyone, begin, before, compute, jobs,
                None if last is None else tail, finish,
            )
        ends = []
        for i, out in enumerate(outs):
            if out.late:
                ends.append((stage[i], out_refs[i]))
        for i, ref in enumerate(total_refs):
            ends.append((ref, out_refs[len(outs) + i]))
        end_copies = [
            pltpu.make_async_copy(here, there, late_sem.at[len(late) + i])
            for i, (here, there) in enumerate(ends)
        ]
        for copy in end_copies:
            copy.start()

        def drain(index):
            for store in stores(pl.multiple_of(index * pack.chunk, pack.chunk), index):
                store.wait()

        loop(pieces, drain)
        finish_tiles()
        finish_parts()
        finish_deals()
        for copy in late_copies + end_copies + ship_local:
            copy.wait()
        for send, _ in swap_sends:
            send.wait_send()
        for send, receive in ship_copies:
            send.wait_send()
            receive.wait_recv()

    low = jnp.bfloat16
    shapes = [jax.ShapeDtypeStruct(out.shape(all_rows), out.dtype) for out in outs]
    shapes += [jax.ShapeDtypeStruct(dims, dtype) for dims, dtype in totals]
    if keep:
        shapes.append(jax.ShapeDtypeStruct((all_rows, all_cols), gathered.dtype))
    shapes += [jax.ShapeDtypeStruct(swaps[i].shape, low) for i in kept_swaps]
    for ship in ships:
        slots = ctx_size if ship.axis == "ctx" else packs - 1
        shapes.append(jax.ShapeDtypeStruct((slots,) + ship.shape, ship.array.dtype))
    if tiles is not None:
        shapes.append(jax.ShapeDtypeStruct((ctx_size, own_features, tiles.width), low))
    part_features = features // packs
    for make in makes:
        shapes.append(jax.ShapeDtypeStruct((part_features, make.width), low))
        shapes.append(jax.ShapeDtypeStruct((packs - 1, part_features, make.width), low))
    for deal in deals:
        shapes.append(
            jax.ShapeDtypeStruct((ctx_size * deal.parts, own_features, deal.width), low)
        )
    out_specs = [ANY] * len(shapes)
    if not gather:
        shapes = [jax.ShapeDtypeStruct(shape, jnp.float32)] + shapes
        out_specs = [pl.BlockSpec(memory_space=pltpu.VMEM)] + out_specs
    tile_scratch = []
    if tiles is not None:
        tile_scratch = [
            pltpu.VMEM((pieces, tile_rows, tiles.width), low),
            pltpu.VMEM((far_tiles, tile_rows, tiles.width), low),
            dma((pieces * splits,)),
            dma((far_tiles,)),
            dma((ctx_size,)),
        ]
    return pl.pallas_call(
        kernel,
        out_shape=tuple(shapes),
        in_specs=[ANY] * len(inputs),
        out_specs=tuple(out_specs),
        scratch_shapes=base
        + [pltpu.VMEM(p.shape, p.pieces[0][0].dtype) for p in parts]
        + [pltpu.VMEM(out.shape(all_rows), out.dtype) for out in outs]
        + [pltpu.VMEM(dims, dtype) for dims, dtype in totals]
        + [pltpu.VMEM(swap.shape, low) for swap in swaps]
        + [
            dma((max(1, sum(len(p.pieces) for p in parts)),)),
            dma(((len(outs) + 1) * pieces,)),
            dma((len(kept_swaps) + len(outs) + len(totals) + 1,)),
            dma((max(1, swap_count),)),
            dma((max(1, swap_count),)),
            dma((max(1, swap_count),)),
            dma((max(1, ship_count),)),
            dma((max(1, ship_count),)),
        ]
        + tile_scratch
        + [pltpu.VMEM((pieces, tile_rows, make.width), low) for make in makes]
        + [
            dma((max(1, len(makes)) * pieces,)),
            dma((max(1, len(makes)) * pieces,)),
            dma((max(1, sum(deal.parts for deal in deals)) * own_tiles * splits,)),
            dma((max(1, sum(deal.parts for deal in deals)) * ctx_size,)),
        ],
        compiler_params=pltpu.CompilerParams(
            collective_id=collective_id, has_side_effects=True, vmem_limit_bytes=VMEM_LIMIT
        ),
        cost_estimate=pl.CostEstimate(
            flops=flops, bytes_accessed=8 * all_rows * all_cols, transcendentals=0
        ),
    )(*inputs)


def small_sums(sizes, tensor, collective_id):
    packs, ctx_size, tp_size = sizes
    dma = pltpu.SemaphoreType.DMA
    count = tensor.shape[0]

    def kernel(src, out_ref, ctx_buf, mid, rest_buf, send_sems, recv_sems):
        f, c, t = (lax.axis_index(axis) for axis in ("fsdp", "ctx", "tp"))
        ctx_peers = [(shift, {"ctx": c ^ shift}) for shift in range(1, ctx_size)]
        rest_peers = [
            (shift * tp_size + turn, {"fsdp": f ^ shift, "tp": t ^ turn})
            for shift in range(packs)
            for turn in range(tp_size)
            if shift or turn
        ]
        barrier = pltpu.get_barrier_semaphore()
        for _, device in ctx_peers + rest_peers:
            pl.semaphore_signal(barrier, inc=1, device_id=device, device_id_type=MESH_ID)
        pl.semaphore_wait(barrier, len(ctx_peers) + len(rest_peers))

        def exchange(source, buf, peers, offset):
            copies = [
                remote(
                    source,
                    buf.at[slot],
                    send_sems.at[offset + slot],
                    recv_sems.at[offset + slot],
                    device,
                )
                for slot, device in peers
            ]
            for copy in copies:
                copy.start()
            for copy in copies:
                copy.wait()

        exchange(src, ctx_buf, ctx_peers, 0)
        total = src[...]
        for slot, _ in ctx_peers:
            total = total + ctx_buf[slot]
        mid[...] = total
        exchange(mid, rest_buf, rest_peers, ctx_size)
        rest_buf[0] = total
        for turn in range(tp_size):
            part = rest_buf[turn]
            for shift in range(1, packs):
                part = part + rest_buf[shift * tp_size + turn]
            out_ref[t ^ turn] = part

    return pl.pallas_call(
        kernel,
        out_shape=jax.ShapeDtypeStruct((tp_size, count, tensor.shape[1]), jnp.float32),
        in_specs=[pl.BlockSpec(memory_space=pltpu.VMEM)],
        out_specs=pl.BlockSpec(memory_space=pltpu.VMEM),
        scratch_shapes=[
            pltpu.VMEM((ctx_size,) + tensor.shape, jnp.float32),
            pltpu.VMEM(tensor.shape, jnp.float32),
            pltpu.VMEM((packs * tp_size,) + tensor.shape, jnp.float32),
            dma((ctx_size + packs * tp_size,)),
            dma((ctx_size + packs * tp_size,)),
        ],
        compiler_params=pltpu.CompilerParams(collective_id=collective_id, has_side_effects=True),
    )(tensor)

def on_device(
    hidden_in,
    cotangent,
    positions,
    seq_lengths,
    expert_ids,
    attn_norm,
    ffn_norm,
    query_norm,
    key_norm,
    w_query,
    w_key,
    w_value,
    w_out,
    w_router,
    w_gate,
    w_up,
    w_down,
):
    tok_rows, col_count = hidden_in.shape
    packs, ctx_size, tp_size = (lax.axis_size(axis) for axis in ("fsdp", "ctx", "tp"))
    sizes = (packs, ctx_size, tp_size)
    own_shape = (tok_rows, col_count)
    ctx_place = lax.axis_index("ctx")
    width_all = col_count * tp_size
    part_width = width_all // packs
    pack_rows = tok_rows * ctx_size
    head_dim = query_norm.shape[0]
    local_heads = w_query.shape[1] // head_dim
    expert_count, hidden_units = w_gate.shape[0], w_gate.shape[2]
    own_experts = expert_count // ctx_size
    own_units = own_experts * hidden_units
    top_count = expert_ids.shape[1]
    sharers = ctx_size // local_heads
    score_scale = head_dim ** (-0.5)
    wide = jnp.float32
    slim = jnp.bfloat16
    lanes = 128

    def row_total(tensor):
        return lax.psum(tensor, "tp")

    def units_of(ref, window, slot):
        return ref[window, pl.ds(slot * hidden_units, hidden_units)]

    def own_queries(window, value):
        if sharers == 1:
            return value
        share = window.start // (pack_rows // sharers)
        return jnp.where(share == lax.axis_index("ctx") // local_heads, value, 0.0)

    def head_window():
        return pl.ds(
            pl.multiple_of(lax.axis_index("ctx") % local_heads * head_dim, head_dim), head_dim
        )

    def part_of(place, size):
        return pl.ds(pl.multiple_of(place * size, size), size)

    half_rows = part_width // 2

    def half_ship(weight, slot, half):
        return Ship(
            "fsdp",
            weight,
            lambda ref, shift: ref.at[
                lax.axis_index("ctx") * own_experts + slot,
                pl.ds(half * half_rows, half_rows),
                :,
            ],
            (half_rows, hidden_units),
        )

    halves = [(slot, half) for slot in range(own_experts) for half in range(2)]
    expert_ships = [half_ship(w, *which) for w in (w_gate, w_up, w_down) for which in halves]
    first_ships = len(expert_ships) // 4
    second_ships = first_ships + (len(expert_ships) - first_ships) // 2

    def expert_weight(weight, far):
        pieces = [
            (
                weight,
                lambda ref: ref.at[pl.ds(lax.axis_index("ctx") * own_experts, own_experts), :, :],
                lambda buf: buf.at[:, part_of(lax.axis_index("fsdp"), part_width), :],
            )
        ]
        for (slot, half), array in zip(halves, far):
            for shift in range(1, packs):
                pieces.append(
                    (
                        array,
                        lambda ref, shift=shift: ref.at[shift - 1],
                        lambda buf, slot=slot, half=half, shift=shift: buf.at[
                            slot,
                            part_of((lax.axis_index("fsdp") ^ shift) * 2 + half, half_rows),
                            :,
                        ],
                    )
                )
        return Parts((own_experts, width_all, hidden_units), pieces)

    segment, place = locate(positions[0], seq_lengths[0])
    cosine, sine = rope_tables(place, head_dim)
    segment_rows = jnp.broadcast_to(segment[:, None], (pack_rows, lanes))
    segment_cols = jnp.broadcast_to(segment[None, :], (8, pack_rows))

    def project(rows, window, held, totals):
        cos_table, sin_table, gain_q, gain_k, weight, _, gain, _ = held
        hidden = rows.astype(wide)
        inverse = lax.rsqrt(jnp.mean(hidden * hidden, axis=1, keepdims=True) + norm_eps)
        normed = (hidden * inverse * gain[...].astype(wide)).astype(slim)
        raw = nn_dot(normed, weight[...])
        cos_rows, sin_rows = cos_table[window, :], sin_table[window, :]

        def prepare(raw_proj, gain_vec):
            inv = lax.rsqrt(jnp.mean(raw_proj * raw_proj, axis=1, keepdims=True) + norm_eps)
            scaled = raw_proj * inv * gain_vec[...]
            return scaled * cos_rows + pltpu.roll(scaled, head_dim // 2, 1) * sin_rows

        query_raw = raw[:, :head_dim]
        key_raw = raw[:, head_dim : 2 * head_dim]
        key_turned = prepare(key_raw, gain_k)
        return (
            normed,
            jnp.broadcast_to(inverse, (rows.shape[0], lanes)),
            query_raw,
            key_raw,
            prepare(query_raw, gain_q),
            key_turned,
            key_turned.T,
            raw[:, 2 * head_dim :],
        )

    gain_query = query_norm.astype(wide)[None, :]
    gain_key = key_norm.astype(wide)[None, :]
    (
        normed_first,
        inv_all,
        query_raw,
        key_raw,
        query_low,
        key_low,
        key_flip,
        value_low,
        qkv_weight,
        out_weight,
        router_full,
        *first_halves,
        ids_all,
    ) = pack_call(
        sizes,
        own_shape,
        project,
        1,
        6 * pack_rows * width_all * head_dim,
        gathered=hidden_in,
        resident=(cosine, sine, gain_query, gain_key),
        outs=(
            Out(width_all, slim),
            Out(lanes, wide),
            Out(head_dim, wide),
            Out(head_dim, wide),
            Out(head_dim, slim),
            Out(head_dim, slim),
            Out(head_dim, slim, flip=True),
            Out(head_dim, slim),
        ),
        swaps=(
            Swap(
                "fsdp",
                (width_all, 3 * head_dim),
                [
                    (
                        w,
                        lambda ref: ref.at[:, head_window()],
                        lambda buf, place, i=i: buf.at[
                            part_of(place, part_width), pl.ds(i * head_dim, head_dim)
                        ],
                    )
                    for i, w in enumerate((w_query, w_key, w_value))
                ],
                True,
            ),
            Swap(
                "fsdp",
                (head_dim, width_all),
                [
                    (
                        w_out,
                        lambda ref: ref.at[head_window(), :],
                        lambda buf, place: buf.at[:, part_of(place, part_width)],
                    )
                ],
                True,
            ),
            Swap(
                "tp",
                (1, width_all),
                [
                    (
                        attn_norm[None, :],
                        whole,
                        lambda buf, place: buf.at[:, part_of(place, col_count)],
                    )
                ],
                False,
            ),
            Swap(
                "fsdp",
                (expert_count, width_all),
                [(w_router, whole, lambda buf, place: buf.at[:, part_of(place, part_width)])],
                True,
            ),
        ),
        ships=expert_ships[:first_ships]
        + [Ship("ctx", expert_ids.T, lambda ref, shift: ref, (top_count, tok_rows))],
        lag=3,
    )
    router_pad = jnp.pad(router_full, ((0, lanes - expert_count), (0, 0)))

    def attend(rows, window, held, totals):
        query, key_t, value, seg_rows, seg_cols = held
        scores = nn_dot(query[window, :], key_t[...]) * score_scale
        same_seq = seg_rows[window, :][:, :1] == seg_cols[0:1, :]
        scores = jnp.where(same_seq, scores, -1e30)
        row_peak = jnp.max(scores, axis=1, keepdims=True)
        row_exp = jnp.exp(scores - row_peak)
        row_sum = jnp.sum(row_exp, axis=1, keepdims=True)
        probs_low = (row_exp * (1.0 / row_sum)).astype(slim)
        log_total = jnp.broadcast_to(row_peak + jnp.log(row_sum), (scores.shape[0], lanes))
        return own_queries(window, nn_dot(probs_low, value[...])), log_total.T[:8, :]

    attended_low, log_total, cotangent_all, *second_halves = pack_call(
        sizes,
        own_shape,
        attend,
        2,
        4 * pack_rows * pack_rows * head_dim,
        gathered=cotangent,
        resident=(query_low, key_flip, value_low, segment_rows, segment_cols),
        outs=(Out(head_dim, slim), Out(8, wide, flip=True)),
        keep=True,
        ships=expert_ships[first_ships:second_ships],
    )
    attn_branch, *third_halves = pack_call(
        sizes,
        own_shape,
        lambda window, held, totals: (nn_dot(held[0][window, :], held[1][...]), ()),
        3,
        2 * pack_rows * width_all * head_dim,
        resident=(attended_low, out_weight),
        ships=expert_ships[second_ships:],
    )
    far_halves = first_halves + second_halves + third_halves
    gate_weight, up_weight, down_weight = (
        expert_weight(w, far_halves[i * len(halves) : (i + 1) * len(halves)])
        for i, w in enumerate((w_gate, w_up, w_down))
    )

    resid_in = hidden_in.astype(wide)
    middle = resid_in + attn_branch
    gain_second = ffn_norm.astype(wide)
    inv_second = lax.rsqrt(row_total(jnp.sum(middle * middle, axis=1)) / width_all + norm_eps)[
        :, None
    ]

    def experts(rows, window, held, totals):
        gate_w, up_w, down_w, router_w, ids_ref, cotangent_ref = held
        lane = lax.broadcasted_iota(jnp.int32, (rows.shape[0], lanes), 1)
        logits = jnp.where(lane < expert_count, nt_dot(rows, router_w[...]), -1e30)
        logit_exp = jnp.exp(logits - jnp.max(logits, axis=1, keepdims=True))
        route_probs = logit_exp / jnp.sum(logit_exp, axis=1, keepdims=True)
        block = window.start // tok_rows
        within = pl.multiple_of(window.start - block * tok_rows, rows.shape[0])
        ids = ids_ref[block, :, pl.ds(within, rows.shape[0])].T
        chosen = jnp.zeros((rows.shape[0], lanes), wide)
        for pick in range(ids.shape[1]):
            chosen = chosen + (ids[:, pick : pick + 1] == lane).astype(wide)
        gate_weights = route_probs * chosen
        first_expert = lax.axis_index("ctx") * own_experts
        rows_grad = cotangent_ref[window, :]
        grad_logits = jnp.zeros((rows.shape[0], lanes), wide)
        mixed_list, gate_list, up_list = [], [], []
        for slot in range(own_experts):
            mine = (lane == first_expert + slot).astype(wide)
            gates = jnp.sum(gate_weights * mine, axis=1, keepdims=True)
            gate_proj = nn_dot(rows, gate_w[slot])
            up_proj = nn_dot(rows, up_w[slot])
            grad_mixed = nn_dot(rows_grad, down_w[slot]).astype(slim).astype(wide)
            gate_sigmoid = jax.nn.sigmoid(gate_proj)
            silu = gate_proj * gate_sigmoid
            activity = silu * up_proj
            mixed_list.append((gates * activity).astype(slim))
            grad_gates = jnp.sum(grad_mixed * activity, axis=1, keepdims=True)
            grad_activity = grad_mixed * gates
            gate_list.append(
                (
                    grad_activity * up_proj * (gate_sigmoid + silu * (1.0 - gate_sigmoid))
                ).astype(slim)
            )
            up_list.append((grad_activity * silu).astype(slim))
            grad_logits = grad_logits + gates * grad_gates * (mine - route_probs)
        return (
            jnp.concatenate(mixed_list, axis=1),
            jnp.concatenate(gate_list, axis=1),
            jnp.concatenate(up_list, axis=1),
            grad_logits,
        )

    mixed_low, grad_gate_low, grad_up_low, grad_logits_low, normed_second = pack_call(
        sizes,
        own_shape,
        experts,
        4,
        6 * pack_rows * width_all * own_units,
        gathered=(middle * inv_second * gain_second).astype(slim),
        resident=(gate_weight, up_weight, down_weight, router_pad, ids_all, cotangent_all),
        outs=(
            Out(own_units, slim),
            Out(own_units, slim),
            Out(own_units, slim),
            Out(lanes, slim),
        ),
        keep=True,
    )

    def back(window, held, totals):
        gate_grad, up_grad, logit_grad, gate_w, up_w, router_w, _ = held
        total = nn_dot(logit_grad[window, :], router_w[...])
        for slot in range(own_experts):
            total = total + nt_dot(units_of(gate_grad, window, slot), gate_w[slot])
            total = total + nt_dot(units_of(up_grad, window, slot), up_w[slot])
        return total, ()

    def feature_tile(left, right):
        return lambda window, held: tn_dot(held[left][:, window], held[right][...])

    grad_second, gate_own, gate_far, router_own, router_far = pack_call(
        sizes,
        own_shape,
        back,
        5,
        6 * pack_rows * width_all * own_units,
        resident=(
            grad_gate_low,
            grad_up_low,
            grad_logits_low,
            gate_weight,
            up_weight,
            router_pad,
            normed_second,
        ),
        makes=(
            Make(own_units, width_all, feature_tile(6, 0), True),
            Make(lanes, width_all, feature_tile(6, 2), True),
        ),
    )

    def by_head(blocks):
        rows = blocks.shape[1]
        summed = jnp.sum(
            blocks.reshape(sharers, local_heads, rows, head_dim).astype(wide), axis=0
        )
        return jnp.swapaxes(summed, 0, 1).reshape(rows, local_heads * head_dim)

    gain_two_grad = jnp.sum(grad_second * middle * inv_second, axis=0)
    second_scaled = grad_second * gain_second
    second_inner = row_total(jnp.sum(second_scaled * middle, axis=1))[:, None]
    grad_middle = (
        cotangent.astype(wide)
        + inv_second * second_scaled
        - middle * inv_second**3 * second_inner / width_all
    )

    half_units = own_units // 2

    def down_tile(half):
        return lambda window, held: tn_dot(
            held[3][:, window], held[4][:, pl.ds(half * half_units, half_units)]
        )

    (
        grad_attended,
        grad_middle_all,
        up_own,
        up_far,
        first_own,
        first_far,
        second_own,
        second_away,
        gate_blocks,
        router_blocks,
    ) = pack_call(
        sizes,
        own_shape,
        lambda rows, window, held, totals: (own_queries(window, nt_dot(rows, held[0][...])),),
        6,
        2 * pack_rows * width_all * (head_dim + own_units),
        gathered=grad_middle.astype(slim),
        resident=(out_weight, normed_second, grad_up_low, cotangent_all, mixed_low),
        outs=(Out(head_dim, slim),),
        keep=True,
        makes=(
            Make(own_units, width_all, feature_tile(1, 2), True),
            Make(half_units, width_all, down_tile(0), True),
            Make(half_units, width_all, down_tile(1), False),
        ),
        deals=(Deal(gate_own, gate_far, own_experts), Deal(router_own, router_far)),
    )
    grad_gate = gate_blocks.astype(wide)
    grad_router = row_total(
        jnp.sum(router_blocks[:, :, :expert_count].astype(wide), axis=0).T
    )

    def attend_back(window, held, totals):
        mixed_ref, down_w, query, key, key_t, value, grad_att = held[:7]
        seg_rows, seg_cols, log_ref = held[7:10]
        grad_query_rot, grad_key_rot, grad_value, _ = totals
        query_chunk, grad_chunk = query[window, :], grad_att[window, :]
        scores = nt_dot(key[...], query_chunk) * score_scale
        key_segments = jnp.concatenate([seg_rows[...]] * (tok_rows // lanes), axis=1)
        same_seq = key_segments == seg_cols[0:1, window]
        probs = jnp.exp(jnp.where(same_seq, scores, -1e30) - log_ref[0:1, window])
        grad_probs = nt_dot(value[...], grad_chunk)
        inner = jnp.sum(probs * grad_probs, axis=0, keepdims=True)
        grad_scores = (probs * (grad_probs - inner)).astype(slim)
        grad_value[...] += nn_dot(probs.astype(slim), grad_chunk)
        grad_key_rot[...] += nn_dot(grad_scores, query_chunk)
        grad_query_rot[window, :] = nn_dot(key_t[...], grad_scores).T
        total = sum(
            nt_dot(units_of(mixed_ref, window, slot), down_w[slot]) for slot in range(own_experts)
        )
        return total, ()

    def unturn(window, held, stage, totals):
        raws, cos_table, sin_table, gains = held[10:12], held[12], held[13], held[14:16]
        grad_rots, grad_value, gain_sums = totals[:2], totals[2], totals[3]
        cos_rows, sin_rows = cos_table[window, :], sin_table[window, :]
        for which in range(2):
            grad_rot = grad_rots[which][window, :] * score_scale
            raw = raws[which][window, :]
            inverse = lax.rsqrt(jnp.mean(raw * raw, axis=1, keepdims=True) + norm_eps)
            grad_normed = grad_rot * cos_rows + pltpu.roll(grad_rot * sin_rows, head_dim // 2, 1)
            weighted = grad_normed * gains[which][...]
            grad_raw = inverse * weighted - raw * inverse**3 * jnp.mean(
                weighted * raw, axis=1, keepdims=True
            )
            stage[0][window, pl.ds(which * head_dim, head_dim)] = grad_raw.astype(slim)
            gain_sums[pl.ds(which, 1), :] += jnp.sum(
                grad_normed * raw * inverse, axis=0, keepdims=True
            )
        stage[0][window, pl.ds(2 * head_dim, head_dim)] = grad_value[window, :].astype(slim)

    expert_branch, grad_qkv_low, _, _, _, gain_sums, second_far, up_blocks, first_blocks = pack_call(
        sizes,
        own_shape,
        attend_back,
        7,
        2 * pack_rows * width_all * own_units + 10 * pack_rows * pack_rows * head_dim,
        resident=(
            mixed_low,
            down_weight,
            query_low,
            key_low,
            key_flip,
            value_low,
            grad_attended,
            segment_rows,
            segment_cols,
            log_total,
            query_raw,
            key_raw,
            cosine,
            sine,
            gain_query,
            gain_key,
        ),
        outs=(Out(3 * head_dim, slim, late=True),),
        totals=(
            ((pack_rows, head_dim), wide),
            ((pack_rows, head_dim), wide),
            ((pack_rows, head_dim), wide),
            ((8, head_dim), wide),
        ),
        last=unturn,
        ships=(
            Ship(
                "fsdp",
                second_away,
                lambda ref, shift: ref.at[shift - 1],
                (part_width, half_units),
            ),
        ),
        deals=(Deal(up_own, up_far, own_experts), Deal(first_own, first_far, own_experts // 2)),
    )
    hidden_out = (middle + expert_branch).astype(slim)
    grad_up = up_blocks.astype(wide)

    def last_tile(window, held):
        return jnp.concatenate(
            [
                tn_dot(held[2][:, window], held[0][...]),
                tn_dot(held[3][:, window], held[4][...]),
            ],
            axis=1,
        )

    grad_first, last_blocks, second_blocks = pack_call(
        sizes,
        own_shape,
        lambda window, held, totals: (nt_dot(held[0][window, :], held[1][...]), ()),
        8,
        2 * pack_rows * width_all * 7 * head_dim,
        resident=(grad_qkv_low, qkv_weight, normed_first, grad_middle_all, attended_low),
        tiles=Tiles(4 * head_dim, width_all, last_tile),
        deals=(Deal(second_own, second_far, own_experts // 2),),
    )
    by_halves = (ctx_size, own_experts // 2) + first_blocks.shape[1:]
    grad_down = (
        jnp.concatenate([first_blocks.reshape(by_halves), second_blocks.reshape(by_halves)], axis=1)
        .reshape((expert_count,) + first_blocks.shape[1:])
        .astype(wide)
    )
    grad_query, grad_key, grad_value, grad_out = (
        by_head(last_blocks[:, :, i * head_dim : (i + 1) * head_dim]) for i in range(4)
    )
    grad_out = grad_out.T

    gain_first = attn_norm.astype(wide)
    inv_first = lax.dynamic_slice_in_dim(inv_all, ctx_place * tok_rows, tok_rows, 0)[:, :1]
    gain_one_grad = jnp.sum(grad_first * resid_in * inv_first, axis=0)
    first_scaled = grad_first * gain_first
    first_inner = row_total(jnp.sum(first_scaled * resid_in, axis=1))[:, None]
    grad_hidden = (
        grad_middle + inv_first * first_scaled - resid_in * inv_first**3 * first_inner / width_all
    )

    stream_part = jnp.stack(
        [
            jnp.sum(middle * middle),
            jnp.sum(attn_branch * attn_branch),
            jnp.sum(expert_branch * expert_branch),
        ]
    )
    gain_rows = col_count // lanes
    sums = small_sums(
        sizes,
        jnp.concatenate(
            [
                gain_one_grad.reshape(gain_rows, lanes),
                gain_two_grad.reshape(gain_rows, lanes),
                gain_sums,
                jnp.pad(stream_part[None, :], ((0, 7), (0, lanes - 3))),
            ],
            axis=0,
        ),
        9,
    )
    tp_sums = jnp.sum(sums[:, 2 * gain_rows :], axis=0)
    token_count = tok_rows * packs * ctx_size
    stream_rms = jnp.sqrt(tp_sums[8, :3] / (token_count * width_all))
    return (
        hidden_out,
        grad_hidden,
        sums[:, :gain_rows].reshape(width_all),
        sums[:, gain_rows : 2 * gain_rows].reshape(width_all),
        tp_sums[0],
        tp_sums[1],
        grad_query,
        grad_key,
        grad_value,
        grad_out,
        grad_router,
        grad_gate,
        grad_up,
        grad_down,
        stream_rms,
    )


def solution(mesh):
    return jax.shard_map(
        on_device,
        mesh=mesh,
        in_specs=(
            P(("fsdp", "ctx"), "tp"),
            P(("fsdp", "ctx"), "tp"),
            P("fsdp", None),
            P("fsdp", None),
            P(("fsdp", "ctx"), None),
            P("tp"),
            P("tp"),
            P(),
            P(),
            P("fsdp", "tp"),
            P("fsdp", "tp"),
            P("fsdp", "tp"),
            P("tp", "fsdp"),
            P(None, "fsdp"),
            P(None, "fsdp", "tp"),
            P(None, "fsdp", "tp"),
            P(None, "fsdp", "tp"),
        ),
        out_specs=(
            P(("fsdp", "ctx"), "tp"),
            P(("fsdp", "ctx"), "tp"),
            P(),
            P(),
            P(),
            P(),
            P(("fsdp", "ctx"), "tp"),
            P(("fsdp", "ctx"), "tp"),
            P(("fsdp", "ctx"), "tp"),
            P("tp", ("fsdp", "ctx")),
            P(None, ("fsdp", "ctx")),
            P(None, ("fsdp", "ctx"), "tp"),
            P(None, ("fsdp", "ctx"), "tp"),
            P(None, ("fsdp", "ctx"), "tp"),
            P(),
        ),
        check_vma=False,
    )
```

```python
import jax
import jax.numpy as jnp
from jax import lax
from jax.experimental import pallas as pl
from jax.experimental.pallas import tpu as pltpu
from jax.sharding import PartitionSpec as P

norm_eps = 1e-06
rope_base = 10000.0


def locate(pack_spots, lengths_row):
    seq_ends = jnp.cumsum(lengths_row)
    starts = seq_ends - lengths_row
    segment = jnp.sum((pack_spots[:, None] >= seq_ends[None, :]).astype(jnp.int32), axis=1)
    slot_ids = jnp.arange(lengths_row.shape[0], dtype=jnp.int32)
    seq_begin = jnp.sum(
        jnp.where(segment[:, None] == slot_ids[None, :], starts[None, :], 0), axis=1
    )
    return (segment, pack_spots - seq_begin)


def rope_tables(pack_spots, head_dim):
    half_dim = head_dim // 2
    inv_freq = rope_base ** (-(jnp.arange(half_dim, dtype=jnp.float32) * 2.0 / head_dim))
    angle_grid = pack_spots.astype(jnp.float32)[:, None] * inv_freq[None, :]
    cosine, sine = jnp.cos(angle_grid), jnp.sin(angle_grid)
    return jnp.concatenate([cosine, cosine], axis=1), jnp.concatenate([-sine, sine], axis=1)


def unrotate(grad_rot, cosine, sine):
    return grad_rot * cosine + jnp.roll(grad_rot * sine, grad_rot.shape[1] // 2, axis=1)


CHUNKS = 2
MESH_ID = pl.DeviceIdType.MESH
VMEM_LIMIT = 64 * 1000 * 1000


class Pack:
    def __init__(self, ctx_size, tp_size, rows, cols, packs=1):
        self.line = ctx_size // 2
        self.packs = packs
        self.tp_size, self.rows, self.cols = tp_size, rows, cols
        self.chunk = rows // CHUNKS
        self.steps = self.line * CHUNKS
        place = lax.axis_index("ctx")
        self.a, self.b = place // 2, place % 2
        self.t = lax.axis_index("tp")
        self.has_up, self.has_down = self.a < self.line - 1, self.a > 0

    def up(self):
        return {"ctx": (self.a + 1) * 2 + self.b}

    def down(self):
        return {"ctx": (self.a - 1) * 2 + self.b}

    def pair(self):
        return {"ctx": self.a * 2 + (1 - self.b)}

    def sibling(self, shift):
        return {"tp": self.t ^ shift}

    def ctx_peer(self, shift):
        return {"ctx": lax.axis_index("ctx") ^ shift}

    def other_pack(self, shift):
        return {"fsdp": lax.axis_index("fsdp") ^ shift}

    def meet(self, everyone):
        barrier = pltpu.get_barrier_semaphore()

        def greet(device):
            pl.semaphore_signal(barrier, inc=1, device_id=device, device_id_type=MESH_ID)

        if everyone:
            near = 2 * self.line - 1
            for shift in range(1, 2 * self.line):
                greet(self.ctx_peer(shift))
        else:
            near = 1 + jnp.where(self.has_up, 1, 0) + jnp.where(self.has_down, 1, 0)

            @pl.when(self.has_up)
            def _():
                greet(self.up())

            @pl.when(self.has_down)
            def _():
                greet(self.down())

            greet(self.pair())
        for shift in range(1, self.tp_size):
            greet(self.sibling(shift))
        for shift in range(1, self.packs):
            greet(self.other_pack(shift))
        pl.semaphore_wait(barrier, near + self.tp_size + self.packs - 2)

    def row0(self, block, k):
        return pl.multiple_of(block * self.rows + k * self.chunk, self.chunk)

    def region(self, ref, block, k, part):
        return ref.at[
            pl.ds(self.row0(block, k), self.chunk),
            pl.ds(pl.multiple_of(part * self.cols, self.cols), self.cols),
        ]


def pick(table, i):
    result = jnp.int32(table[-1])
    for at, value in enumerate(table[:-1]):
        result = jnp.where(i == at, value, result)
    return result


def remote(src, dst, send_sem, recv_sem, device):
    return pltpu.make_async_remote_copy(
        src_ref=src,
        dst_ref=dst,
        send_sem=send_sem,
        recv_sem=recv_sem,
        device_id=device,
        device_id_type=MESH_ID,
    )


def loop(count, body):
    lax.fori_loop(0, count, lambda i, carry: (body(i), carry)[1], 0)


def gather_scratch(ctx_size, tp_size, rows, cols, dtype):
    line, dma = ctx_size // 2, pltpu.SemaphoreType.DMA
    return [
        pltpu.VMEM((ctx_size * rows, tp_size * cols), dtype),
        dma((2 * line * CHUNKS,)),
        dma((2 * line * CHUNKS,)),
        dma((4 * line * (tp_size - 1) * CHUNKS,)),
        dma((ctx_size * CHUNKS,)),
        dma(((tp_size - 1) * ctx_size * CHUNKS,)),
        dma,
    ]


def gather_steps(pack, src, scratch, everyone, lag, begin, before, compute):
    buf, line_sems, pair_sems, tp_sems, own_sems, sib_sems, local_sem = scratch
    line, t, a, b = pack.line, pack.t, pack.a, pack.b
    ctx_size = 2 * line

    def part(block, k):
        return pack.region(buf, block, k, t)

    def line_copy(piece, block, k, down, dist):
        return remote(
            piece,
            part(block, k),
            line_sems.at[(down * line + dist) * CHUNKS + k],
            own_sems.at[block * CHUNKS + k],
            pack.down() if down else pack.up(),
        )

    def pair_copy(piece, block, k, slot):
        return remote(
            piece,
            part(block, k),
            pair_sems.at[slot * CHUNKS + k],
            own_sems.at[block * CHUNKS + k],
            pack.pair(),
        )

    def tp_copy(piece, block, k, slot, shift):
        return remote(
            piece,
            part(block, k),
            tp_sems.at[(slot * (pack.tp_size - 1) + shift - 1) * CHUNKS + k],
            sib_sems.at[((shift - 1) * ctx_size + block) * CHUNKS + k],
            pack.sibling(shift),
        )

    def send_tp(piece, block, k, slot):
        for shift in range(1, pack.tp_size):
            tp_copy(piece, block, k, slot, shift).start()

    def await_own(block, k):
        piece = part(block, k)
        pair_copy(piece, block, k, 0).wait_recv()

    pack.meet(everyone)
    mine = a * 2 + b
    own_copy = pltpu.make_async_copy(
        src,
        buf.at[
            pl.ds(pl.multiple_of(mine * pack.rows, pack.rows), pack.rows),
            pl.ds(pl.multiple_of(t * pack.cols, pack.cols), pack.cols),
        ],
        local_sem,
    )
    own_copy.start()
    for k in range(CHUNKS):
        piece = src.at[pl.ds(k * pack.chunk, pack.chunk), :]

        @pl.when(pack.has_up)
        def _():
            line_copy(piece, mine, k, 0, 0).start()

        @pl.when(pack.has_down)
        def _():
            line_copy(piece, mine, k, 1, 0).start()

        pair_copy(piece, mine, k, 0).start()
    for k in range(CHUNKS):
        send_tp(src.at[pl.ds(k * pack.chunk, pack.chunk), :], mine, k, 0)
    begin()
    own_copy.wait()

    def ways(dist):
        below, above = a - dist, a + dist
        return (
            (0, below, below >= 0, jnp.logical_and(below >= 0, pack.has_up)),
            (1, above, above < line, jnp.logical_and(above < line, pack.has_down)),
        )

    def from_line(dist, k):
        for down, node, there, onward in ways(dist):
            block = node * 2 + b

            @pl.when(there)
            def _():
                await_own(block, k)

            @pl.when(onward)
            def _():
                line_copy(part(block, k), block, k, down, dist).start()

            @pl.when(there)
            def _():
                pair_copy(part(block, k), block, k, down * line + dist).start()
                send_tp(part(block, k), block, k, down * line + dist)

    def from_pair(dist, k):
        for down, node, there, _ in ways(dist):
            block = node * 2 + (1 - b)
            if down:
                there = jnp.logical_and(there, dist > 0)

            @pl.when(there)
            def _():
                await_own(block, k)
                send_tp(part(block, k), block, k, (2 + down) * line + dist)

    def work(block, k, order):
        for shift in range(1, pack.tp_size):
            piece = pack.region(buf, block, k, t ^ shift)
            remote(
                piece,
                piece,
                tp_sems.at[0],
                sib_sems.at[((shift - 1) * ctx_size + block) * CHUNKS + k],
                pack.sibling(shift),
            ).wait_recv()
        compute(pack.row0(block, k), block * CHUNKS + k, order)

    def step(s):
        dist, k = s // CHUNKS, s % CHUNKS

        @pl.when(s == lag)
        def _():
            before()

        turn = s - lag

        def side(i):
            @pl.when(jnp.logical_and(i == 0, dist + 1 < line))
            def _():
                from_line(dist + 1, k)

            @pl.when(jnp.logical_and(i == 1, s < pack.steps))
            def _():
                from_pair(dist, k)

            late = turn - i
            node, late_k = a ^ (late // CHUNKS), late % CHUNKS

            @pl.when(jnp.logical_and(late >= 0, late < pack.steps))
            def _():
                order = jnp.where(
                    i == 0,
                    jnp.maximum(2 * turn - 1, 0),
                    jnp.minimum(2 * turn, 2 * pack.steps - 1),
                )
                work(node * 2 + jnp.where(i == 0, b, 1 - b), late_k, order)

        loop(2, side)

    loop(pack.steps + 1 + lag, step)

    def drain(s):
        dist, k = s // CHUNKS, s % CHUNKS
        piece = part(0, 0)
        for down, _, there, onward in ways(dist):

            @pl.when(jnp.logical_and(onward, dist < line - 1))
            def _():
                line_copy(piece, 0, k, down, dist).wait_send()

            if down:
                there = jnp.logical_and(there, dist > 0)

            @pl.when(there)
            def _():
                pair_copy(piece, 0, k, down * line + dist).wait_send()
                for shift in range(1, pack.tp_size):
                    tp_copy(piece, 0, k, down * line + dist, shift).wait_send()
                    tp_copy(piece, 0, k, (2 + down) * line + dist, shift).wait_send()

    loop(pack.steps, drain)


def scatter_scratch(ctx_size, tp_size, rows, cols):
    line, dma = ctx_size // 2, pltpu.SemaphoreType.DMA
    low = jnp.bfloat16
    return [
        pltpu.VMEM((ctx_size * rows, tp_size * cols), low),
        pltpu.VMEM(((tp_size - 1) * ctx_size * rows, cols), low),
        pltpu.VMEM((line * rows, cols), low),
        pltpu.VMEM((2 * line * rows, cols), low),
        dma(((tp_size - 1) * ctx_size * CHUNKS,)),
        dma((line * CHUNKS,)),
        dma((line * CHUNKS,)),
        dma(((tp_size - 1) * ctx_size * CHUNKS,)),
        dma((line * CHUNKS,)),
        dma((2 * line * CHUNKS,)),
    ]


def scatter_steps(pack, scratch, everyone, begin, before, compute, jobs, tail, finish):
    (full, sib_buf, pair_buf, line_buf, tp_send, pair_send, line_send, tp_recv, pair_recv, line_recv) = scratch
    line, t, a, b = pack.line, pack.t, pack.a, pack.b
    ctx_size = 2 * line
    wide, low = jnp.float32, jnp.bfloat16
    table = [
        sorted(range(line), key=lambda o, node=node: (-abs(o - node), o)) for node in range(line)
    ]

    def owner(i):
        result = jnp.int32(0)
        for node in range(line):
            for place in range(line):
                here = jnp.logical_and(a == node, i == place)
                result = jnp.where(here, table[node][place], result)
        return result

    def tp_copy(block, k, shift):
        return remote(
            pack.region(full, block, k, t ^ shift),
            sib_buf.at[
                pl.ds(pack.row0((shift - 1) * ctx_size + block, k), pack.chunk), :
            ],
            tp_send.at[((shift - 1) * ctx_size + block) * CHUNKS + k],
            tp_recv.at[((shift - 1) * ctx_size + block) * CHUNKS + k],
            pack.sibling(shift),
        )

    def pair_copy(node, k):
        return remote(
            pack.region(full, node * 2 + (1 - b), k, t),
            pair_buf.at[pl.ds(pack.row0(node, k), pack.chunk), :],
            pair_send.at[node * CHUNKS + k],
            pair_recv.at[node * CHUNKS + k],
            pack.pair(),
        )

    def line_copy(node, k, down):
        return remote(
            pack.region(full, node * 2 + b, k, t),
            line_buf.at[pl.ds(pack.row0(down * line + node, k), pack.chunk), :],
            line_send.at[node * CHUNKS + k],
            line_recv.at[(down * line + node) * CHUNKS + k],
            pack.down() if down else pack.up(),
        )

    def own_part(block, k):
        return full[
            pl.ds(pack.row0(block, k), pack.chunk),
            pl.ds(pl.multiple_of(t * pack.cols, pack.cols), pack.cols),
        ].astype(wide)

    def put_part(block, k, value):
        full[
            pl.ds(pack.row0(block, k), pack.chunk),
            pl.ds(pl.multiple_of(t * pack.cols, pack.cols), pack.cols),
        ] = value.astype(low)

    def landed(ref, block, k):
        return ref[pl.ds(pack.row0(block, k), pack.chunk), :].astype(wide)

    def fill(block):
        row0 = pl.multiple_of(block * pack.rows, pack.rows)
        full[pl.ds(row0, pack.rows), :] = compute(row0)
        for k in range(CHUNKS):
            for shift in range(1, pack.tp_size):
                tp_copy(block, k, shift).start()

    def join(block, k):
        total = own_part(block, k)
        for shift in range(1, pack.tp_size):
            tp_copy(block, k, shift).wait_recv()
            total = total + landed(sib_buf, (shift - 1) * ctx_size + block, k)
        put_part(block, k, total)

    pack.meet(everyone)
    begin()
    before()

    def step(s):
        @pl.when(s < pack.steps)
        def _():
            node, k = owner(s // CHUNKS), s % CHUNKS

            def side(i):
                @pl.when(k == 0)
                def _():
                    fill(node * 2 + jnp.where(i == 0, 1 - b, b))

                jobs(2 * s + i)

            loop(2, side)

        late = s - 1

        @pl.when(jnp.logical_and(late >= 0, late < pack.steps))
        def _():
            node, k = owner(late // CHUNKS), late % CHUNKS

            def side(i):
                join(node * 2 + jnp.where(i == 0, 1 - b, b), k)

                @pl.when(i == 0)
                def _():
                    pair_copy(node, k).start()

            loop(2, side)

        if tail is not None:
            turn = s - (pack.steps - 1)
            share = ctx_size * CHUNKS // 4

            @pl.when(jnp.logical_and(turn >= 0, turn < 4))
            def _():
                loop(share, lambda i: tail(turn * share + i))

        later = s - 4

        @pl.when(later >= 0)
        def _():
            node, k = owner(later // CHUNKS), later % CHUNKS
            pair_copy(node, k).wait_recv()
            put_part(
                node * 2 + b, k, own_part(node * 2 + b, k) + landed(pair_buf, node, k)
            )
            from_below = jnp.logical_and(pack.has_down, node >= a)
            from_above = jnp.logical_and(pack.has_up, node <= a)
            for down, there in ((0, from_below), (1, from_above)):

                @pl.when(there)
                def _():
                    line_copy(node, k, down).wait_recv()
                    put_part(
                        node * 2 + b,
                        k,
                        own_part(node * 2 + b, k) + landed(line_buf, down * line + node, k),
                    )

            @pl.when(node > a)
            def _():
                line_copy(node, k, 0).start()

            @pl.when(node < a)
            def _():
                line_copy(node, k, 1).start()

            @pl.when(node == a)
            def _():
                finish(k, own_part(node * 2 + b, k))

    loop(pack.steps + 4, step)

    def drain(s):
        node, k = s // CHUNKS, s % CHUNKS
        pair_copy(node, k).wait_send()
        for shift in range(1, pack.tp_size):
            tp_copy(node * 2, k, shift).wait_send()
            tp_copy(node * 2 + 1, k, shift).wait_send()

        @pl.when(node > a)
        def _():
            line_copy(node, k, 0).wait_send()

        @pl.when(node < a)
        def _():
            line_copy(node, k, 1).wait_send()

    loop(pack.steps, drain)


ANY = pl.BlockSpec(memory_space=pl.ANY)


def nn_dot(left, right):
    return lax.dot_general(
        left, right, (((1,), (0,)), ((), ())), preferred_element_type=jnp.float32
    )


def nt_dot(left, right):
    return lax.dot_general(
        left, right, (((1,), (1,)), ((), ())), preferred_element_type=jnp.float32
    )


def tn_dot(left, right):
    return lax.dot_general(
        left, right, (((0,), (0,)), ((), ())), preferred_element_type=jnp.float32
    )


class Out:
    def __init__(self, width, dtype, flip=False, late=False):
        self.width, self.dtype, self.flip, self.late = width, dtype, flip, late

    def shape(self, rows):
        return (self.width, rows) if self.flip else (rows, self.width)

    def window(self, ref, window):
        return ref.at[:, window] if self.flip else ref.at[window, :]


class Parts:
    def __init__(self, shape, pieces):
        self.shape, self.pieces = shape, pieces


class Swap:
    def __init__(self, axis, shape, pieces, keep):
        self.axis, self.shape, self.pieces, self.keep = axis, shape, pieces, keep


class Ship:
    def __init__(self, axis, array, source, shape):
        self.axis, self.array, self.source, self.shape = axis, array, source, shape


class Make:
    def __init__(self, width, features, tile, send):
        self.width, self.features, self.tile, self.send = width, features, tile, send


class Deal:
    def __init__(self, own, far, parts=1):
        self.own, self.far, self.parts = own, far, parts
        self.width = own.shape[1] // parts


class Tiles:
    def __init__(self, width, features, tile):
        self.width, self.features, self.tile = width, features, tile


def whole(ref):
    return ref


def pack_call(
    sizes,
    shape,
    piece,
    collective_id,
    flops,
    gathered=None,
    resident=(),
    outs=(),
    totals=(),
    last=None,
    keep=False,
    swaps=(),
    ships=(),
    tiles=None,
    makes=(),
    deals=(),
    lag=0,
    needed=None,
):
    packs, ctx_size, tp_size = sizes
    rows, cols = shape
    all_rows, all_cols = ctx_size * rows, tp_size * cols
    pieces = ctx_size * CHUNKS
    dma = pltpu.SemaphoreType.DMA
    gather = gathered is not None
    if gather:
        base = gather_scratch(ctx_size, tp_size, rows, cols, gathered.dtype)
    else:
        base = scatter_scratch(ctx_size, tp_size, rows, cols)
    axis_size = {"fsdp": packs, "ctx": ctx_size, "tp": tp_size}
    inputs = []

    def enlist(array):
        for i, known in enumerate(inputs):
            if known is array:
                return i
        inputs.append(array)
        return len(inputs) - 1

    if gather:
        enlist(gathered)
    resident = list(resident)
    first_deal = len(resident)
    for deal in deals:
        resident += [deal.own, deal.far]
    parts = [
        r if isinstance(r, Parts) else Parts(r.shape, [(r, whole, whole)]) for r in resident
    ]
    part_list = [[(enlist(x), src, dst) for x, src, dst in p.pieces] for p in parts]
    swap_list = [[(enlist(x), src, dst) for x, src, dst in w.pieces] for w in swaps]
    ship_list = [enlist(ship.array) for ship in ships]
    swap_count = sum(len(w.pieces) * axis_size[w.axis] for w in swaps)
    ship_count = sum(axis_size[ship.axis] for ship in ships)
    kept_swaps = [i for i, w in enumerate(swaps) if w.keep]
    n_out = len(outs) + len(totals) + keep + len(kept_swaps) + len(ships)
    tile_rows = 128
    features = all_cols
    own_features = features // (packs * ctx_size)
    splits = tile_rows // own_features
    own_tiles = features // packs // tile_rows
    far_tiles = (packs - 1) * own_tiles
    assert own_tiles + far_tiles == pieces
    stride = pieces // own_tiles
    deal_order = (4, 1, 6, 2, 5, 3, 7, 0) if own_tiles == 8 else tuple(range(own_tiles))

    def kernel(*refs):
        refs = list(refs)

        def take(count):
            taken = refs[:count]
            del refs[:count]
            return taken

        given = take(len(inputs))
        sum_ref = None if gather else take(1)[0]
        out_refs = take(n_out)
        blocks_ref = None if tiles is None else take(1)[0]
        make_outs = [take(2) for _ in makes]
        deal_outs = take(len(deals))
        scratch = take(len(base))
        held = take(len(resident))
        stage = take(len(outs))
        total_refs = take(len(totals))
        swap_bufs = take(len(swaps))
        (held_sem, out_sem, late_sem, swap_local, swap_send, swap_recv, ship_send, ship_recv) = take(8)
        if tiles is not None:
            tile_stage, tile_far, tile_send, far_recv, block_recv = take(5)
        make_stages = take(len(makes))
        make_send, make_recv, deal_send, deal_recv = take(4)
        over_packs = swaps or ships or tiles is not None or any(make.send for make in makes)
        everyone = tiles is not None or deals or any(ship.axis == "ctx" for ship in ships)
        pack = Pack(ctx_size, tp_size, rows, cols, packs if over_packs else 1)
        mine = {axis: lax.axis_index(axis) for axis in axis_size}
        loads = []
        for target_ref, copies in zip(held, part_list):
            for which, source, target in copies:
                loads.append(
                    pltpu.make_async_copy(
                        source(given[which]), target(target_ref), held_sem.at[len(loads)]
                    )
                )
        swap_copies, swap_sends = [], []
        index = 0
        for swap, buf, copies in zip(swaps, swap_bufs, swap_list):
            for which, source, target in copies:
                here = source(given[which])
                there = target(buf, mine[swap.axis])
                swap_copies.append(pltpu.make_async_copy(here, there, swap_local.at[index]))
                for shift in range(1, axis_size[swap.axis]):
                    slot = index + shift
                    device = {swap.axis: mine[swap.axis] ^ shift}
                    theirs = target(buf, mine[swap.axis] ^ shift)
                    swap_sends.append(
                        (
                            remote(here, there, swap_send.at[slot], swap_recv.at[slot], device),
                            remote(theirs, theirs, swap_send.at[slot], swap_recv.at[slot], device),
                        )
                    )
                index += axis_size[swap.axis]
        late = []
        for i, where in enumerate(kept_swaps):
            late.append((swap_bufs[where], out_refs[len(outs) + len(totals) + keep + i]))
        late_copies = [
            pltpu.make_async_copy(here, there, late_sem.at[i])
            for i, (here, there) in enumerate(late)
        ]
        ship_local, ship_copies = [], []
        index = 0
        for ship, which, landing in zip(ships, ship_list, out_refs[n_out - len(ships) :]):
            place = mine[ship.axis]
            if ship.axis == "ctx":
                here = ship.source(given[which], 0)
                ship_local.append(
                    pltpu.make_async_copy(here, landing.at[place], ship_send.at[index])
                )
            for shift in range(1, axis_size[ship.axis]):
                here = ship.source(given[which], shift)
                there = landing.at[place] if ship.axis == "ctx" else landing.at[shift - 1]
                theirs = landing.at[place ^ shift] if ship.axis == "ctx" else there
                device = {ship.axis: place ^ shift}
                sems = ship_send.at[index + shift], ship_recv.at[index + shift]
                ship_copies.append(
                    (remote(here, there, *sems, device), remote(theirs, theirs, *sems, device))
                )
            index += axis_size[ship.axis]

        prompt = sum(len(copies) for copies in part_list[:needed])

        def await_rest(order):
            @pl.when(order == 0)
            def _():
                for load in loads[prompt:]:
                    load.wait()

        def begin():
            for copy in swap_copies + ship_local:
                copy.start()
            for send, _ in swap_sends + ship_copies:
                send.start()

        def before():
            for ref in total_refs:
                ref[...] = jnp.zeros_like(ref)
            for load in loads[:prompt]:
                load.wait()
            for copy in swap_copies:
                copy.wait()
            for send, receive in swap_sends:
                receive.wait_recv()
            for copy in late_copies:
                copy.start()

        def stores(row0, index):
            window = pl.ds(row0, pack.chunk)
            copies = []
            for i, out in enumerate(outs):
                if not out.late:
                    copies.append((out.window(stage[i], window), out.window(out_refs[i], window), i))
            if keep:
                i = len(outs)
                copies.append(
                    (scratch[0].at[window, :], out_refs[i + len(totals)].at[window, :], i)
                )
            return [
                pltpu.make_async_copy(here, there, out_sem.at[i * pieces + index])
                for here, there, i in copies
            ]

        def put(window, values):
            early = [i for i, out in enumerate(outs) if not out.late]
            for i, value in zip(early, values):
                out = outs[i]
                if out.flip:
                    stage[i][:, window] = value.astype(out.dtype)
                else:
                    stage[i][window, :] = value.astype(out.dtype)

        ahead = 3

        def is_far(order):
            if far_tiles != own_tiles:
                return order < far_tiles
            middle = jnp.logical_and(order >= ahead, order < pieces - ahead)
            return jnp.where(middle, (order - ahead) % 2 == 1, order < ahead)

        def rank(order):
            if far_tiles != own_tiles:
                return jnp.where(order < far_tiles, order, order - far_tiles)
            middle = (order - ahead) // 2
            return jnp.where(
                order < ahead,
                order,
                jnp.where(
                    order >= pieces - ahead,
                    order - far_tiles,
                    jnp.where(is_far(order), ahead + middle, middle),
                ),
            )

        def tile_copy(order, which, shift):
            return remote(
                tile_stage.at[order],
                tile_far.at[which],
                tile_send.at[order * splits],
                far_recv.at[which],
                {"fsdp": mine["fsdp"] ^ shift},
            )

        def block_copy(order, split, owner):
            return remote(
                tile_stage.at[order, pl.ds(split * own_features, own_features), :],
                blocks_ref.at[mine["ctx"]],
                tile_send.at[order * splits + split],
                block_recv.at[mine["ctx"]],
                {"ctx": owner},
            )

        def block_store(order, split):
            return pltpu.make_async_copy(
                tile_stage.at[order, pl.ds(split * own_features, own_features), :],
                blocks_ref.at[mine["ctx"]],
                tile_send.at[order * splits + split],
            )

        def each_block(order, go_away, stay):
            for split in range(splits):
                owner = ((mine["ctx"] // splits) ^ pick(deal_order, rank(order))) * splits + split

                @pl.when(owner != mine["ctx"])
                def _():
                    go_away(order, split, owner)

                @pl.when(owner == mine["ctx"])
                def _():
                    stay(order, split)

        def make_tile(order):
            if tiles is None:
                return
            far, which = is_far(order), rank(order)
            shift = jnp.where(far, which // own_tiles + 1, 0)
            place = (mine["ctx"] // splits) ^ pick(deal_order, which % own_tiles)
            first = ((mine["fsdp"] ^ shift) * own_tiles + place) * tile_rows
            value = tiles.tile(pl.ds(pl.multiple_of(first, tile_rows), tile_rows), held)

            @pl.when(far)
            def _():
                tile_stage[order] = value.astype(jnp.bfloat16)
                tile_copy(order, which, shift).start()

            @pl.when(jnp.logical_not(far))
            def _():
                total = value
                for other in range(packs - 1):
                    slot = other * own_tiles + which
                    tile_copy(order, slot, 1).wait_recv()
                    total = total + tile_far[slot].astype(jnp.float32)
                tile_stage[order] = total.astype(jnp.bfloat16)
                each_block(
                    order,
                    lambda *where: block_copy(*where).start(),
                    lambda *where: block_store(*where).start(),
                )

        def finish_tiles():
            if tiles is None:
                return

            def sent(order):
                @pl.when(is_far(order))
                def _():
                    tile_copy(order, 0, 1).wait_send()

                @pl.when(jnp.logical_not(is_far(order)))
                def _():
                    each_block(
                        order,
                        lambda *where: block_copy(*where).wait_send(),
                        lambda *where: block_store(*where).wait(),
                    )

            loop(pieces, sent)
            for shift in range(1, ctx_size):
                landed = blocks_ref.at[mine["ctx"] ^ shift]
                remote(
                    landed,
                    landed,
                    tile_send.at[0],
                    block_recv.at[mine["ctx"] ^ shift],
                    {"ctx": mine["ctx"] ^ shift},
                ).wait_recv()

        def make_copies(i, order):
            far = order < far_tiles
            which = jnp.where(far, order, order - far_tiles)
            shift = jnp.where(far, which // own_tiles + 1, 0)
            window = pl.ds(
                pl.multiple_of(which % own_tiles * tile_rows, tile_rows), tile_rows
            )
            here = make_stages[i].at[order]
            sem = make_send.at[i * pieces + order]
            own_out, far_out = make_outs[i]
            slot = jnp.maximum(shift - 1, 0)
            send = remote(
                here,
                far_out.at[slot, window, :],
                sem,
                make_recv.at[i * pieces + order],
                {"fsdp": mine["fsdp"] ^ shift},
            )
            away = pltpu.make_async_copy(here, far_out.at[slot, window, :], sem)
            stay = pltpu.make_async_copy(here, own_out.at[window, :], sem)
            return far, shift, which % own_tiles, send, away, stay

        def make_parts(order):
            for i, make in enumerate(makes):
                far, shift, place, send, away, stay = make_copies(i, order)
                first = ((mine["fsdp"] ^ shift) * own_tiles + place) * tile_rows
                value = make.tile(pl.ds(pl.multiple_of(first, tile_rows), tile_rows), held)
                make_stages[i][order] = value.astype(jnp.bfloat16)

                @pl.when(far)
                def _():
                    (send if make.send else away).start()

                @pl.when(jnp.logical_not(far))
                def _():
                    stay.start()

        def finish_parts():
            def sent(order):
                for i, make in enumerate(makes):
                    far, _, _, send, away, stay = make_copies(i, order)

                    @pl.when(far)
                    def _():
                        if make.send:
                            send.wait_send()
                            send.wait_recv()
                        else:
                            away.wait()

                    @pl.when(jnp.logical_not(far))
                    def _():
                        stay.wait()

            loop(pieces, sent)

        deal_first = [sum(d.parts for d in deals[:i]) for i in range(len(deals))]

        def deal_blocks(i, turn, go_away, stay):
            own_buf, landing = held[first_deal + 2 * i], deal_outs[i]
            parts, width = deals[i].parts, deals[i].width
            for split in range(splits):
                owner = ((mine["ctx"] // splits) ^ pick(deal_order, turn)) * splits + split
                window = pl.ds(pl.multiple_of(owner * own_features, own_features), own_features)
                copies = []
                for part in range(parts):
                    here = own_buf.at[window, pl.ds(part * width, width)]
                    there = landing.at[mine["ctx"] * parts + part]
                    sem = deal_send.at[
                        (deal_first[i] + part) * own_tiles * splits + turn * splits + split
                    ]
                    arrived = deal_recv.at[(deal_first[i] + part) * ctx_size + mine["ctx"]]
                    copies.append((here, there, sem, arrived))

                @pl.when(owner != mine["ctx"])
                def _():
                    for copy in copies:
                        go_away(remote(*copy, {"ctx": owner}))

                @pl.when(owner == mine["ctx"])
                def _():
                    for here, there, sem, _ in copies:
                        stay(pltpu.make_async_copy(here, there, sem))

        def deal_out(order):
            if not deals:
                return

            @pl.when(order % stride == 0)
            def _():
                turn = order // stride
                place = (mine["ctx"] // splits) ^ pick(deal_order, turn)
                window = pl.ds(pl.multiple_of(place * tile_rows, tile_rows), tile_rows)
                for i in range(len(deals)):
                    own_buf, far_buf = held[first_deal + 2 * i], held[first_deal + 2 * i + 1]
                    total = own_buf[window, :].astype(jnp.float32)
                    for other in range(packs - 1):
                        total = total + far_buf[other, window, :].astype(jnp.float32)
                    own_buf[window, :] = total.astype(jnp.bfloat16)
                    deal_blocks(i, turn, lambda copy: copy.start(), lambda copy: copy.start())

        def finish_deals():
            if not deals:
                return

            def sent(turn):
                for i in range(len(deals)):
                    deal_blocks(i, turn, lambda copy: copy.wait_send(), lambda copy: copy.wait())

            loop(own_tiles, sent)
            for i in range(len(deals)):
                for shift in range(1, ctx_size):
                    place = mine["ctx"] ^ shift
                    for part in range(deals[i].parts):
                        landed = deal_outs[i].at[place * deals[i].parts + part]
                        sem = deal_recv.at[(deal_first[i] + part) * ctx_size + place]
                        remote(landed, landed, deal_send.at[0], sem, {"ctx": place}).wait_recv()

        for load in loads:
            load.start()
        if gather:

            def compute(row0, index, order):
                window = pl.ds(row0, pack.chunk)
                put(window, piece(scratch[0][window, :], window, held + swap_bufs, total_refs))
                for store in stores(row0, index):
                    store.start()
                await_rest(order)
                deal_out(order)
                make_tile(order)
                make_parts(order)

            gather_steps(pack, given[0], scratch, everyone, lag, begin, before, compute)
        else:

            def compute(row0):
                window = pl.ds(row0, pack.rows)
                rows_value, values = piece(window, held + swap_bufs, total_refs)
                put(window, values)
                return rows_value.astype(jnp.bfloat16)

            def jobs(order):
                await_rest(order)
                deal_out(order)
                make_tile(order)
                make_parts(order)

            def finish(k, total):
                sum_ref[pl.ds(pl.multiple_of(k * pack.chunk, pack.chunk), pack.chunk), :] = total

            def tail(i):
                last(
                    pl.ds(pl.multiple_of(i * pack.chunk, pack.chunk), pack.chunk),
                    held + swap_bufs,
                    stage,
                    total_refs,
                )

            scatter_steps(
                pack, scratch, everyone, begin, before, compute, jobs,
                None if last is None else tail, finish,
            )
        ends = []
        for i, out in enumerate(outs):
            if out.late:
                ends.append((stage[i], out_refs[i]))
        for i, ref in enumerate(total_refs):
            ends.append((ref, out_refs[len(outs) + i]))
        end_copies = [
            pltpu.make_async_copy(here, there, late_sem.at[len(late) + i])
            for i, (here, there) in enumerate(ends)
        ]
        for copy in end_copies:
            copy.start()

        def drain(index):
            for store in stores(pl.multiple_of(index * pack.chunk, pack.chunk), index):
                store.wait()

        loop(pieces, drain)
        finish_tiles()
        finish_parts()
        finish_deals()
        for copy in late_copies + end_copies + ship_local:
            copy.wait()
        for send, _ in swap_sends:
            send.wait_send()
        for send, receive in ship_copies:
            send.wait_send()
            receive.wait_recv()

    low = jnp.bfloat16
    shapes = [jax.ShapeDtypeStruct(out.shape(all_rows), out.dtype) for out in outs]
    shapes += [jax.ShapeDtypeStruct(dims, dtype) for dims, dtype in totals]
    if keep:
        shapes.append(jax.ShapeDtypeStruct((all_rows, all_cols), gathered.dtype))
    shapes += [jax.ShapeDtypeStruct(swaps[i].shape, low) for i in kept_swaps]
    for ship in ships:
        slots = ctx_size if ship.axis == "ctx" else packs - 1
        shapes.append(jax.ShapeDtypeStruct((slots,) + ship.shape, ship.array.dtype))
    if tiles is not None:
        shapes.append(jax.ShapeDtypeStruct((ctx_size, own_features, tiles.width), low))
    part_features = features // packs
    for make in makes:
        shapes.append(jax.ShapeDtypeStruct((part_features, make.width), low))
        shapes.append(jax.ShapeDtypeStruct((packs - 1, part_features, make.width), low))
    for deal in deals:
        shapes.append(
            jax.ShapeDtypeStruct((ctx_size * deal.parts, own_features, deal.width), low)
        )
    out_specs = [ANY] * len(shapes)
    if not gather:
        shapes = [jax.ShapeDtypeStruct(shape, jnp.float32)] + shapes
        out_specs = [pl.BlockSpec(memory_space=pltpu.VMEM)] + out_specs
    tile_scratch = []
    if tiles is not None:
        tile_scratch = [
            pltpu.VMEM((pieces, tile_rows, tiles.width), low),
            pltpu.VMEM((far_tiles, tile_rows, tiles.width), low),
            dma((pieces * splits,)),
            dma((far_tiles,)),
            dma((ctx_size,)),
        ]
    return pl.pallas_call(
        kernel,
        out_shape=tuple(shapes),
        in_specs=[ANY] * len(inputs),
        out_specs=tuple(out_specs),
        scratch_shapes=base
        + [pltpu.VMEM(p.shape, p.pieces[0][0].dtype) for p in parts]
        + [pltpu.VMEM(out.shape(all_rows), out.dtype) for out in outs]
        + [pltpu.VMEM(dims, dtype) for dims, dtype in totals]
        + [pltpu.VMEM(swap.shape, low) for swap in swaps]
        + [
            dma((max(1, sum(len(p.pieces) for p in parts)),)),
            dma(((len(outs) + 1) * pieces,)),
            dma((len(kept_swaps) + len(outs) + len(totals) + 1,)),
            dma((max(1, swap_count),)),
            dma((max(1, swap_count),)),
            dma((max(1, swap_count),)),
            dma((max(1, ship_count),)),
            dma((max(1, ship_count),)),
        ]
        + tile_scratch
        + [pltpu.VMEM((pieces, tile_rows, make.width), low) for make in makes]
        + [
            dma((max(1, len(makes)) * pieces,)),
            dma((max(1, len(makes)) * pieces,)),
            dma((max(1, sum(deal.parts for deal in deals)) * own_tiles * splits,)),
            dma((max(1, sum(deal.parts for deal in deals)) * ctx_size,)),
        ],
        compiler_params=pltpu.CompilerParams(
            collective_id=collective_id, has_side_effects=True, vmem_limit_bytes=VMEM_LIMIT
        ),
        cost_estimate=pl.CostEstimate(
            flops=flops, bytes_accessed=8 * all_rows * all_cols, transcendentals=0
        ),
    )(*inputs)


def small_sums(sizes, tensor, collective_id):
    packs, ctx_size, tp_size = sizes
    dma = pltpu.SemaphoreType.DMA
    count = tensor.shape[0]

    def kernel(src, out_ref, ctx_buf, mid, rest_buf, send_sems, recv_sems):
        f, c, t = (lax.axis_index(axis) for axis in ("fsdp", "ctx", "tp"))
        ctx_peers = [(shift, {"ctx": c ^ shift}) for shift in range(1, ctx_size)]
        rest_peers = [
            (shift * tp_size + turn, {"fsdp": f ^ shift, "tp": t ^ turn})
            for shift in range(packs)
            for turn in range(tp_size)
            if shift or turn
        ]
        barrier = pltpu.get_barrier_semaphore()
        for _, device in ctx_peers + rest_peers:
            pl.semaphore_signal(barrier, inc=1, device_id=device, device_id_type=MESH_ID)
        pl.semaphore_wait(barrier, len(ctx_peers) + len(rest_peers))

        def exchange(source, buf, peers, offset):
            copies = [
                remote(
                    source,
                    buf.at[slot],
                    send_sems.at[offset + slot],
                    recv_sems.at[offset + slot],
                    device,
                )
                for slot, device in peers
            ]
            for copy in copies:
                copy.start()
            for copy in copies:
                copy.wait()

        exchange(src, ctx_buf, ctx_peers, 0)
        total = src[...]
        for slot, _ in ctx_peers:
            total = total + ctx_buf[slot]
        mid[...] = total
        exchange(mid, rest_buf, rest_peers, ctx_size)
        rest_buf[0] = total
        for turn in range(tp_size):
            part = rest_buf[turn]
            for shift in range(1, packs):
                part = part + rest_buf[shift * tp_size + turn]
            out_ref[t ^ turn] = part

    return pl.pallas_call(
        kernel,
        out_shape=jax.ShapeDtypeStruct((tp_size, count, tensor.shape[1]), jnp.float32),
        in_specs=[pl.BlockSpec(memory_space=pltpu.VMEM)],
        out_specs=pl.BlockSpec(memory_space=pltpu.VMEM),
        scratch_shapes=[
            pltpu.VMEM((ctx_size,) + tensor.shape, jnp.float32),
            pltpu.VMEM(tensor.shape, jnp.float32),
            pltpu.VMEM((packs * tp_size,) + tensor.shape, jnp.float32),
            dma((ctx_size + packs * tp_size,)),
            dma((ctx_size + packs * tp_size,)),
        ],
        compiler_params=pltpu.CompilerParams(collective_id=collective_id, has_side_effects=True),
    )(tensor)

def on_device(
    hidden_in,
    cotangent,
    positions,
    seq_lengths,
    expert_ids,
    attn_norm,
    ffn_norm,
    query_norm,
    key_norm,
    w_query,
    w_key,
    w_value,
    w_out,
    w_router,
    w_gate,
    w_up,
    w_down,
):
    tok_rows, col_count = hidden_in.shape
    packs, ctx_size, tp_size = (lax.axis_size(axis) for axis in ("fsdp", "ctx", "tp"))
    sizes = (packs, ctx_size, tp_size)
    own_shape = (tok_rows, col_count)
    ctx_place = lax.axis_index("ctx")
    width_all = col_count * tp_size
    part_width = width_all // packs
    pack_rows = tok_rows * ctx_size
    head_dim = query_norm.shape[0]
    local_heads = w_query.shape[1] // head_dim
    expert_count, hidden_units = w_gate.shape[0], w_gate.shape[2]
    own_experts = expert_count // ctx_size
    own_units = own_experts * hidden_units
    top_count = expert_ids.shape[1]
    sharers = ctx_size // local_heads
    score_scale = head_dim ** (-0.5)
    wide = jnp.float32
    slim = jnp.bfloat16
    lanes = 128

    def row_total(tensor):
        return lax.psum(tensor, "tp")

    def units_of(ref, window, slot):
        return ref[window, pl.ds(slot * hidden_units, hidden_units)]

    def own_queries(window, value):
        if sharers == 1:
            return value
        share = window.start // (pack_rows // sharers)
        return jnp.where(share == lax.axis_index("ctx") // local_heads, value, 0.0)

    def head_window():
        return pl.ds(
            pl.multiple_of(lax.axis_index("ctx") % local_heads * head_dim, head_dim), head_dim
        )

    def part_of(place, size):
        return pl.ds(pl.multiple_of(place * size, size), size)

    half_rows = part_width // 2

    def half_ship(weight, slot, half):
        return Ship(
            "fsdp",
            weight,
            lambda ref, shift: ref.at[
                lax.axis_index("ctx") * own_experts + slot,
                pl.ds(half * half_rows, half_rows),
                :,
            ],
            (half_rows, hidden_units),
        )

    halves = [(slot, half) for slot in range(own_experts) for half in range(2)]
    expert_ships = [half_ship(w, *which) for w in (w_gate, w_up, w_down) for which in halves]
    first_ships = len(expert_ships) // 4
    second_ships = first_ships + (len(expert_ships) - first_ships) // 2

    def expert_weight(weight, far):
        pieces = [
            (
                weight,
                lambda ref: ref.at[pl.ds(lax.axis_index("ctx") * own_experts, own_experts), :, :],
                lambda buf: buf.at[:, part_of(lax.axis_index("fsdp"), part_width), :],
            )
        ]
        for (slot, half), array in zip(halves, far):
            for shift in range(1, packs):
                pieces.append(
                    (
                        array,
                        lambda ref, shift=shift: ref.at[shift - 1],
                        lambda buf, slot=slot, half=half, shift=shift: buf.at[
                            slot,
                            part_of((lax.axis_index("fsdp") ^ shift) * 2 + half, half_rows),
                            :,
                        ],
                    )
                )
        return Parts((own_experts, width_all, hidden_units), pieces)

    segment, place = locate(positions[0], seq_lengths[0])
    cosine, sine = rope_tables(place, head_dim)
    segment_rows = jnp.broadcast_to(segment[:, None], (pack_rows, lanes))
    segment_cols = jnp.broadcast_to(segment[None, :], (8, pack_rows))

    def project(rows, window, held, totals):
        cos_table, sin_table, gain_q, gain_k, weight, _, gain, _ = held
        hidden = rows.astype(wide)
        inverse = lax.rsqrt(jnp.mean(hidden * hidden, axis=1, keepdims=True) + norm_eps)
        normed = (hidden * inverse * gain[...].astype(wide)).astype(slim)
        raw = nn_dot(normed, weight[...])
        cos_rows, sin_rows = cos_table[window, :], sin_table[window, :]

        def prepare(raw_proj, gain_vec):
            inv = lax.rsqrt(jnp.mean(raw_proj * raw_proj, axis=1, keepdims=True) + norm_eps)
            scaled = raw_proj * inv * gain_vec[...]
            return scaled * cos_rows + pltpu.roll(scaled, head_dim // 2, 1) * sin_rows

        query_raw = raw[:, :head_dim]
        key_raw = raw[:, head_dim : 2 * head_dim]
        key_turned = prepare(key_raw, gain_k)
        return (
            normed,
            jnp.broadcast_to(inverse, (rows.shape[0], lanes)),
            query_raw,
            key_raw,
            prepare(query_raw, gain_q),
            key_turned,
            key_turned.T,
            raw[:, 2 * head_dim :],
        )

    gain_query = query_norm.astype(wide)[None, :]
    gain_key = key_norm.astype(wide)[None, :]
    (
        normed_first,
        inv_all,
        query_raw,
        key_raw,
        query_low,
        key_low,
        key_flip,
        value_low,
        qkv_weight,
        out_weight,
        router_full,
        *first_halves,
        ids_all,
    ) = pack_call(
        sizes,
        own_shape,
        project,
        1,
        6 * pack_rows * width_all * head_dim,
        gathered=hidden_in,
        resident=(cosine, sine, gain_query, gain_key),
        outs=(
            Out(width_all, slim),
            Out(lanes, wide),
            Out(head_dim, wide),
            Out(head_dim, wide),
            Out(head_dim, slim),
            Out(head_dim, slim),
            Out(head_dim, slim, flip=True),
            Out(head_dim, slim),
        ),
        swaps=(
            Swap(
                "fsdp",
                (width_all, 3 * head_dim),
                [
                    (
                        w,
                        lambda ref: ref.at[:, head_window()],
                        lambda buf, place, i=i: buf.at[
                            part_of(place, part_width), pl.ds(i * head_dim, head_dim)
                        ],
                    )
                    for i, w in enumerate((w_query, w_key, w_value))
                ],
                True,
            ),
            Swap(
                "fsdp",
                (head_dim, width_all),
                [
                    (
                        w_out,
                        lambda ref: ref.at[head_window(), :],
                        lambda buf, place: buf.at[:, part_of(place, part_width)],
                    )
                ],
                True,
            ),
            Swap(
                "tp",
                (1, width_all),
                [
                    (
                        attn_norm[None, :],
                        whole,
                        lambda buf, place: buf.at[:, part_of(place, col_count)],
                    )
                ],
                False,
            ),
            Swap(
                "fsdp",
                (expert_count, width_all),
                [(w_router, whole, lambda buf, place: buf.at[:, part_of(place, part_width)])],
                True,
            ),
        ),
        ships=expert_ships[:first_ships]
        + [Ship("ctx", expert_ids.T, lambda ref, shift: ref, (top_count, tok_rows))],
        lag=2,
    )
    router_pad = jnp.pad(router_full, ((0, lanes - expert_count), (0, 0)))

    def attend(rows, window, held, totals):
        query, key_t, value, seg_rows, seg_cols = held
        scores = nn_dot(query[window, :], key_t[...]) * score_scale
        same_seq = seg_rows[window, :][:, :1] == seg_cols[0:1, :]
        scores = jnp.where(same_seq, scores, -1e30)
        row_peak = jnp.max(scores, axis=1, keepdims=True)
        row_exp = jnp.exp(scores - row_peak)
        row_sum = jnp.sum(row_exp, axis=1, keepdims=True)
        probs_low = (row_exp * (1.0 / row_sum)).astype(slim)
        log_total = jnp.broadcast_to(row_peak + jnp.log(row_sum), (scores.shape[0], lanes))
        return own_queries(window, nn_dot(probs_low, value[...])), log_total.T[:8, :]

    attended_low, log_total, cotangent_all, *second_halves = pack_call(
        sizes,
        own_shape,
        attend,
        2,
        4 * pack_rows * pack_rows * head_dim,
        gathered=cotangent,
        resident=(query_low, key_flip, value_low, segment_rows, segment_cols),
        outs=(Out(head_dim, slim), Out(8, wide, flip=True)),
        keep=True,
        ships=expert_ships[first_ships:second_ships],
    )
    attn_branch, *third_halves = pack_call(
        sizes,
        own_shape,
        lambda window, held, totals: (nn_dot(held[0][window, :], held[1][...]), ()),
        3,
        2 * pack_rows * width_all * head_dim,
        resident=(attended_low, out_weight),
        ships=expert_ships[second_ships:],
    )
    far_halves = first_halves + second_halves + third_halves
    gate_weight, up_weight, down_weight = (
        expert_weight(w, far_halves[i * len(halves) : (i + 1) * len(halves)])
        for i, w in enumerate((w_gate, w_up, w_down))
    )

    resid_in = hidden_in.astype(wide)
    middle = resid_in + attn_branch
    gain_second = ffn_norm.astype(wide)
    inv_second = lax.rsqrt(row_total(jnp.sum(middle * middle, axis=1)) / width_all + norm_eps)[
        :, None
    ]

    def experts(rows, window, held, totals):
        gate_w, up_w, down_w, router_w, ids_ref, cotangent_ref = held
        lane = lax.broadcasted_iota(jnp.int32, (rows.shape[0], lanes), 1)
        logits = jnp.where(lane < expert_count, nt_dot(rows, router_w[...]), -1e30)
        logit_exp = jnp.exp(logits - jnp.max(logits, axis=1, keepdims=True))
        route_probs = logit_exp / jnp.sum(logit_exp, axis=1, keepdims=True)
        block = window.start // tok_rows
        within = pl.multiple_of(window.start - block * tok_rows, rows.shape[0])
        ids = ids_ref[block, :, pl.ds(within, rows.shape[0])].T
        chosen = jnp.zeros((rows.shape[0], lanes), wide)
        for pick in range(ids.shape[1]):
            chosen = chosen + (ids[:, pick : pick + 1] == lane).astype(wide)
        gate_weights = route_probs * chosen
        first_expert = lax.axis_index("ctx") * own_experts
        rows_grad = cotangent_ref[window, :]
        grad_logits = jnp.zeros((rows.shape[0], lanes), wide)
        mixed_list, gate_list, up_list = [], [], []
        for slot in range(own_experts):
            mine = (lane == first_expert + slot).astype(wide)
            gates = jnp.sum(gate_weights * mine, axis=1, keepdims=True)
            gate_proj = nn_dot(rows, gate_w[slot])
            up_proj = nn_dot(rows, up_w[slot])
            grad_mixed = nn_dot(rows_grad, down_w[slot]).astype(slim).astype(wide)
            gate_sigmoid = jax.nn.sigmoid(gate_proj)
            silu = gate_proj * gate_sigmoid
            activity = silu * up_proj
            mixed_list.append((gates * activity).astype(slim))
            grad_gates = jnp.sum(grad_mixed * activity, axis=1, keepdims=True)
            grad_activity = grad_mixed * gates
            gate_list.append(
                (
                    grad_activity * up_proj * (gate_sigmoid + silu * (1.0 - gate_sigmoid))
                ).astype(slim)
            )
            up_list.append((grad_activity * silu).astype(slim))
            grad_logits = grad_logits + gates * grad_gates * (mine - route_probs)
        return (
            jnp.concatenate(mixed_list, axis=1),
            jnp.concatenate(gate_list, axis=1),
            jnp.concatenate(up_list, axis=1),
            grad_logits,
        )

    mixed_low, grad_gate_low, grad_up_low, grad_logits_low, normed_second = pack_call(
        sizes,
        own_shape,
        experts,
        4,
        6 * pack_rows * width_all * own_units,
        gathered=(middle * inv_second * gain_second).astype(slim),
        resident=(gate_weight, up_weight, down_weight, router_pad, ids_all, cotangent_all),
        outs=(
            Out(own_units, slim),
            Out(own_units, slim),
            Out(own_units, slim),
            Out(lanes, slim),
        ),
        keep=True,
    )

    def back(window, held, totals):
        gate_grad, up_grad, logit_grad, gate_w, up_w, router_w, _ = held
        total = nn_dot(logit_grad[window, :], router_w[...])
        for slot in range(own_experts):
            total = total + nt_dot(units_of(gate_grad, window, slot), gate_w[slot])
            total = total + nt_dot(units_of(up_grad, window, slot), up_w[slot])
        return total, ()

    def feature_tile(left, right):
        return lambda window, held: tn_dot(held[left][:, window], held[right][...])

    grad_second, gate_own, gate_far, router_own, router_far = pack_call(
        sizes,
        own_shape,
        back,
        5,
        6 * pack_rows * width_all * own_units,
        resident=(
            grad_gate_low,
            grad_up_low,
            grad_logits_low,
            gate_weight,
            up_weight,
            router_pad,
            normed_second,
        ),
        needed=6,
        makes=(
            Make(own_units, width_all, feature_tile(6, 0), True),
            Make(lanes, width_all, feature_tile(6, 2), True),
        ),
    )

    def by_head(blocks):
        rows = blocks.shape[1]
        summed = jnp.sum(
            blocks.reshape(sharers, local_heads, rows, head_dim).astype(wide), axis=0
        )
        return jnp.swapaxes(summed, 0, 1).reshape(rows, local_heads * head_dim)

    gain_two_grad = jnp.sum(grad_second * middle * inv_second, axis=0)
    second_scaled = grad_second * gain_second
    second_inner = row_total(jnp.sum(second_scaled * middle, axis=1))[:, None]
    grad_middle = (
        cotangent.astype(wide)
        + inv_second * second_scaled
        - middle * inv_second**3 * second_inner / width_all
    )

    half_units = own_units // 2

    def down_tile(half):
        return lambda window, held: tn_dot(
            held[3][:, window], held[4][:, pl.ds(half * half_units, half_units)]
        )

    (
        grad_attended,
        grad_middle_all,
        up_own,
        up_far,
        first_own,
        first_far,
        second_own,
        second_away,
        gate_blocks,
        router_blocks,
    ) = pack_call(
        sizes,
        own_shape,
        lambda rows, window, held, totals: (own_queries(window, nt_dot(rows, held[0][...])),),
        6,
        2 * pack_rows * width_all * (head_dim + own_units),
        gathered=grad_middle.astype(slim),
        resident=(out_weight, normed_second, grad_up_low, cotangent_all, mixed_low),
        outs=(Out(head_dim, slim),),
        keep=True,
        makes=(
            Make(own_units, width_all, feature_tile(1, 2), True),
            Make(half_units, width_all, down_tile(0), True),
            Make(half_units, width_all, down_tile(1), False),
        ),
        deals=(Deal(gate_own, gate_far, own_experts), Deal(router_own, router_far)),
        needed=1,
    )
    grad_gate = gate_blocks.astype(wide)
    grad_router = row_total(
        jnp.sum(router_blocks[:, :, :expert_count].astype(wide), axis=0).T
    )

    def attend_back(window, held, totals):
        mixed_ref, down_w, query, key, key_t, value, grad_att = held[:7]
        seg_rows, seg_cols, log_ref = held[7:10]
        grad_query_rot, grad_key_rot, grad_value, _ = totals
        query_chunk, grad_chunk = query[window, :], grad_att[window, :]
        scores = nt_dot(key[...], query_chunk) * score_scale
        key_segments = jnp.concatenate([seg_rows[...]] * (tok_rows // lanes), axis=1)
        same_seq = key_segments == seg_cols[0:1, window]
        probs = jnp.exp(jnp.where(same_seq, scores, -1e30) - log_ref[0:1, window])
        grad_probs = nt_dot(value[...], grad_chunk)
        inner = jnp.sum(probs * grad_probs, axis=0, keepdims=True)
        grad_scores = (probs * (grad_probs - inner)).astype(slim)
        grad_value[...] += nn_dot(probs.astype(slim), grad_chunk)
        grad_key_rot[...] += nn_dot(grad_scores, query_chunk)
        grad_query_rot[window, :] = nn_dot(key_t[...], grad_scores).T
        total = sum(
            nt_dot(units_of(mixed_ref, window, slot), down_w[slot]) for slot in range(own_experts)
        )
        return total, ()

    def unturn(window, held, stage, totals):
        raws, cos_table, sin_table, gains = held[10:12], held[12], held[13], held[14:16]
        grad_rots, grad_value, gain_sums = totals[:2], totals[2], totals[3]
        cos_rows, sin_rows = cos_table[window, :], sin_table[window, :]
        for which in range(2):
            grad_rot = grad_rots[which][window, :] * score_scale
            raw = raws[which][window, :]
            inverse = lax.rsqrt(jnp.mean(raw * raw, axis=1, keepdims=True) + norm_eps)
            grad_normed = grad_rot * cos_rows + pltpu.roll(grad_rot * sin_rows, head_dim // 2, 1)
            weighted = grad_normed * gains[which][...]
            grad_raw = inverse * weighted - raw * inverse**3 * jnp.mean(
                weighted * raw, axis=1, keepdims=True
            )
            stage[0][window, pl.ds(which * head_dim, head_dim)] = grad_raw.astype(slim)
            gain_sums[pl.ds(which, 1), :] += jnp.sum(
                grad_normed * raw * inverse, axis=0, keepdims=True
            )
        stage[0][window, pl.ds(2 * head_dim, head_dim)] = grad_value[window, :].astype(slim)

    expert_branch, grad_qkv_low, _, _, _, gain_sums, second_far, up_blocks, first_blocks = pack_call(
        sizes,
        own_shape,
        attend_back,
        7,
        2 * pack_rows * width_all * own_units + 10 * pack_rows * pack_rows * head_dim,
        resident=(
            mixed_low,
            down_weight,
            query_low,
            key_low,
            key_flip,
            value_low,
            grad_attended,
            segment_rows,
            segment_cols,
            log_total,
            query_raw,
            key_raw,
            cosine,
            sine,
            gain_query,
            gain_key,
        ),
        outs=(Out(3 * head_dim, slim, late=True),),
        totals=(
            ((pack_rows, head_dim), wide),
            ((pack_rows, head_dim), wide),
            ((pack_rows, head_dim), wide),
            ((8, head_dim), wide),
        ),
        last=unturn,
        ships=(
            Ship(
                "fsdp",
                second_away,
                lambda ref, shift: ref.at[shift - 1],
                (part_width, half_units),
            ),
        ),
        deals=(Deal(up_own, up_far, own_experts), Deal(first_own, first_far, own_experts // 2)),
    )
    hidden_out = (middle + expert_branch).astype(slim)
    grad_up = up_blocks.astype(wide)

    def last_tile(window, held):
        return jnp.concatenate(
            [
                tn_dot(held[2][:, window], held[0][...]),
                tn_dot(held[3][:, window], held[4][...]),
            ],
            axis=1,
        )

    grad_first, last_blocks, second_blocks = pack_call(
        sizes,
        own_shape,
        lambda window, held, totals: (nt_dot(held[0][window, :], held[1][...]), ()),
        8,
        2 * pack_rows * width_all * 7 * head_dim,
        resident=(grad_qkv_low, qkv_weight, normed_first, grad_middle_all, attended_low),
        tiles=Tiles(4 * head_dim, width_all, last_tile),
        deals=(Deal(second_own, second_far, own_experts // 2),),
        needed=2,
    )
    by_halves = (ctx_size, own_experts // 2) + first_blocks.shape[1:]
    grad_down = (
        jnp.concatenate([first_blocks.reshape(by_halves), second_blocks.reshape(by_halves)], axis=1)
        .reshape((expert_count,) + first_blocks.shape[1:])
        .astype(wide)
    )
    grad_query, grad_key, grad_value, grad_out = (
        by_head(last_blocks[:, :, i * head_dim : (i + 1) * head_dim]) for i in range(4)
    )
    grad_out = grad_out.T

    gain_first = attn_norm.astype(wide)
    inv_first = lax.dynamic_slice_in_dim(inv_all, ctx_place * tok_rows, tok_rows, 0)[:, :1]
    gain_one_grad = jnp.sum(grad_first * resid_in * inv_first, axis=0)
    first_scaled = grad_first * gain_first
    first_inner = row_total(jnp.sum(first_scaled * resid_in, axis=1))[:, None]
    grad_hidden = (
        grad_middle + inv_first * first_scaled - resid_in * inv_first**3 * first_inner / width_all
    )

    stream_part = jnp.stack(
        [
            jnp.sum(middle * middle),
            jnp.sum(attn_branch * attn_branch),
            jnp.sum(expert_branch * expert_branch),
        ]
    )
    gain_rows = col_count // lanes
    sums = small_sums(
        sizes,
        jnp.concatenate(
            [
                gain_one_grad.reshape(gain_rows, lanes),
                gain_two_grad.reshape(gain_rows, lanes),
                gain_sums,
                jnp.pad(stream_part[None, :], ((0, 7), (0, lanes - 3))),
            ],
            axis=0,
        ),
        9,
    )
    tp_sums = jnp.sum(sums[:, 2 * gain_rows :], axis=0)
    token_count = tok_rows * packs * ctx_size
    stream_rms = jnp.sqrt(tp_sums[8, :3] / (token_count * width_all))
    return (
        hidden_out,
        grad_hidden,
        sums[:, :gain_rows].reshape(width_all),
        sums[:, gain_rows : 2 * gain_rows].reshape(width_all),
        tp_sums[0],
        tp_sums[1],
        grad_query,
        grad_key,
        grad_value,
        grad_out,
        grad_router,
        grad_gate,
        grad_up,
        grad_down,
        stream_rms,
    )


def solution(mesh):
    return jax.shard_map(
        on_device,
        mesh=mesh,
        in_specs=(
            P(("fsdp", "ctx"), "tp"),
            P(("fsdp", "ctx"), "tp"),
            P("fsdp", None),
            P("fsdp", None),
            P(("fsdp", "ctx"), None),
            P("tp"),
            P("tp"),
            P(),
            P(),
            P("fsdp", "tp"),
            P("fsdp", "tp"),
            P("fsdp", "tp"),
            P("tp", "fsdp"),
            P(None, "fsdp"),
            P(None, "fsdp", "tp"),
            P(None, "fsdp", "tp"),
            P(None, "fsdp", "tp"),
        ),
        out_specs=(
            P(("fsdp", "ctx"), "tp"),
            P(("fsdp", "ctx"), "tp"),
            P(),
            P(),
            P(),
            P(),
            P(("fsdp", "ctx"), "tp"),
            P(("fsdp", "ctx"), "tp"),
            P(("fsdp", "ctx"), "tp"),
            P("tp", ("fsdp", "ctx")),
            P(None, ("fsdp", "ctx")),
            P(None, ("fsdp", "ctx"), "tp"),
            P(None, ("fsdp", "ctx"), "tp"),
            P(None, ("fsdp", "ctx"), "tp"),
            P(),
        ),
        check_vma=False,
    )
```

```python
import jax
import jax.numpy as jnp
from jax import lax
from jax.experimental import pallas as pl
from jax.experimental.pallas import tpu as pltpu
from jax.sharding import PartitionSpec as P

norm_eps = 1e-06
rope_base = 10000.0


def locate(pack_spots, lengths_row):
    seq_ends = jnp.cumsum(lengths_row)
    starts = seq_ends - lengths_row
    segment = jnp.sum((pack_spots[:, None] >= seq_ends[None, :]).astype(jnp.int32), axis=1)
    slot_ids = jnp.arange(lengths_row.shape[0], dtype=jnp.int32)
    seq_begin = jnp.sum(
        jnp.where(segment[:, None] == slot_ids[None, :], starts[None, :], 0), axis=1
    )
    return (segment, pack_spots - seq_begin)


def rope_tables(pack_spots, head_dim):
    half_dim = head_dim // 2
    inv_freq = rope_base ** (-(jnp.arange(half_dim, dtype=jnp.float32) * 2.0 / head_dim))
    angle_grid = pack_spots.astype(jnp.float32)[:, None] * inv_freq[None, :]
    cosine, sine = jnp.cos(angle_grid), jnp.sin(angle_grid)
    return cosine, sine


def full_turn(cosine, sine):
    return jnp.concatenate([cosine, cosine], axis=1), jnp.concatenate([-sine, sine], axis=1)


def unrotate(grad_rot, cosine, sine):
    return grad_rot * cosine + jnp.roll(grad_rot * sine, grad_rot.shape[1] // 2, axis=1)


CHUNKS = 2
MESH_ID = pl.DeviceIdType.MESH
VMEM_LIMIT = 64 * 1000 * 1000


class Pack:
    def __init__(self, ctx_size, tp_size, rows, cols, packs=1):
        self.line = ctx_size // 2
        self.packs = packs
        self.tp_size, self.rows, self.cols = tp_size, rows, cols
        self.chunk = rows // CHUNKS
        self.steps = self.line * CHUNKS
        place = lax.axis_index("ctx")
        self.a, self.b = place // 2, place % 2
        self.t = lax.axis_index("tp")
        self.has_up, self.has_down = self.a < self.line - 1, self.a > 0

    def up(self):
        return {"ctx": (self.a + 1) * 2 + self.b}

    def down(self):
        return {"ctx": (self.a - 1) * 2 + self.b}

    def pair(self):
        return {"ctx": self.a * 2 + (1 - self.b)}

    def sibling(self, shift):
        return {"tp": self.t ^ shift}

    def ctx_peer(self, shift):
        return {"ctx": lax.axis_index("ctx") ^ shift}

    def other_pack(self, shift):
        return {"fsdp": lax.axis_index("fsdp") ^ shift}

    def meet(self, everyone):
        barrier = pltpu.get_barrier_semaphore()

        def greet(device):
            pl.semaphore_signal(barrier, inc=1, device_id=device, device_id_type=MESH_ID)

        if everyone:
            near = 2 * self.line - 1
            for shift in range(1, 2 * self.line):
                greet(self.ctx_peer(shift))
        else:
            near = 1 + jnp.where(self.has_up, 1, 0) + jnp.where(self.has_down, 1, 0)

            @pl.when(self.has_up)
            def _():
                greet(self.up())

            @pl.when(self.has_down)
            def _():
                greet(self.down())

            greet(self.pair())
        for shift in range(1, self.tp_size):
            greet(self.sibling(shift))
        for shift in range(1, self.packs):
            greet(self.other_pack(shift))
        pl.semaphore_wait(barrier, near + self.tp_size + self.packs - 2)

    def row0(self, block, k):
        return pl.multiple_of(block * self.rows + k * self.chunk, self.chunk)

    def region(self, ref, block, k, part):
        return ref.at[
            pl.ds(self.row0(block, k), self.chunk),
            pl.ds(pl.multiple_of(part * self.cols, self.cols), self.cols),
        ]


def pick(table, i):
    result = jnp.int32(table[-1])
    for at, value in enumerate(table[:-1]):
        result = jnp.where(i == at, value, result)
    return result


def remote(src, dst, send_sem, recv_sem, device):
    return pltpu.make_async_remote_copy(
        src_ref=src,
        dst_ref=dst,
        send_sem=send_sem,
        recv_sem=recv_sem,
        device_id=device,
        device_id_type=MESH_ID,
    )


def loop(count, body):
    lax.fori_loop(0, count, lambda i, carry: (body(i), carry)[1], 0)


def gather_scratch(ctx_size, tp_size, rows, cols, dtype):
    line, dma = ctx_size // 2, pltpu.SemaphoreType.DMA
    return [
        pltpu.VMEM((ctx_size * rows, tp_size * cols), dtype),
        dma((2 * line * CHUNKS,)),
        dma((2 * line * CHUNKS,)),
        dma((4 * line * (tp_size - 1) * CHUNKS,)),
        dma((ctx_size * CHUNKS,)),
        dma(((tp_size - 1) * ctx_size * CHUNKS,)),
        dma,
    ]


def gather_steps(pack, src, scratch, everyone, lag, begin, before, compute):
    buf, line_sems, pair_sems, tp_sems, own_sems, sib_sems, local_sem = scratch
    line, t, a, b = pack.line, pack.t, pack.a, pack.b
    ctx_size = 2 * line

    def part(block, k):
        return pack.region(buf, block, k, t)

    def line_copy(piece, block, k, down, dist):
        return remote(
            piece,
            part(block, k),
            line_sems.at[(down * line + dist) * CHUNKS + k],
            own_sems.at[block * CHUNKS + k],
            pack.down() if down else pack.up(),
        )

    def pair_copy(piece, block, k, slot):
        return remote(
            piece,
            part(block, k),
            pair_sems.at[slot * CHUNKS + k],
            own_sems.at[block * CHUNKS + k],
            pack.pair(),
        )

    def tp_copy(piece, block, k, slot, shift):
        return remote(
            piece,
            part(block, k),
            tp_sems.at[(slot * (pack.tp_size - 1) + shift - 1) * CHUNKS + k],
            sib_sems.at[((shift - 1) * ctx_size + block) * CHUNKS + k],
            pack.sibling(shift),
        )

    def send_tp(piece, block, k, slot):
        for shift in range(1, pack.tp_size):
            tp_copy(piece, block, k, slot, shift).start()

    def await_own(block, k):
        piece = part(block, k)
        pair_copy(piece, block, k, 0).wait_recv()

    pack.meet(everyone)
    mine = a * 2 + b
    own_copy = pltpu.make_async_copy(
        src,
        buf.at[
            pl.ds(pl.multiple_of(mine * pack.rows, pack.rows), pack.rows),
            pl.ds(pl.multiple_of(t * pack.cols, pack.cols), pack.cols),
        ],
        local_sem,
    )
    own_copy.start()
    for k in range(CHUNKS):
        piece = src.at[pl.ds(k * pack.chunk, pack.chunk), :]

        @pl.when(pack.has_up)
        def _():
            line_copy(piece, mine, k, 0, 0).start()

        @pl.when(pack.has_down)
        def _():
            line_copy(piece, mine, k, 1, 0).start()

        pair_copy(piece, mine, k, 0).start()
    for k in range(CHUNKS):
        send_tp(src.at[pl.ds(k * pack.chunk, pack.chunk), :], mine, k, 0)
    begin()
    own_copy.wait()

    def ways(dist):
        below, above = a - dist, a + dist
        return (
            (0, below, below >= 0, jnp.logical_and(below >= 0, pack.has_up)),
            (1, above, above < line, jnp.logical_and(above < line, pack.has_down)),
        )

    def from_line(dist, k):
        for down, node, there, onward in ways(dist):
            block = node * 2 + b

            @pl.when(there)
            def _():
                await_own(block, k)

            @pl.when(onward)
            def _():
                line_copy(part(block, k), block, k, down, dist).start()

            @pl.when(there)
            def _():
                pair_copy(part(block, k), block, k, down * line + dist).start()
                send_tp(part(block, k), block, k, down * line + dist)

    def from_pair(dist, k):
        for down, node, there, _ in ways(dist):
            block = node * 2 + (1 - b)
            if down:
                there = jnp.logical_and(there, dist > 0)

            @pl.when(there)
            def _():
                await_own(block, k)
                send_tp(part(block, k), block, k, (2 + down) * line + dist)

    def work(block, k, order):
        for shift in range(1, pack.tp_size):
            piece = pack.region(buf, block, k, t ^ shift)
            remote(
                piece,
                piece,
                tp_sems.at[0],
                sib_sems.at[((shift - 1) * ctx_size + block) * CHUNKS + k],
                pack.sibling(shift),
            ).wait_recv()
        compute(pack.row0(block, k), block * CHUNKS + k, order)

    def step(s):
        dist, k = s // CHUNKS, s % CHUNKS

        @pl.when(s == lag)
        def _():
            before()

        turn = s - lag

        def side(i):
            @pl.when(jnp.logical_and(i == 0, dist + 1 < line))
            def _():
                from_line(dist + 1, k)

            @pl.when(jnp.logical_and(i == 1, s < pack.steps))
            def _():
                from_pair(dist, k)

            late = turn - i
            node, late_k = a ^ (late // CHUNKS), late % CHUNKS

            @pl.when(jnp.logical_and(late >= 0, late < pack.steps))
            def _():
                order = jnp.where(
                    i == 0,
                    jnp.maximum(2 * turn - 1, 0),
                    jnp.minimum(2 * turn, 2 * pack.steps - 1),
                )
                work(node * 2 + jnp.where(i == 0, b, 1 - b), late_k, order)

        loop(2, side)

    loop(pack.steps + 1 + lag, step)

    def drain(s):
        dist, k = s // CHUNKS, s % CHUNKS
        piece = part(0, 0)
        for down, _, there, onward in ways(dist):

            @pl.when(jnp.logical_and(onward, dist < line - 1))
            def _():
                line_copy(piece, 0, k, down, dist).wait_send()

            if down:
                there = jnp.logical_and(there, dist > 0)

            @pl.when(there)
            def _():
                pair_copy(piece, 0, k, down * line + dist).wait_send()
                for shift in range(1, pack.tp_size):
                    tp_copy(piece, 0, k, down * line + dist, shift).wait_send()
                    tp_copy(piece, 0, k, (2 + down) * line + dist, shift).wait_send()

    loop(pack.steps, drain)


def scatter_scratch(ctx_size, tp_size, rows, cols):
    line, dma = ctx_size // 2, pltpu.SemaphoreType.DMA
    low = jnp.bfloat16
    return [
        pltpu.VMEM((ctx_size * rows, tp_size * cols), low),
        pltpu.VMEM(((tp_size - 1) * ctx_size * rows, cols), low),
        pltpu.VMEM((line * rows, cols), low),
        pltpu.VMEM((2 * line * rows, cols), low),
        dma(((tp_size - 1) * ctx_size * CHUNKS,)),
        dma((line * CHUNKS,)),
        dma((line * CHUNKS,)),
        dma(((tp_size - 1) * ctx_size * CHUNKS,)),
        dma((line * CHUNKS,)),
        dma((2 * line * CHUNKS,)),
    ]


def scatter_steps(pack, scratch, everyone, begin, before, compute, jobs, tail, finish):
    (full, sib_buf, pair_buf, line_buf, tp_send, pair_send, line_send, tp_recv, pair_recv, line_recv) = scratch
    line, t, a, b = pack.line, pack.t, pack.a, pack.b
    ctx_size = 2 * line
    wide, low = jnp.float32, jnp.bfloat16
    table = [
        sorted(range(line), key=lambda o, node=node: (-abs(o - node), o)) for node in range(line)
    ]

    def owner(i):
        result = jnp.int32(0)
        for node in range(line):
            for place in range(line):
                here = jnp.logical_and(a == node, i == place)
                result = jnp.where(here, table[node][place], result)
        return result

    def tp_copy(block, k, shift):
        return remote(
            pack.region(full, block, k, t ^ shift),
            sib_buf.at[
                pl.ds(pack.row0((shift - 1) * ctx_size + block, k), pack.chunk), :
            ],
            tp_send.at[((shift - 1) * ctx_size + block) * CHUNKS + k],
            tp_recv.at[((shift - 1) * ctx_size + block) * CHUNKS + k],
            pack.sibling(shift),
        )

    def pair_copy(node, k):
        return remote(
            pack.region(full, node * 2 + (1 - b), k, t),
            pair_buf.at[pl.ds(pack.row0(node, k), pack.chunk), :],
            pair_send.at[node * CHUNKS + k],
            pair_recv.at[node * CHUNKS + k],
            pack.pair(),
        )

    def line_copy(node, k, down):
        return remote(
            pack.region(full, node * 2 + b, k, t),
            line_buf.at[pl.ds(pack.row0(down * line + node, k), pack.chunk), :],
            line_send.at[node * CHUNKS + k],
            line_recv.at[(down * line + node) * CHUNKS + k],
            pack.down() if down else pack.up(),
        )

    def own_part(block, k):
        return full[
            pl.ds(pack.row0(block, k), pack.chunk),
            pl.ds(pl.multiple_of(t * pack.cols, pack.cols), pack.cols),
        ].astype(wide)

    def put_part(block, k, value):
        full[
            pl.ds(pack.row0(block, k), pack.chunk),
            pl.ds(pl.multiple_of(t * pack.cols, pack.cols), pack.cols),
        ] = value.astype(low)

    def landed(ref, block, k):
        return ref[pl.ds(pack.row0(block, k), pack.chunk), :].astype(wide)

    def fill(block):
        row0 = pl.multiple_of(block * pack.rows, pack.rows)
        full[pl.ds(row0, pack.rows), :] = compute(row0)
        for k in range(CHUNKS):
            for shift in range(1, pack.tp_size):
                tp_copy(block, k, shift).start()

    def join(block, k):
        total = own_part(block, k)
        for shift in range(1, pack.tp_size):
            tp_copy(block, k, shift).wait_recv()
            total = total + landed(sib_buf, (shift - 1) * ctx_size + block, k)
        put_part(block, k, total)

    pack.meet(everyone)
    begin()
    before()

    def step(s):
        @pl.when(s < pack.steps)
        def _():
            node, k = owner(s // CHUNKS), s % CHUNKS

            def side(i):
                @pl.when(k == 0)
                def _():
                    fill(node * 2 + jnp.where(i == 0, 1 - b, b))

                jobs(2 * s + i)

            loop(2, side)

        late = s - 1

        @pl.when(jnp.logical_and(late >= 0, late < pack.steps))
        def _():
            node, k = owner(late // CHUNKS), late % CHUNKS

            def side(i):
                join(node * 2 + jnp.where(i == 0, 1 - b, b), k)

                @pl.when(i == 0)
                def _():
                    pair_copy(node, k).start()

            loop(2, side)

        if tail is not None:
            turn = s - (pack.steps - 1)
            share = ctx_size * CHUNKS // 4

            @pl.when(jnp.logical_and(turn >= 0, turn < 4))
            def _():
                loop(share, lambda i: tail(turn * share + i))

        later = s - 4

        @pl.when(later >= 0)
        def _():
            node, k = owner(later // CHUNKS), later % CHUNKS
            pair_copy(node, k).wait_recv()
            put_part(
                node * 2 + b, k, own_part(node * 2 + b, k) + landed(pair_buf, node, k)
            )
            from_below = jnp.logical_and(pack.has_down, node >= a)
            from_above = jnp.logical_and(pack.has_up, node <= a)
            for down, there in ((0, from_below), (1, from_above)):

                @pl.when(there)
                def _():
                    line_copy(node, k, down).wait_recv()
                    put_part(
                        node * 2 + b,
                        k,
                        own_part(node * 2 + b, k) + landed(line_buf, down * line + node, k),
                    )

            @pl.when(node > a)
            def _():
                line_copy(node, k, 0).start()

            @pl.when(node < a)
            def _():
                line_copy(node, k, 1).start()

            @pl.when(node == a)
            def _():
                finish(k, own_part(node * 2 + b, k))

    loop(pack.steps + 4, step)

    def drain(s):
        node, k = s // CHUNKS, s % CHUNKS
        pair_copy(node, k).wait_send()
        for shift in range(1, pack.tp_size):
            tp_copy(node * 2, k, shift).wait_send()
            tp_copy(node * 2 + 1, k, shift).wait_send()

        @pl.when(node > a)
        def _():
            line_copy(node, k, 0).wait_send()

        @pl.when(node < a)
        def _():
            line_copy(node, k, 1).wait_send()

    loop(pack.steps, drain)


ANY = pl.BlockSpec(memory_space=pl.ANY)


def nn_dot(left, right):
    return lax.dot_general(
        left, right, (((1,), (0,)), ((), ())), preferred_element_type=jnp.float32
    )


def nt_dot(left, right):
    return lax.dot_general(
        left, right, (((1,), (1,)), ((), ())), preferred_element_type=jnp.float32
    )


def tn_dot(left, right):
    return lax.dot_general(
        left, right, (((0,), (0,)), ((), ())), preferred_element_type=jnp.float32
    )


class Out:
    def __init__(self, width, dtype, flip=False, late=False):
        self.width, self.dtype, self.flip, self.late = width, dtype, flip, late

    def shape(self, rows):
        return (self.width, rows) if self.flip else (rows, self.width)

    def window(self, ref, window):
        return ref.at[:, window] if self.flip else ref.at[window, :]


class Parts:
    def __init__(self, shape, pieces):
        self.shape, self.pieces = shape, pieces


class Swap:
    def __init__(self, axis, shape, pieces, keep):
        self.axis, self.shape, self.pieces, self.keep = axis, shape, pieces, keep


class Ship:
    def __init__(self, axis, array, source, shape):
        self.axis, self.array, self.source, self.shape = axis, array, source, shape


class Make:
    def __init__(self, width, features, tile, send):
        self.width, self.features, self.tile, self.send = width, features, tile, send


class Deal:
    def __init__(self, own, far, parts=1):
        self.own, self.far, self.parts = own, far, parts
        self.width = own.shape[1] // parts


class Tiles:
    def __init__(self, width, features, tile):
        self.width, self.features, self.tile = width, features, tile


def whole(ref):
    return ref


def pack_call(
    sizes,
    shape,
    piece,
    collective_id,
    flops,
    gathered=None,
    resident=(),
    outs=(),
    totals=(),
    last=None,
    keep=False,
    swaps=(),
    ships=(),
    tiles=None,
    makes=(),
    deals=(),
    lag=0,
    needed=None,
):
    packs, ctx_size, tp_size = sizes
    rows, cols = shape
    all_rows, all_cols = ctx_size * rows, tp_size * cols
    pieces = ctx_size * CHUNKS
    dma = pltpu.SemaphoreType.DMA
    gather = gathered is not None
    if gather:
        base = gather_scratch(ctx_size, tp_size, rows, cols, gathered.dtype)
    else:
        base = scatter_scratch(ctx_size, tp_size, rows, cols)
    axis_size = {"fsdp": packs, "ctx": ctx_size, "tp": tp_size}
    inputs = []

    def enlist(array):
        for i, known in enumerate(inputs):
            if known is array:
                return i
        inputs.append(array)
        return len(inputs) - 1

    if gather:
        enlist(gathered)
    resident = list(resident)
    first_deal = len(resident)
    for deal in deals:
        resident += [deal.own, deal.far]
    parts = [
        r if isinstance(r, Parts) else Parts(r.shape, [(r, whole, whole)]) for r in resident
    ]
    part_list = [[(enlist(x), src, dst) for x, src, dst in p.pieces] for p in parts]
    swap_list = [[(enlist(x), src, dst) for x, src, dst in w.pieces] for w in swaps]
    ship_list = [enlist(ship.array) for ship in ships]
    swap_count = sum(len(w.pieces) * axis_size[w.axis] for w in swaps)
    ship_count = sum(axis_size[ship.axis] for ship in ships)
    kept_swaps = [i for i, w in enumerate(swaps) if w.keep]
    n_out = len(outs) + len(totals) + keep + len(kept_swaps) + len(ships)
    tile_rows = 128
    features = all_cols
    own_features = features // (packs * ctx_size)
    splits = tile_rows // own_features
    own_tiles = features // packs // tile_rows
    far_tiles = (packs - 1) * own_tiles
    assert own_tiles + far_tiles == pieces
    stride = pieces // own_tiles
    deal_order = (4, 1, 6, 2, 5, 3, 7, 0) if own_tiles == 8 else tuple(range(own_tiles))

    def kernel(*refs):
        refs = list(refs)

        def take(count):
            taken = refs[:count]
            del refs[:count]
            return taken

        given = take(len(inputs))
        sum_ref = None if gather else take(1)[0]
        out_refs = take(n_out)
        blocks_ref = None if tiles is None else take(1)[0]
        make_outs = [take(2) for _ in makes]
        deal_outs = take(len(deals))
        scratch = take(len(base))
        held = take(len(resident))
        stage = take(len(outs))
        total_refs = take(len(totals))
        swap_bufs = take(len(swaps))
        (held_sem, out_sem, late_sem, swap_local, swap_send, swap_recv, ship_send, ship_recv) = take(8)
        if tiles is not None:
            tile_stage, tile_far, tile_send, far_recv, block_recv = take(5)
        make_stages = take(len(makes))
        make_send, make_recv, deal_send, deal_recv = take(4)
        over_packs = swaps or ships or tiles is not None or any(make.send for make in makes)
        everyone = tiles is not None or deals or any(ship.axis == "ctx" for ship in ships)
        pack = Pack(ctx_size, tp_size, rows, cols, packs if over_packs else 1)
        mine = {axis: lax.axis_index(axis) for axis in axis_size}
        loads = []
        for target_ref, copies in zip(held, part_list):
            for which, source, target in copies:
                loads.append(
                    pltpu.make_async_copy(
                        source(given[which]), target(target_ref), held_sem.at[len(loads)]
                    )
                )
        swap_copies, swap_sends = [], []
        index = 0
        for swap, buf, copies in zip(swaps, swap_bufs, swap_list):
            for which, source, target in copies:
                here = source(given[which])
                there = target(buf, mine[swap.axis])
                swap_copies.append(pltpu.make_async_copy(here, there, swap_local.at[index]))
                for shift in range(1, axis_size[swap.axis]):
                    slot = index + shift
                    device = {swap.axis: mine[swap.axis] ^ shift}
                    theirs = target(buf, mine[swap.axis] ^ shift)
                    swap_sends.append(
                        (
                            remote(here, there, swap_send.at[slot], swap_recv.at[slot], device),
                            remote(theirs, theirs, swap_send.at[slot], swap_recv.at[slot], device),
                        )
                    )
                index += axis_size[swap.axis]
        late = []
        for i, where in enumerate(kept_swaps):
            late.append((swap_bufs[where], out_refs[len(outs) + len(totals) + keep + i]))
        late_copies = [
            pltpu.make_async_copy(here, there, late_sem.at[i])
            for i, (here, there) in enumerate(late)
        ]
        ship_local, ship_copies = [], []
        index = 0
        for ship, which, landing in zip(ships, ship_list, out_refs[n_out - len(ships) :]):
            place = mine[ship.axis]
            if ship.axis == "ctx":
                here = ship.source(given[which], 0)
                ship_local.append(
                    pltpu.make_async_copy(here, landing.at[place], ship_send.at[index])
                )
            for shift in range(1, axis_size[ship.axis]):
                here = ship.source(given[which], shift)
                there = landing.at[place] if ship.axis == "ctx" else landing.at[shift - 1]
                theirs = landing.at[place ^ shift] if ship.axis == "ctx" else there
                device = {ship.axis: place ^ shift}
                sems = ship_send.at[index + shift], ship_recv.at[index + shift]
                ship_copies.append(
                    (remote(here, there, *sems, device), remote(theirs, theirs, *sems, device))
                )
            index += axis_size[ship.axis]

        prompt = sum(len(copies) for copies in part_list[:needed])

        def await_rest(order):
            @pl.when(order == 0)
            def _():
                for load in loads[prompt:]:
                    load.wait()

        def begin():
            for copy in swap_copies + ship_local:
                copy.start()
            for send, _ in swap_sends + ship_copies:
                send.start()

        def before():
            for ref in total_refs:
                ref[...] = jnp.zeros_like(ref)
            for load in loads[:prompt]:
                load.wait()
            for copy in swap_copies:
                copy.wait()
            for send, receive in swap_sends:
                receive.wait_recv()
            for copy in late_copies:
                copy.start()

        def stores(row0, index):
            window = pl.ds(row0, pack.chunk)
            copies = []
            for i, out in enumerate(outs):
                if not out.late:
                    copies.append((out.window(stage[i], window), out.window(out_refs[i], window), i))
            if keep:
                i = len(outs)
                copies.append(
                    (scratch[0].at[window, :], out_refs[i + len(totals)].at[window, :], i)
                )
            return [
                pltpu.make_async_copy(here, there, out_sem.at[i * pieces + index])
                for here, there, i in copies
            ]

        def put(window, values):
            early = [i for i, out in enumerate(outs) if not out.late]
            for i, value in zip(early, values):
                out = outs[i]
                if out.flip:
                    stage[i][:, window] = value.astype(out.dtype)
                else:
                    stage[i][window, :] = value.astype(out.dtype)

        ahead = 3

        def is_far(order):
            if far_tiles != own_tiles:
                return order < far_tiles
            middle = jnp.logical_and(order >= ahead, order < pieces - ahead)
            return jnp.where(middle, (order - ahead) % 2 == 1, order < ahead)

        def rank(order):
            if far_tiles != own_tiles:
                return jnp.where(order < far_tiles, order, order - far_tiles)
            middle = (order - ahead) // 2
            return jnp.where(
                order < ahead,
                order,
                jnp.where(
                    order >= pieces - ahead,
                    order - far_tiles,
                    jnp.where(is_far(order), ahead + middle, middle),
                ),
            )

        def tile_copy(order, which, shift):
            return remote(
                tile_stage.at[order],
                tile_far.at[which],
                tile_send.at[order * splits],
                far_recv.at[which],
                {"fsdp": mine["fsdp"] ^ shift},
            )

        def block_copy(order, split, owner):
            return remote(
                tile_stage.at[order, pl.ds(split * own_features, own_features), :],
                blocks_ref.at[mine["ctx"]],
                tile_send.at[order * splits + split],
                block_recv.at[mine["ctx"]],
                {"ctx": owner},
            )

        def block_store(order, split):
            return pltpu.make_async_copy(
                tile_stage.at[order, pl.ds(split * own_features, own_features), :],
                blocks_ref.at[mine["ctx"]],
                tile_send.at[order * splits + split],
            )

        def each_block(order, go_away, stay):
            for split in range(splits):
                owner = ((mine["ctx"] // splits) ^ pick(deal_order, rank(order))) * splits + split

                @pl.when(owner != mine["ctx"])
                def _():
                    go_away(order, split, owner)

                @pl.when(owner == mine["ctx"])
                def _():
                    stay(order, split)

        def make_tile(order):
            if tiles is None:
                return
            far, which = is_far(order), rank(order)
            shift = jnp.where(far, which // own_tiles + 1, 0)
            place = (mine["ctx"] // splits) ^ pick(deal_order, which % own_tiles)
            first = ((mine["fsdp"] ^ shift) * own_tiles + place) * tile_rows
            value = tiles.tile(pl.ds(pl.multiple_of(first, tile_rows), tile_rows), held)

            @pl.when(far)
            def _():
                tile_stage[order] = value.astype(jnp.bfloat16)
                tile_copy(order, which, shift).start()

            @pl.when(jnp.logical_not(far))
            def _():
                total = value
                for other in range(packs - 1):
                    slot = other * own_tiles + which
                    tile_copy(order, slot, 1).wait_recv()
                    total = total + tile_far[slot].astype(jnp.float32)
                tile_stage[order] = total.astype(jnp.bfloat16)
                each_block(
                    order,
                    lambda *where: block_copy(*where).start(),
                    lambda *where: block_store(*where).start(),
                )

        def finish_tiles():
            if tiles is None:
                return

            def sent(order):
                @pl.when(is_far(order))
                def _():
                    tile_copy(order, 0, 1).wait_send()

                @pl.when(jnp.logical_not(is_far(order)))
                def _():
                    each_block(
                        order,
                        lambda *where: block_copy(*where).wait_send(),
                        lambda *where: block_store(*where).wait(),
                    )

            loop(pieces, sent)
            for shift in range(1, ctx_size):
                landed = blocks_ref.at[mine["ctx"] ^ shift]
                remote(
                    landed,
                    landed,
                    tile_send.at[0],
                    block_recv.at[mine["ctx"] ^ shift],
                    {"ctx": mine["ctx"] ^ shift},
                ).wait_recv()

        def make_copies(i, order):
            far = order < far_tiles
            which = jnp.where(far, order, order - far_tiles)
            shift = jnp.where(far, which // own_tiles + 1, 0)
            window = pl.ds(
                pl.multiple_of(which % own_tiles * tile_rows, tile_rows), tile_rows
            )
            here = make_stages[i].at[order]
            sem = make_send.at[i * pieces + order]
            own_out, far_out = make_outs[i]
            slot = jnp.maximum(shift - 1, 0)
            send = remote(
                here,
                far_out.at[slot, window, :],
                sem,
                make_recv.at[i * pieces + order],
                {"fsdp": mine["fsdp"] ^ shift},
            )
            away = pltpu.make_async_copy(here, far_out.at[slot, window, :], sem)
            stay = pltpu.make_async_copy(here, own_out.at[window, :], sem)
            return far, shift, which % own_tiles, send, away, stay

        def make_parts(order):
            for i, make in enumerate(makes):
                far, shift, place, send, away, stay = make_copies(i, order)
                first = ((mine["fsdp"] ^ shift) * own_tiles + place) * tile_rows
                value = make.tile(pl.ds(pl.multiple_of(first, tile_rows), tile_rows), held)
                make_stages[i][order] = value.astype(jnp.bfloat16)

                @pl.when(far)
                def _():
                    (send if make.send else away).start()

                @pl.when(jnp.logical_not(far))
                def _():
                    stay.start()

        def finish_parts():
            def sent(order):
                for i, make in enumerate(makes):
                    far, _, _, send, away, stay = make_copies(i, order)

                    @pl.when(far)
                    def _():
                        if make.send:
                            send.wait_send()
                            send.wait_recv()
                        else:
                            away.wait()

                    @pl.when(jnp.logical_not(far))
                    def _():
                        stay.wait()

            loop(pieces, sent)

        deal_first = [sum(d.parts for d in deals[:i]) for i in range(len(deals))]

        def deal_blocks(i, turn, go_away, stay):
            own_buf, landing = held[first_deal + 2 * i], deal_outs[i]
            parts, width = deals[i].parts, deals[i].width
            for split in range(splits):
                owner = ((mine["ctx"] // splits) ^ pick(deal_order, turn)) * splits + split
                window = pl.ds(pl.multiple_of(owner * own_features, own_features), own_features)
                copies = []
                for part in range(parts):
                    here = own_buf.at[window, pl.ds(part * width, width)]
                    there = landing.at[mine["ctx"] * parts + part]
                    sem = deal_send.at[
                        (deal_first[i] + part) * own_tiles * splits + turn * splits + split
                    ]
                    arrived = deal_recv.at[(deal_first[i] + part) * ctx_size + mine["ctx"]]
                    copies.append((here, there, sem, arrived))

                @pl.when(owner != mine["ctx"])
                def _():
                    for copy in copies:
                        go_away(remote(*copy, {"ctx": owner}))

                @pl.when(owner == mine["ctx"])
                def _():
                    for here, there, sem, _ in copies:
                        stay(pltpu.make_async_copy(here, there, sem))

        def deal_out(order):
            if not deals:
                return

            @pl.when(order % stride == 0)
            def _():
                turn = order // stride
                place = (mine["ctx"] // splits) ^ pick(deal_order, turn)
                window = pl.ds(pl.multiple_of(place * tile_rows, tile_rows), tile_rows)
                for i in range(len(deals)):
                    own_buf, far_buf = held[first_deal + 2 * i], held[first_deal + 2 * i + 1]
                    total = own_buf[window, :].astype(jnp.float32)
                    for other in range(packs - 1):
                        total = total + far_buf[other, window, :].astype(jnp.float32)
                    own_buf[window, :] = total.astype(jnp.bfloat16)
                    deal_blocks(i, turn, lambda copy: copy.start(), lambda copy: copy.start())

        def finish_deals():
            if not deals:
                return

            def sent(turn):
                for i in range(len(deals)):
                    deal_blocks(i, turn, lambda copy: copy.wait_send(), lambda copy: copy.wait())

            loop(own_tiles, sent)
            for i in range(len(deals)):
                for shift in range(1, ctx_size):
                    place = mine["ctx"] ^ shift
                    for part in range(deals[i].parts):
                        landed = deal_outs[i].at[place * deals[i].parts + part]
                        sem = deal_recv.at[(deal_first[i] + part) * ctx_size + place]
                        remote(landed, landed, deal_send.at[0], sem, {"ctx": place}).wait_recv()

        for load in loads:
            load.start()
        if gather:

            def compute(row0, index, order):
                window = pl.ds(row0, pack.chunk)
                put(window, piece(scratch[0][window, :], window, held + swap_bufs, total_refs))
                for store in stores(row0, index):
                    store.start()
                await_rest(order)
                deal_out(order)
                make_tile(order)
                make_parts(order)

            gather_steps(pack, given[0], scratch, everyone, lag, begin, before, compute)
        else:

            def compute(row0):
                window = pl.ds(row0, pack.rows)
                rows_value, values = piece(window, held + swap_bufs, total_refs)
                put(window, values)
                return rows_value.astype(jnp.bfloat16)

            def jobs(order):
                await_rest(order)
                deal_out(order)
                make_tile(order)
                make_parts(order)

            def finish(k, total):
                sum_ref[pl.ds(pl.multiple_of(k * pack.chunk, pack.chunk), pack.chunk), :] = total

            def tail(i):
                last(
                    pl.ds(pl.multiple_of(i * pack.chunk, pack.chunk), pack.chunk),
                    held + swap_bufs,
                    stage,
                    total_refs,
                )

            scatter_steps(
                pack, scratch, everyone, begin, before, compute, jobs,
                None if last is None else tail, finish,
            )
        ends = []
        for i, out in enumerate(outs):
            if out.late:
                ends.append((stage[i], out_refs[i]))
        for i, ref in enumerate(total_refs):
            ends.append((ref, out_refs[len(outs) + i]))
        end_copies = [
            pltpu.make_async_copy(here, there, late_sem.at[len(late) + i])
            for i, (here, there) in enumerate(ends)
        ]
        for copy in end_copies:
            copy.start()

        def drain(index):
            for store in stores(pl.multiple_of(index * pack.chunk, pack.chunk), index):
                store.wait()

        loop(pieces, drain)
        finish_tiles()
        finish_parts()
        finish_deals()
        for copy in late_copies + end_copies + ship_local:
            copy.wait()
        for send, _ in swap_sends:
            send.wait_send()
        for send, receive in ship_copies:
            send.wait_send()
            receive.wait_recv()

    low = jnp.bfloat16
    shapes = [jax.ShapeDtypeStruct(out.shape(all_rows), out.dtype) for out in outs]
    shapes += [jax.ShapeDtypeStruct(dims, dtype) for dims, dtype in totals]
    if keep:
        shapes.append(jax.ShapeDtypeStruct((all_rows, all_cols), gathered.dtype))
    shapes += [jax.ShapeDtypeStruct(swaps[i].shape, low) for i in kept_swaps]
    for ship in ships:
        slots = ctx_size if ship.axis == "ctx" else packs - 1
        shapes.append(jax.ShapeDtypeStruct((slots,) + ship.shape, ship.array.dtype))
    if tiles is not None:
        shapes.append(jax.ShapeDtypeStruct((ctx_size, own_features, tiles.width), low))
    part_features = features // packs
    for make in makes:
        shapes.append(jax.ShapeDtypeStruct((part_features, make.width), low))
        shapes.append(jax.ShapeDtypeStruct((packs - 1, part_features, make.width), low))
    for deal in deals:
        shapes.append(
            jax.ShapeDtypeStruct((ctx_size * deal.parts, own_features, deal.width), low)
        )
    out_specs = [ANY] * len(shapes)
    if not gather:
        shapes = [jax.ShapeDtypeStruct(shape, jnp.float32)] + shapes
        out_specs = [pl.BlockSpec(memory_space=pltpu.VMEM)] + out_specs
    tile_scratch = []
    if tiles is not None:
        tile_scratch = [
            pltpu.VMEM((pieces, tile_rows, tiles.width), low),
            pltpu.VMEM((far_tiles, tile_rows, tiles.width), low),
            dma((pieces * splits,)),
            dma((far_tiles,)),
            dma((ctx_size,)),
        ]
    return pl.pallas_call(
        kernel,
        out_shape=tuple(shapes),
        in_specs=[ANY] * len(inputs),
        out_specs=tuple(out_specs),
        scratch_shapes=base
        + [pltpu.VMEM(p.shape, p.pieces[0][0].dtype) for p in parts]
        + [pltpu.VMEM(out.shape(all_rows), out.dtype) for out in outs]
        + [pltpu.VMEM(dims, dtype) for dims, dtype in totals]
        + [pltpu.VMEM(swap.shape, low) for swap in swaps]
        + [
            dma((max(1, sum(len(p.pieces) for p in parts)),)),
            dma(((len(outs) + 1) * pieces,)),
            dma((len(kept_swaps) + len(outs) + len(totals) + 1,)),
            dma((max(1, swap_count),)),
            dma((max(1, swap_count),)),
            dma((max(1, swap_count),)),
            dma((max(1, ship_count),)),
            dma((max(1, ship_count),)),
        ]
        + tile_scratch
        + [pltpu.VMEM((pieces, tile_rows, make.width), low) for make in makes]
        + [
            dma((max(1, len(makes)) * pieces,)),
            dma((max(1, len(makes)) * pieces,)),
            dma((max(1, sum(deal.parts for deal in deals)) * own_tiles * splits,)),
            dma((max(1, sum(deal.parts for deal in deals)) * ctx_size,)),
        ],
        compiler_params=pltpu.CompilerParams(
            collective_id=collective_id, has_side_effects=True, vmem_limit_bytes=VMEM_LIMIT
        ),
        cost_estimate=pl.CostEstimate(
            flops=flops, bytes_accessed=8 * all_rows * all_cols, transcendentals=0
        ),
    )(*inputs)


def small_sums(sizes, tensor, collective_id):
    packs, ctx_size, tp_size = sizes
    dma = pltpu.SemaphoreType.DMA
    count = tensor.shape[0]

    def kernel(src, out_ref, ctx_buf, mid, rest_buf, send_sems, recv_sems):
        f, c, t = (lax.axis_index(axis) for axis in ("fsdp", "ctx", "tp"))
        ctx_peers = [(shift, {"ctx": c ^ shift}) for shift in range(1, ctx_size)]
        rest_peers = [
            (shift * tp_size + turn, {"fsdp": f ^ shift, "tp": t ^ turn})
            for shift in range(packs)
            for turn in range(tp_size)
            if shift or turn
        ]
        barrier = pltpu.get_barrier_semaphore()
        for _, device in ctx_peers + rest_peers:
            pl.semaphore_signal(barrier, inc=1, device_id=device, device_id_type=MESH_ID)
        pl.semaphore_wait(barrier, len(ctx_peers) + len(rest_peers))

        def exchange(source, buf, peers, offset):
            copies = [
                remote(
                    source,
                    buf.at[slot],
                    send_sems.at[offset + slot],
                    recv_sems.at[offset + slot],
                    device,
                )
                for slot, device in peers
            ]
            for copy in copies:
                copy.start()
            for copy in copies:
                copy.wait()

        exchange(src, ctx_buf, ctx_peers, 0)
        total = src[...]
        for slot, _ in ctx_peers:
            total = total + ctx_buf[slot]
        mid[...] = total
        exchange(mid, rest_buf, rest_peers, ctx_size)
        rest_buf[0] = total
        for turn in range(tp_size):
            part = rest_buf[turn]
            for shift in range(1, packs):
                part = part + rest_buf[shift * tp_size + turn]
            out_ref[t ^ turn] = part

    return pl.pallas_call(
        kernel,
        out_shape=jax.ShapeDtypeStruct((tp_size, count, tensor.shape[1]), jnp.float32),
        in_specs=[pl.BlockSpec(memory_space=pltpu.VMEM)],
        out_specs=pl.BlockSpec(memory_space=pltpu.VMEM),
        scratch_shapes=[
            pltpu.VMEM((ctx_size,) + tensor.shape, jnp.float32),
            pltpu.VMEM(tensor.shape, jnp.float32),
            pltpu.VMEM((packs * tp_size,) + tensor.shape, jnp.float32),
            dma((ctx_size + packs * tp_size,)),
            dma((ctx_size + packs * tp_size,)),
        ],
        compiler_params=pltpu.CompilerParams(collective_id=collective_id, has_side_effects=True),
    )(tensor)

def on_device(
    hidden_in,
    cotangent,
    positions,
    seq_lengths,
    expert_ids,
    attn_norm,
    ffn_norm,
    query_norm,
    key_norm,
    w_query,
    w_key,
    w_value,
    w_out,
    w_router,
    w_gate,
    w_up,
    w_down,
):
    tok_rows, col_count = hidden_in.shape
    packs, ctx_size, tp_size = (lax.axis_size(axis) for axis in ("fsdp", "ctx", "tp"))
    sizes = (packs, ctx_size, tp_size)
    own_shape = (tok_rows, col_count)
    ctx_place = lax.axis_index("ctx")
    width_all = col_count * tp_size
    part_width = width_all // packs
    pack_rows = tok_rows * ctx_size
    head_dim = query_norm.shape[0]
    local_heads = w_query.shape[1] // head_dim
    expert_count, hidden_units = w_gate.shape[0], w_gate.shape[2]
    own_experts = expert_count // ctx_size
    own_units = own_experts * hidden_units
    top_count = expert_ids.shape[1]
    sharers = ctx_size // local_heads
    score_scale = head_dim ** (-0.5)
    wide = jnp.float32
    slim = jnp.bfloat16
    lanes = 128

    def row_total(tensor):
        return lax.psum(tensor, "tp")

    def units_of(ref, window, slot):
        return ref[window, pl.ds(slot * hidden_units, hidden_units)]

    def own_queries(window, value):
        if sharers == 1:
            return value
        share = window.start // (pack_rows // sharers)
        return jnp.where(share == lax.axis_index("ctx") // local_heads, value, 0.0)

    def head_window():
        return pl.ds(
            pl.multiple_of(lax.axis_index("ctx") % local_heads * head_dim, head_dim), head_dim
        )

    def part_of(place, size):
        return pl.ds(pl.multiple_of(place * size, size), size)

    half_rows = part_width // 2

    def half_ship(weight, slot, half):
        return Ship(
            "fsdp",
            weight,
            lambda ref, shift: ref.at[
                lax.axis_index("ctx") * own_experts + slot,
                pl.ds(half * half_rows, half_rows),
                :,
            ],
            (half_rows, hidden_units),
        )

    halves = [(slot, half) for slot in range(own_experts) for half in range(2)]
    expert_ships = [half_ship(w, *which) for w in (w_gate, w_up, w_down) for which in halves]
    first_ships = len(expert_ships) // 4
    second_ships = first_ships + (len(expert_ships) - first_ships) // 2

    def expert_weight(weight, far):
        pieces = [
            (
                weight,
                lambda ref: ref.at[pl.ds(lax.axis_index("ctx") * own_experts, own_experts), :, :],
                lambda buf: buf.at[:, part_of(lax.axis_index("fsdp"), part_width), :],
            )
        ]
        for (slot, half), array in zip(halves, far):
            for shift in range(1, packs):
                pieces.append(
                    (
                        array,
                        lambda ref, shift=shift: ref.at[shift - 1],
                        lambda buf, slot=slot, half=half, shift=shift: buf.at[
                            slot,
                            part_of((lax.axis_index("fsdp") ^ shift) * 2 + half, half_rows),
                            :,
                        ],
                    )
                )
        return Parts((own_experts, width_all, hidden_units), pieces)

    segment, place = locate(positions[0], seq_lengths[0])
    cosine, sine = rope_tables(place, head_dim)
    segment_rows = jnp.broadcast_to(segment[:, None], (pack_rows, lanes))
    segment_cols = jnp.broadcast_to(segment[None, :], (8, pack_rows))

    def project(rows, window, held, totals):
        cos_table, sin_table, gain_q, gain_k, weight, _, gain, _ = held
        hidden = rows.astype(wide)
        inverse = lax.rsqrt(jnp.mean(hidden * hidden, axis=1, keepdims=True) + norm_eps)
        normed = (hidden * inverse * gain[...].astype(wide)).astype(slim)
        raw = nn_dot(normed, weight[...])
        cos_rows, sin_rows = full_turn(cos_table[window, :], sin_table[window, :])

        def prepare(raw_proj, gain_vec):
            inv = lax.rsqrt(jnp.mean(raw_proj * raw_proj, axis=1, keepdims=True) + norm_eps)
            scaled = raw_proj * inv * gain_vec[...]
            return scaled * cos_rows + pltpu.roll(scaled, head_dim // 2, 1) * sin_rows

        query_raw = raw[:, :head_dim]
        key_raw = raw[:, head_dim : 2 * head_dim]
        key_turned = prepare(key_raw, gain_k)
        return (
            normed,
            jnp.broadcast_to(inverse, (rows.shape[0], lanes)),
            query_raw,
            key_raw,
            prepare(query_raw, gain_q),
            key_turned,
            key_turned.T,
            raw[:, 2 * head_dim :],
        )

    gain_query = query_norm.astype(wide)[None, :]
    gain_key = key_norm.astype(wide)[None, :]
    (
        normed_first,
        inv_all,
        query_raw,
        key_raw,
        query_low,
        key_low,
        key_flip,
        value_low,
        qkv_weight,
        out_weight,
        router_full,
        *first_halves,
        ids_all,
    ) = pack_call(
        sizes,
        own_shape,
        project,
        1,
        6 * pack_rows * width_all * head_dim,
        gathered=hidden_in,
        resident=(cosine, sine, gain_query, gain_key),
        outs=(
            Out(width_all, slim),
            Out(lanes, wide),
            Out(head_dim, wide),
            Out(head_dim, wide),
            Out(head_dim, slim),
            Out(head_dim, slim),
            Out(head_dim, slim, flip=True),
            Out(head_dim, slim),
        ),
        swaps=(
            Swap(
                "fsdp",
                (width_all, 3 * head_dim),
                [
                    (
                        w,
                        lambda ref: ref.at[:, head_window()],
                        lambda buf, place, i=i: buf.at[
                            part_of(place, part_width), pl.ds(i * head_dim, head_dim)
                        ],
                    )
                    for i, w in enumerate((w_query, w_key, w_value))
                ],
                True,
            ),
            Swap(
                "fsdp",
                (head_dim, width_all),
                [
                    (
                        w_out,
                        lambda ref: ref.at[head_window(), :],
                        lambda buf, place: buf.at[:, part_of(place, part_width)],
                    )
                ],
                True,
            ),
            Swap(
                "tp",
                (1, width_all),
                [
                    (
                        attn_norm[None, :],
                        whole,
                        lambda buf, place: buf.at[:, part_of(place, col_count)],
                    )
                ],
                False,
            ),
            Swap(
                "fsdp",
                (expert_count, width_all),
                [(w_router, whole, lambda buf, place: buf.at[:, part_of(place, part_width)])],
                True,
            ),
        ),
        ships=expert_ships[:first_ships]
        + [Ship("ctx", expert_ids.T, lambda ref, shift: ref, (top_count, tok_rows))],
        lag=2,
    )
    router_pad = jnp.pad(router_full, ((0, lanes - expert_count), (0, 0)))

    def attend(rows, window, held, totals):
        query, key_t, value, seg_rows, seg_cols = held
        scores = nn_dot(query[window, :], key_t[...]) * score_scale
        same_seq = seg_rows[window, :][:, :1] == seg_cols[0:1, :]
        scores = jnp.where(same_seq, scores, -1e30)
        row_peak = jnp.max(scores, axis=1, keepdims=True)
        row_exp = jnp.exp(scores - row_peak)
        row_sum = jnp.sum(row_exp, axis=1, keepdims=True)
        probs_low = (row_exp * (1.0 / row_sum)).astype(slim)
        log_total = jnp.broadcast_to(row_peak + jnp.log(row_sum), (scores.shape[0], lanes))
        return own_queries(window, nn_dot(probs_low, value[...])), log_total.T[:8, :]

    attended_low, log_total, cotangent_all, *second_halves = pack_call(
        sizes,
        own_shape,
        attend,
        2,
        4 * pack_rows * pack_rows * head_dim,
        gathered=cotangent,
        resident=(query_low, key_flip, value_low, segment_rows, segment_cols),
        outs=(Out(head_dim, slim), Out(8, wide, flip=True)),
        keep=True,
        ships=expert_ships[first_ships:second_ships],
    )
    attn_branch, *third_halves = pack_call(
        sizes,
        own_shape,
        lambda window, held, totals: (nn_dot(held[0][window, :], held[1][...]), ()),
        3,
        2 * pack_rows * width_all * head_dim,
        resident=(attended_low, out_weight),
        ships=expert_ships[second_ships:],
    )
    far_halves = first_halves + second_halves + third_halves
    gate_weight, up_weight, down_weight = (
        expert_weight(w, far_halves[i * len(halves) : (i + 1) * len(halves)])
        for i, w in enumerate((w_gate, w_up, w_down))
    )

    resid_in = hidden_in.astype(wide)
    middle = resid_in + attn_branch
    gain_second = ffn_norm.astype(wide)
    inv_second = lax.rsqrt(row_total(jnp.sum(middle * middle, axis=1)) / width_all + norm_eps)[
        :, None
    ]

    def experts(rows, window, held, totals):
        gate_w, up_w, down_w, router_w, ids_ref, cotangent_ref = held
        lane = lax.broadcasted_iota(jnp.int32, (rows.shape[0], lanes), 1)
        logits = jnp.where(lane < expert_count, nt_dot(rows, router_w[...]), -1e30)
        logit_exp = jnp.exp(logits - jnp.max(logits, axis=1, keepdims=True))
        route_probs = logit_exp / jnp.sum(logit_exp, axis=1, keepdims=True)
        block = window.start // tok_rows
        within = pl.multiple_of(window.start - block * tok_rows, rows.shape[0])
        ids = ids_ref[block, :, pl.ds(within, rows.shape[0])].T
        chosen = jnp.zeros((rows.shape[0], lanes), wide)
        for pick in range(ids.shape[1]):
            chosen = chosen + (ids[:, pick : pick + 1] == lane).astype(wide)
        gate_weights = route_probs * chosen
        first_expert = lax.axis_index("ctx") * own_experts
        rows_grad = cotangent_ref[window, :]
        grad_logits = jnp.zeros((rows.shape[0], lanes), wide)
        mixed_list, gate_list, up_list = [], [], []
        for slot in range(own_experts):
            mine = (lane == first_expert + slot).astype(wide)
            gates = jnp.sum(gate_weights * mine, axis=1, keepdims=True)
            gate_proj = nn_dot(rows, gate_w[slot])
            up_proj = nn_dot(rows, up_w[slot])
            grad_mixed = nn_dot(rows_grad, down_w[slot]).astype(slim).astype(wide)
            gate_sigmoid = jax.nn.sigmoid(gate_proj)
            silu = gate_proj * gate_sigmoid
            activity = silu * up_proj
            mixed_list.append((gates * activity).astype(slim))
            grad_gates = jnp.sum(grad_mixed * activity, axis=1, keepdims=True)
            grad_activity = grad_mixed * gates
            gate_list.append(
                (
                    grad_activity * up_proj * (gate_sigmoid + silu * (1.0 - gate_sigmoid))
                ).astype(slim)
            )
            up_list.append((grad_activity * silu).astype(slim))
            grad_logits = grad_logits + gates * grad_gates * (mine - route_probs)
        return (
            jnp.concatenate(mixed_list, axis=1),
            jnp.concatenate(gate_list, axis=1),
            jnp.concatenate(up_list, axis=1),
            grad_logits,
        )

    mixed_low, grad_gate_low, grad_up_low, grad_logits_low, normed_second = pack_call(
        sizes,
        own_shape,
        experts,
        4,
        6 * pack_rows * width_all * own_units,
        gathered=(middle * inv_second * gain_second).astype(slim),
        resident=(gate_weight, up_weight, down_weight, router_pad, ids_all, cotangent_all),
        outs=(
            Out(own_units, slim),
            Out(own_units, slim),
            Out(own_units, slim),
            Out(lanes, slim),
        ),
        keep=True,
    )

    def back(window, held, totals):
        gate_grad, up_grad, logit_grad, gate_w, up_w, router_w, _ = held
        total = nn_dot(logit_grad[window, :], router_w[...])
        for slot in range(own_experts):
            total = total + nt_dot(units_of(gate_grad, window, slot), gate_w[slot])
            total = total + nt_dot(units_of(up_grad, window, slot), up_w[slot])
        return total, ()

    def feature_tile(left, right):
        return lambda window, held: tn_dot(held[left][:, window], held[right][...])

    grad_second, gate_own, gate_far, router_own, router_far = pack_call(
        sizes,
        own_shape,
        back,
        5,
        6 * pack_rows * width_all * own_units,
        resident=(
            grad_gate_low,
            grad_up_low,
            grad_logits_low,
            gate_weight,
            up_weight,
            router_pad,
            normed_second,
        ),
        needed=6,
        makes=(
            Make(own_units, width_all, feature_tile(6, 0), True),
            Make(lanes, width_all, feature_tile(6, 2), True),
        ),
    )

    def by_head(blocks):
        rows = blocks.shape[1]
        summed = jnp.sum(
            blocks.reshape(sharers, local_heads, rows, head_dim).astype(wide), axis=0
        )
        return jnp.swapaxes(summed, 0, 1).reshape(rows, local_heads * head_dim)

    gain_two_grad = jnp.sum(grad_second * middle * inv_second, axis=0)
    second_scaled = grad_second * gain_second
    second_inner = row_total(jnp.sum(second_scaled * middle, axis=1))[:, None]
    grad_middle = (
        cotangent.astype(wide)
        + inv_second * second_scaled
        - middle * inv_second**3 * second_inner / width_all
    )

    half_units = own_units // 2

    def down_tile(half):
        return lambda window, held: tn_dot(
            held[3][:, window], held[4][:, pl.ds(half * half_units, half_units)]
        )

    (
        grad_attended,
        grad_middle_all,
        up_own,
        up_far,
        first_own,
        first_far,
        second_own,
        second_away,
        gate_blocks,
        router_blocks,
    ) = pack_call(
        sizes,
        own_shape,
        lambda rows, window, held, totals: (own_queries(window, nt_dot(rows, held[0][...])),),
        6,
        2 * pack_rows * width_all * (head_dim + own_units),
        gathered=grad_middle.astype(slim),
        resident=(out_weight, normed_second, grad_up_low, cotangent_all, mixed_low),
        outs=(Out(head_dim, slim),),
        keep=True,
        makes=(
            Make(own_units, width_all, feature_tile(1, 2), True),
            Make(half_units, width_all, down_tile(0), True),
            Make(half_units, width_all, down_tile(1), False),
        ),
        deals=(Deal(gate_own, gate_far, own_experts), Deal(router_own, router_far)),
        needed=1,
    )
    grad_gate = gate_blocks.astype(wide)
    grad_router = row_total(
        jnp.sum(router_blocks[:, :, :expert_count].astype(wide), axis=0).T
    )

    def attend_back(window, held, totals):
        mixed_ref, down_w, query, key, key_t, value, grad_att = held[:7]
        seg_rows, seg_cols, log_ref = held[7:10]
        grad_query_rot, grad_key_rot, grad_value, _ = totals
        query_chunk, grad_chunk = query[window, :], grad_att[window, :]
        scores = nt_dot(key[...], query_chunk) * score_scale
        key_segments = jnp.concatenate([seg_rows[...]] * (tok_rows // lanes), axis=1)
        same_seq = key_segments == seg_cols[0:1, window]
        probs = jnp.exp(jnp.where(same_seq, scores, -1e30) - log_ref[0:1, window])
        grad_probs = nt_dot(value[...], grad_chunk)
        inner = jnp.sum(probs * grad_probs, axis=0, keepdims=True)
        grad_scores = (probs * (grad_probs - inner)).astype(slim)
        grad_value[...] += nn_dot(probs.astype(slim), grad_chunk)
        grad_key_rot[...] += nn_dot(grad_scores, query_chunk)
        grad_query_rot[window, :] = nn_dot(key_t[...], grad_scores).T
        total = sum(
            nt_dot(units_of(mixed_ref, window, slot), down_w[slot]) for slot in range(own_experts)
        )
        return total, ()

    def unturn(window, held, stage, totals):
        raws, cos_table, sin_table, gains = held[10:12], held[12], held[13], held[14:16]
        grad_rots, grad_value, gain_sums = totals[:2], totals[2], totals[3]
        cos_rows, sin_rows = full_turn(cos_table[window, :], sin_table[window, :])
        for which in range(2):
            grad_rot = grad_rots[which][window, :] * score_scale
            raw = raws[which][window, :]
            inverse = lax.rsqrt(jnp.mean(raw * raw, axis=1, keepdims=True) + norm_eps)
            grad_normed = grad_rot * cos_rows + pltpu.roll(grad_rot * sin_rows, head_dim // 2, 1)
            weighted = grad_normed * gains[which][...]
            grad_raw = inverse * weighted - raw * inverse**3 * jnp.mean(
                weighted * raw, axis=1, keepdims=True
            )
            stage[0][window, pl.ds(which * head_dim, head_dim)] = grad_raw.astype(slim)
            gain_sums[pl.ds(which, 1), :] += jnp.sum(
                grad_normed * raw * inverse, axis=0, keepdims=True
            )
        stage[0][window, pl.ds(2 * head_dim, head_dim)] = grad_value[window, :].astype(slim)

    expert_branch, grad_qkv_low, _, _, _, gain_sums, second_far, up_blocks, first_blocks = pack_call(
        sizes,
        own_shape,
        attend_back,
        7,
        2 * pack_rows * width_all * own_units + 10 * pack_rows * pack_rows * head_dim,
        resident=(
            mixed_low,
            down_weight,
            query_low,
            key_low,
            key_flip,
            value_low,
            grad_attended,
            segment_rows,
            segment_cols,
            log_total,
            query_raw,
            key_raw,
            cosine,
            sine,
            gain_query,
            gain_key,
        ),
        outs=(Out(3 * head_dim, slim, late=True),),
        totals=(
            ((pack_rows, head_dim), wide),
            ((pack_rows, head_dim), wide),
            ((pack_rows, head_dim), wide),
            ((8, head_dim), wide),
        ),
        last=unturn,
        ships=(
            Ship(
                "fsdp",
                second_away,
                lambda ref, shift: ref.at[shift - 1],
                (part_width, half_units),
            ),
        ),
        deals=(Deal(up_own, up_far, own_experts), Deal(first_own, first_far, own_experts // 2)),
    )
    hidden_out = (middle + expert_branch).astype(slim)
    grad_up = up_blocks.astype(wide)

    def last_tile(window, held):
        return jnp.concatenate(
            [
                tn_dot(held[2][:, window], held[0][...]),
                tn_dot(held[3][:, window], held[4][...]),
            ],
            axis=1,
        )

    grad_first, last_blocks, second_blocks = pack_call(
        sizes,
        own_shape,
        lambda window, held, totals: (nt_dot(held[0][window, :], held[1][...]), ()),
        8,
        2 * pack_rows * width_all * 7 * head_dim,
        resident=(grad_qkv_low, qkv_weight, normed_first, grad_middle_all, attended_low),
        tiles=Tiles(4 * head_dim, width_all, last_tile),
        deals=(Deal(second_own, second_far, own_experts // 2),),
        needed=2,
    )
    by_halves = (ctx_size, own_experts // 2) + first_blocks.shape[1:]
    grad_down = (
        jnp.concatenate([first_blocks.reshape(by_halves), second_blocks.reshape(by_halves)], axis=1)
        .reshape((expert_count,) + first_blocks.shape[1:])
        .astype(wide)
    )
    grad_query, grad_key, grad_value, grad_out = (
        by_head(last_blocks[:, :, i * head_dim : (i + 1) * head_dim]) for i in range(4)
    )
    grad_out = grad_out.T

    gain_first = attn_norm.astype(wide)
    inv_first = lax.dynamic_slice_in_dim(inv_all, ctx_place * tok_rows, tok_rows, 0)[:, :1]
    gain_one_grad = jnp.sum(grad_first * resid_in * inv_first, axis=0)
    first_scaled = grad_first * gain_first
    first_inner = row_total(jnp.sum(first_scaled * resid_in, axis=1))[:, None]
    grad_hidden = (
        grad_middle + inv_first * first_scaled - resid_in * inv_first**3 * first_inner / width_all
    )

    stream_part = jnp.stack(
        [
            jnp.sum(middle * middle),
            jnp.sum(attn_branch * attn_branch),
            jnp.sum(expert_branch * expert_branch),
        ]
    )
    gain_rows = col_count // lanes
    sums = small_sums(
        sizes,
        jnp.concatenate(
            [
                gain_one_grad.reshape(gain_rows, lanes),
                gain_two_grad.reshape(gain_rows, lanes),
                gain_sums,
                jnp.pad(stream_part[None, :], ((0, 7), (0, lanes - 3))),
            ],
            axis=0,
        ),
        9,
    )
    tp_sums = jnp.sum(sums[:, 2 * gain_rows :], axis=0)
    token_count = tok_rows * packs * ctx_size
    stream_rms = jnp.sqrt(tp_sums[8, :3] / (token_count * width_all))
    return (
        hidden_out,
        grad_hidden,
        sums[:, :gain_rows].reshape(width_all),
        sums[:, gain_rows : 2 * gain_rows].reshape(width_all),
        tp_sums[0],
        tp_sums[1],
        grad_query,
        grad_key,
        grad_value,
        grad_out,
        grad_router,
        grad_gate,
        grad_up,
        grad_down,
        stream_rms,
    )


def solution(mesh):
    return jax.shard_map(
        on_device,
        mesh=mesh,
        in_specs=(
            P(("fsdp", "ctx"), "tp"),
            P(("fsdp", "ctx"), "tp"),
            P("fsdp", None),
            P("fsdp", None),
            P(("fsdp", "ctx"), None),
            P("tp"),
            P("tp"),
            P(),
            P(),
            P("fsdp", "tp"),
            P("fsdp", "tp"),
            P("fsdp", "tp"),
            P("tp", "fsdp"),
            P(None, "fsdp"),
            P(None, "fsdp", "tp"),
            P(None, "fsdp", "tp"),
            P(None, "fsdp", "tp"),
        ),
        out_specs=(
            P(("fsdp", "ctx"), "tp"),
            P(("fsdp", "ctx"), "tp"),
            P(),
            P(),
            P(),
            P(),
            P(("fsdp", "ctx"), "tp"),
            P(("fsdp", "ctx"), "tp"),
            P(("fsdp", "ctx"), "tp"),
            P("tp", ("fsdp", "ctx")),
            P(None, ("fsdp", "ctx")),
            P(None, ("fsdp", "ctx"), "tp"),
            P(None, ("fsdp", "ctx"), "tp"),
            P(None, ("fsdp", "ctx"), "tp"),
            P(),
        ),
        check_vma=False,
    )
```
